32 devices in a mesh: seq: 4 (over y, core), ctx: 8 (over z, x).
Axes of the slice: x: 2, y: 2, z: 4, core: 2. Of those that a mesh axis runs over, the one named last changes fastest.
Arguments:
- tokens: bfloat16 [8, 1024, 768], P('seq', 'ctx'), may hold values from -6 to 6
- grad_out: bfloat16 [8, 1024, 768], P('seq', 'ctx'), may hold values from -6 to 6
- timestep: int32 [8], P('seq'), may hold values from 0 to 1999
- w_time: bfloat16 [768, 768], P('seq'), may hold values from -0.21875 to 0.21875
- b_time: bfloat16 [768], P('seq'), may hold values from -3 to 3
- ln1_gain: bfloat16 [768], P('seq'), may hold values from 0.099609375 to 1.8984375
- ln1_bias: bfloat16 [768], P('seq'), may hold values from -3 to 3
- w_qkv: bfloat16 [768, 2304], P('seq'), may hold values from -0.3125 to 0.3125
- b_query: bfloat16 [768], P('seq'), may hold values from -3 to 3
- b_value: bfloat16 [768], P('seq'), may hold values from -3 to 3
- w_out: bfloat16 [768, 768], P('seq'), may hold values from -1 to 1
- b_out: bfloat16 [768], P('seq'), may hold values from -3 to 3
- ln2_gain: bfloat16 [768], P('seq'), may hold values from 0.099609375 to 1.8984375
- ln2_bias: bfloat16 [768], P('seq'), may hold values from -3 to 3
- w_up: bfloat16 [768, 3072], P('seq'), may hold values from -0.21875 to 0.21875
- b_up: bfloat16 [3072], P('seq'), may hold values from -3 to 3
- w_down: bfloat16 [3072, 768], P('seq'), may hold values from -0.109375 to 0.109375
- b_down: bfloat16 [768], P('seq'), may hold values from -3 to 3
Outputs:
- output: bfloat16 [8, 1024, 768], P('seq', 'ctx')
- grad_tokens: bfloat16 [8, 1024, 768], P('seq', 'ctx')
- grad_w_time: float32 [768, 768], P('seq')
- grad_b_time: float32 [768], P('seq')
- grad_ln1_gain: float32 [768], P('seq')
- grad_ln1_bias: float32 [768], P('seq')
- grad_w_qkv: float32 [768, 2304], P('seq')
- grad_b_query: float32 [768], P('seq')
- grad_b_value: float32 [768], P('seq')
- grad_w_out: float32 [768, 768], P('seq')
- grad_b_out: float32 [768], P('seq')
- grad_ln2_gain: float32 [768], P('seq')
- grad_ln2_bias: float32 [768], P('seq')
- grad_w_up: float32 [768, 3072], P('seq')
- grad_b_up: float32 [3072], P('seq')
- grad_w_down: float32 [3072, 768], P('seq')
- grad_b_down: float32 [768], P('seq')
The draws below stay inside these ranges and needn't reach their ends.
All inputs are finite; a program needn't handle non-finite values.
Results may differ from the reference program's by a relative error of at most 0.028.
Values may be sent and summed in bfloat16 or wider, within the bound.
No kernel may reach another device: no remote copies, remote signals or barrier semaphores. Data moves between devices by JAX's collectives and lax.ppermute only.
A program may use at most 320 MiB of HBM per device.

```python
import math
import jax
import jax.numpy as jnp
from jax import lax

D = 768
HEADS = 12
HEAD_DIM = 64
FF = 3072
TSTEPS = 2000
SEQS = 8
LENGTH = 1024


def touch_ends(drawn, rng, smallest, high):
    longest = drawn.shape.index(max(drawn.shape))
    spots = []
    for shift in (0, 1):
        where = [jax.random.randint(jax.random.fold_in(rng, axis), (), 0, length) for axis, length in enumerate(drawn.shape)]
        where[longest] = (where[longest] + shift) % drawn.shape[longest]
        spots.append(tuple(where))
    return drawn.at[spots[0]].set(smallest).at[spots[1]].set(high)


def block_scale(key, shape, pieces, smallest, largest):
    level = 1.0
    for dim, shards_of in pieces:
        heights = jax.random.uniform(jax.random.fold_in(jax.random.fold_in(key, 6), dim), (shards_of,), jnp.float32, smallest / len(pieces), largest / len(pieces))
        level = level * jnp.repeat(jnp.exp(heights), shape[dim] // shards_of).reshape((-1,) + (1,) * (len(shape) - 1 - dim))
    return level


def normal_values(stream_key, extent, width, limit, split=(), dtype=jnp.bfloat16):
    entries = jax.random.normal(stream_key, extent, jnp.float32) * width
    if len(split) > 0:
        entries = block_scale(stream_key, extent, split, -0.22, 0.18) * entries
    return jnp.clip(entries, min=-limit, max=limit).astype(dtype)


def setup_inputs(seed: int = 0) -> dict:
    key_list = jax.random.split(jax.random.key(seed), 19)
    tokens = normal_values(key_list[0], (SEQS, LENGTH, D), 1.0, 6.0, ((0, 4), (1, 8)))
    grad_out = normal_values(key_list[1], (SEQS, LENGTH, D), 1.0, 6.0, ((0, 4), (1, 8)))
    timestep = touch_ends(jax.random.randint(key_list[2], (SEQS,), 0, TSTEPS), jax.random.fold_in(key_list[2], 1), 0, TSTEPS - 1).astype(jnp.int32)
    w_time = normal_values(key_list[3], (D, D), D ** -0.5, 0.21875, ((0, 4),))
    b_time = normal_values(key_list[4], (D,), 0.5, 3.0, ((0, 4),))
    ln1_gain = jnp.clip(1.0 + 0.18 * jax.random.normal(key_list[5], (D,), jnp.float32), 0.099609375, 1.8984375).astype(jnp.bfloat16)
    ln1_bias = normal_values(key_list[6], (D,), 0.5, 3.0, ((0, 4),))
    w_qkv = normal_values(key_list[7], (D, 3 * D), (D // 2) ** -0.5, 0.3125, ((0, 4),))
    b_query = normal_values(key_list[8], (D,), 0.5, 3.0, ((0, 4),))
    b_value = normal_values(key_list[9], (D,), 0.5, 3.0, ((0, 4),))
    w_out = normal_values(key_list[10], (D, D), (max(1, D * 48 // LENGTH)) ** -0.5, 1.0, ((0, 4),))
    b_out = normal_values(key_list[11], (D,), 0.5, 3.0, ((0, 4),))
    ln2_gain = jnp.clip(1.0 + 0.18 * jax.random.normal(key_list[12], (D,), jnp.float32), 0.099609375, 1.8984375).astype(jnp.bfloat16)
    ln2_bias = normal_values(key_list[13], (D,), 0.5, 3.0, ((0, 4),))
    w_up = normal_values(key_list[14], (D, FF), D ** -0.5, 0.21875, ((0, 4),))
    b_up = normal_values(key_list[15], (FF,), 0.5, 3.0, ((0, 4),))
    w_down = normal_values(key_list[16], (FF, D), FF ** -0.5, 0.109375, ((0, 4),))
    b_down = normal_values(key_list[17], (D,), 0.5, 3.0, ((0, 4),))
    return dict(tokens=tokens, grad_out=grad_out, timestep=timestep, w_time=w_time, b_time=b_time, ln1_gain=ln1_gain, ln1_bias=ln1_bias, w_qkv=w_qkv, b_query=b_query, b_value=b_value, w_out=w_out, b_out=b_out, ln2_gain=ln2_gain, ln2_bias=ln2_bias, w_up=w_up, b_up=b_up, w_down=w_down, b_down=b_down)


@jax.custom_vjp
def low(v):
    return lax.optimization_barrier(v.astype(jnp.bfloat16)).astype(jnp.float32)

@jax.custom_vjp
def low_back(v):
    return v

def low_keep(v):
    return (low(v), None)

def low_pass(kept, grad):
    return (grad,)

def back_keep(v):
    return (v, None)

def back_low(kept, grad):
    return (low(grad),)
low.defvjp(low_keep, low_pass)
low_back.defvjp(back_keep, back_low)
norm_eps = 1e-05
highest = lax.Precision.HIGHEST

def matmul(left, right):
    return jnp.dot(left, right, precision=highest)

def layer_norm(hidden, norm_gain, offset):
    center = hidden - lax.optimization_barrier(jnp.mean(hidden, axis=-1, keepdims=True))
    variance = lax.optimization_barrier(jnp.mean(center * center, axis=-1, keepdims=True))
    return center * lax.rsqrt(variance + norm_eps) * norm_gain + offset

def sinusoid(timestep, model_width):
    half_width = model_width // 2
    frequency = jnp.exp(-math.log(10000.0) * jnp.arange(half_width).astype(jnp.float32) / half_width)
    angles = timestep.astype(jnp.float32)[:, None] * frequency[None, :]
    return jnp.concatenate([jnp.sin(angles), jnp.cos(angles)], axis=-1)

def attention(query, keys, values):
    length = keys.shape[0]
    block_len = min(length, 1024)
    score_scale = 1.0 / math.sqrt(HEAD_DIM)

    def one_block(query_blk):
        scores = low_back(score_scale * jnp.einsum('qhe,khe->hqk', query_blk, keys, precision=highest))
        top_score = lax.optimization_barrier(jnp.max(scores, axis=-1, keepdims=True))
        weights = jnp.exp(scores - top_score)
        probs = low(weights / lax.optimization_barrier(jnp.sum(weights, axis=-1, keepdims=True)))
        return jnp.einsum('hqk,khe->qhe', probs, values, precision=highest)
    blocks = query.reshape(length // block_len, block_len, HEADS, HEAD_DIM)
    return lax.map(jax.checkpoint(one_block), blocks).reshape(length, HEADS * HEAD_DIM)

def sequence_layer(params, seq_tokens, sinus_row):
    w_time, b_time, ln1_gain, ln1_bias, w_qkv, b_query, b_value, w_out, b_out, ln2_gain, ln2_bias, w_up, b_up, w_down, b_down = params
    model_width = seq_tokens.shape[-1]
    length = seq_tokens.shape[0]
    time_embed = matmul(low(sinus_row)[None, :], w_time)[0] + b_time
    hidden = seq_tokens + time_embed[None, :]
    attn_in = low(layer_norm(hidden, ln1_gain, ln1_bias))
    qkv_bias = jnp.concatenate([b_query, jnp.zeros_like(b_query), b_value])
    projected = matmul(attn_in, w_qkv) + qkv_bias
    query = low(low_back(projected[:, :model_width]))
    keys = low(low_back(projected[:, model_width:2 * model_width]))
    values = low(low_back(projected[:, 2 * model_width:]))
    attn = attention(query.reshape(length, HEADS, HEAD_DIM), keys.reshape(length, HEADS, HEAD_DIM), values.reshape(length, HEADS, HEAD_DIM))
    attn_low = low(low_back(attn))
    hidden_two = hidden + low_back(matmul(attn_low, w_out) + b_out)
    mlp_in = low(layer_norm(hidden_two, ln2_gain, ln2_bias))
    pre_act = low_back(matmul(mlp_in, w_up) + b_up)
    act_low = low(jax.nn.gelu(pre_act, approximate=False))
    return hidden_two + matmul(act_low, w_down) + b_down

def reference(tokens, grad_out, timestep, w_time, b_time, ln1_gain, ln1_bias, w_qkv, b_query, b_value, w_out, b_out, ln2_gain, ln2_bias, w_up, b_up, w_down, b_down):
    params = tuple((parameter.astype(jnp.float32) for parameter in (w_time, b_time, ln1_gain, ln1_bias, w_qkv, b_query, b_value, w_out, b_out, ln2_gain, ln2_bias, w_up, b_up, w_down, b_down)))
    sinus = sinusoid(timestep, D)

    def whole(token_values, param_values):

        def one_seq(paired):
            return sequence_layer(param_values, paired[0], paired[1])
        return lax.map(jax.checkpoint(one_seq), (token_values, sinus))
    output, pull = jax.vjp(whole, tokens.astype(jnp.float32), params)
    grad_tokens, grad_params = pull(grad_out.astype(jnp.float32))
    g_w_time, g_b_time, g_ln1_gain, g_ln1_bias, g_w_qkv, g_b_query, g_b_value, g_w_out, g_b_out, g_ln2_gain, g_ln2_bias, g_w_up, g_b_up, g_w_down, g_b_down = grad_params
    return (output.astype(jnp.bfloat16), grad_tokens.astype(jnp.bfloat16), g_w_time, g_b_time, g_ln1_gain, g_ln1_bias, g_w_qkv, g_b_query, g_b_value, g_w_out, g_b_out, g_ln2_gain, g_ln2_bias, g_w_up, g_b_up, g_w_down, g_b_down)
```

```python
import math

import jax
import jax.numpy as jnp
from jax import lax
from jax.sharding import Mesh
from jax.sharding import PartitionSpec as P

F32 = jnp.float32
BF16 = jnp.bfloat16


HEADS = 12
HEAD_DIM = 64


norm_eps = 1e-05
block_keys = 1024


def layer_norm(hidden, norm_gain, offset):
    center = hidden - jnp.mean(hidden, axis=-1, keepdims=True)
    variance = jnp.mean(center * center, axis=-1, keepdims=True)
    return center * lax.rsqrt(variance + norm_eps) * norm_gain + offset


def gelu_exact(values):
    return jax.nn.gelu(values, approximate=False)


def sinusoid(timestep, model_width):
    half_width = model_width // 2
    frequency = jnp.exp(
        -math.log(10000.0) * jnp.arange(half_width).astype(jnp.float32) / half_width
    )
    angles = timestep.astype(jnp.float32)[:, None] * frequency[None, :]
    return jnp.concatenate([jnp.sin(angles), jnp.cos(angles)], axis=-1)


def scores_of(queries, keys_blk, score_scale):
    return score_scale * jnp.einsum(
        "sphe,skhe->shpk", queries, keys_blk, preferred_element_type=jnp.float32
    )


def token_sum(values):
    return jnp.sum(values.astype(jnp.float32), axis=(0, 1))


def softmax_totals(query_low, key_all, score_scale, block_len):
    seq_count, row_count, head_count, head_width = query_low.shape
    blocks = key_all.shape[1] // block_len

    def softmax_block_step(carry, block_index):
        top_now, running = carry
        keys_blk = lax.dynamic_slice_in_dim(key_all, block_index * block_len, block_len, 1)
        scores = scores_of(query_low, keys_blk, score_scale)
        top_new = jnp.maximum(top_now, jnp.max(scores, axis=-1))
        running = running * jnp.exp(top_now - top_new) + jnp.sum(
            jnp.exp(scores - top_new[..., None]), axis=-1
        )
        return ((top_new, running), None)

    initial = (
        jnp.full((seq_count, head_count, row_count), -jnp.inf, jnp.float32),
        jnp.zeros((seq_count, head_count, row_count), jnp.float32),
    )
    (top_now, running), unused = lax.scan(softmax_block_step, initial, jnp.arange(blocks))
    return top_now + jnp.log(running)


def attend(query_low, key_all, value_all, log_totals, score_scale, block_len):
    blocks = key_all.shape[1] // block_len

    def attend_block_step(running, block_index):
        offset = block_index * block_len
        keys_blk = lax.dynamic_slice_in_dim(key_all, offset, block_len, 1)
        values_blk = lax.dynamic_slice_in_dim(value_all, offset, block_len, 1)
        probs_low = jnp.exp(
            scores_of(query_low, keys_blk, score_scale) - log_totals[..., None]
        ).astype(jnp.bfloat16)
        running = running + jnp.einsum(
            "shpk,skhe->sphe", probs_low, values_blk, preferred_element_type=jnp.float32
        )
        return (running, None)

    result, unused = lax.scan(
        attend_block_step, jnp.zeros(query_low.shape, jnp.float32), jnp.arange(blocks)
    )
    return result


def backward_reduce(
    query_low, key_all, value_all, grad_attn, log_totals, delta, score_scale, block_len
):
    blocks = key_all.shape[1] // block_len

    def backward_block_step(carry, block_index):
        grad_query, grad_key, grad_value = carry
        offset = block_index * block_len
        keys_blk = lax.dynamic_slice_in_dim(key_all, offset, block_len, 1)
        values_blk = lax.dynamic_slice_in_dim(value_all, offset, block_len, 1)
        weights = jnp.exp(scores_of(query_low, keys_blk, score_scale) - log_totals[..., None])
        probs_low = weights.astype(jnp.bfloat16)
        value_part = jnp.einsum(
            "shpk,sphe->skhe", probs_low, grad_attn, preferred_element_type=jnp.float32
        )
        grad_probs = jnp.einsum(
            "sphe,skhe->shpk", grad_attn, values_blk, preferred_element_type=jnp.float32
        )
        grad_scores = (weights * (grad_probs - delta[..., None])).astype(jnp.bfloat16)
        grad_query = grad_query + score_scale * jnp.einsum(
            "shpk,skhe->sphe", grad_scores, keys_blk, preferred_element_type=jnp.float32
        )
        key_part = score_scale * jnp.einsum(
            "shpk,sphe->skhe", grad_scores, query_low, preferred_element_type=jnp.float32
        )
        grad_key = lax.dynamic_update_slice_in_dim(grad_key, key_part, offset, 1)
        grad_value = lax.dynamic_update_slice_in_dim(grad_value, value_part, offset, 1)
        return ((grad_query, grad_key, grad_value), None)

    initial = (
        jnp.zeros(query_low.shape, jnp.float32),
        jnp.zeros(key_all.shape, jnp.float32),
        jnp.zeros(value_all.shape, jnp.float32),
    )
    result, unused = lax.scan(backward_block_step, initial, jnp.arange(blocks))
    return result


def body(
    tokens,
    grad_out,
    timestep,
    w_time,
    b_time,
    ln1_gain,
    ln1_bias,
    w_qkv,
    b_query,
    b_value,
    w_out,
    b_out,
    ln2_gain,
    ln2_bias,
    w_up,
    b_up,
    w_down,
    b_down,
):
    (
        time_full,
        time_bias,
        gain_one,
        bias_one,
        qkv_full,
        query_bias,
        value_bias,
        out_full,
        out_bias,
        gain_two,
        bias_two,
        up_full,
        up_bias,
        down_full,
        down_bias,
    ) = (
        lax.all_gather(w_time, "seq", axis=0, tiled=True),
        lax.all_gather(b_time, "seq", axis=0, tiled=True),
        lax.all_gather(ln1_gain, "seq", axis=0, tiled=True),
        lax.all_gather(ln1_bias, "seq", axis=0, tiled=True),
        lax.all_gather(w_qkv, "seq", axis=0, tiled=True),
        lax.all_gather(b_query, "seq", axis=0, tiled=True),
        lax.all_gather(b_value, "seq", axis=0, tiled=True),
        lax.all_gather(w_out, "seq", axis=0, tiled=True),
        lax.all_gather(b_out, "seq", axis=0, tiled=True),
        lax.all_gather(ln2_gain, "seq", axis=0, tiled=True),
        lax.all_gather(ln2_bias, "seq", axis=0, tiled=True),
        lax.all_gather(w_up, "seq", axis=0, tiled=True),
        lax.all_gather(b_up, "seq", axis=0, tiled=True),
        lax.all_gather(w_down, "seq", axis=0, tiled=True),
        lax.all_gather(b_down, "seq", axis=0, tiled=True),
    )
    seq_count, piece_len, model_width = tokens.shape
    score_scale = 1.0 / math.sqrt(HEAD_DIM)
    split_shape = (seq_count, piece_len, HEADS, HEAD_DIM)
    flat_shape = (seq_count, piece_len, model_width)
    sinus_low = sinusoid(timestep, model_width).astype(jnp.bfloat16)
    time_embed = jnp.dot(
        sinus_low, time_full, preferred_element_type=jnp.float32
    ) + time_bias.astype(jnp.float32)
    hidden = tokens.astype(jnp.float32) + time_embed[:, None, :]
    attn_in = layer_norm(hidden, gain_one.astype(jnp.float32), bias_one.astype(jnp.float32)).astype(
        jnp.bfloat16
    )
    qkv_bias = jnp.concatenate([query_bias, jnp.zeros_like(query_bias), value_bias]).astype(
        jnp.float32
    )
    projected = (
        jnp.einsum("spd,de->spe", attn_in, qkv_full, preferred_element_type=jnp.float32) + qkv_bias
    )
    query_low = projected[..., :model_width].astype(jnp.bfloat16).reshape(split_shape)
    key_low = (
        projected[..., model_width : 2 * model_width].astype(jnp.bfloat16).reshape(split_shape)
    )
    value_low = projected[..., 2 * model_width :].astype(jnp.bfloat16).reshape(split_shape)
    key_all, value_all = (
        lax.all_gather(key_low, "ctx", axis=1, tiled=True),
        lax.all_gather(value_low, "ctx", axis=1, tiled=True),
    )
    block_len = min(key_all.shape[1], block_keys)
    log_totals = softmax_totals(query_low, key_all, score_scale, block_len)
    attn = attend(query_low, key_all, value_all, log_totals, score_scale, block_len)
    attn_low = attn.reshape(flat_shape).astype(jnp.bfloat16)
    hidden_two = (
        hidden
        + jnp.einsum("spd,de->spe", attn_low, out_full, preferred_element_type=jnp.float32)
        + out_bias.astype(jnp.float32)
    )
    mlp_in = layer_norm(
        hidden_two, gain_two.astype(jnp.float32), bias_two.astype(jnp.float32)
    ).astype(jnp.bfloat16)
    pre_act = jnp.einsum(
        "spd,df->spf", mlp_in, up_full, preferred_element_type=jnp.float32
    ) + up_bias.astype(jnp.float32)
    act_low = gelu_exact(pre_act).astype(jnp.bfloat16)
    output = (
        hidden_two
        + jnp.einsum("spf,fd->spd", act_low, down_full, preferred_element_type=jnp.float32)
        + down_bias.astype(jnp.float32)
    ).astype(jnp.bfloat16)
    qkv_back, out_back, up_back, down_back, gain_one_back, gain_two_back = (
        lax.all_gather(w_qkv, "seq", axis=0, tiled=True),
        lax.all_gather(w_out, "seq", axis=0, tiled=True),
        lax.all_gather(w_up, "seq", axis=0, tiled=True),
        lax.all_gather(w_down, "seq", axis=0, tiled=True),
        lax.all_gather(ln1_gain, "seq", axis=0, tiled=True),
        lax.all_gather(ln2_gain, "seq", axis=0, tiled=True),
    )
    grad_w_down = jnp.einsum("spf,spd->fd", act_low, grad_out, preferred_element_type=jnp.float32)
    grad_b_down = token_sum(grad_out)
    grad_act = jnp.einsum("spd,fd->spf", grad_out, down_back, preferred_element_type=jnp.float32)
    unused, gelu_pull = jax.vjp(gelu_exact, pre_act)
    grad_pre = gelu_pull(grad_act)[0].astype(jnp.bfloat16)
    grad_w_up = jnp.einsum("spd,spf->df", mlp_in, grad_pre, preferred_element_type=jnp.float32)
    grad_b_up = token_sum(grad_pre)
    grad_mlp = jnp.einsum("spf,df->spd", grad_pre, up_back, preferred_element_type=jnp.float32)
    unused, norm_two_pull = jax.vjp(
        layer_norm, hidden_two, gain_two_back.astype(jnp.float32), bias_two.astype(jnp.float32)
    )
    grad_hidden_two, grad_ln2_gain, grad_ln2_bias = norm_two_pull(grad_mlp)
    grad_hidden_two = grad_hidden_two + grad_out.astype(jnp.float32)
    grad_branch = grad_hidden_two.astype(jnp.bfloat16)
    grad_w_out = jnp.einsum(
        "spd,spe->de", attn_low, grad_branch, preferred_element_type=jnp.float32
    )
    grad_b_out = token_sum(grad_branch)
    grad_attn = (
        jnp.einsum("spe,de->spd", grad_branch, out_back, preferred_element_type=jnp.float32)
        .astype(jnp.bfloat16)
        .reshape(split_shape)
    )
    delta = jnp.transpose(jnp.sum(grad_attn.astype(jnp.float32) * attn, axis=-1), (0, 2, 1))
    grad_query, key_terms, value_terms = backward_reduce(
        query_low, key_all, value_all, grad_attn, log_totals, delta, score_scale, block_len
    )
    grad_key, grad_value = (
        lax.psum_scatter(key_terms, "ctx", scatter_dimension=1, tiled=True),
        lax.psum_scatter(value_terms, "ctx", scatter_dimension=1, tiled=True),
    )
    grad_qkv = jnp.concatenate(
        [
            grad_query.reshape(flat_shape),
            grad_key.reshape(flat_shape),
            grad_value.reshape(flat_shape),
        ],
        axis=-1,
    ).astype(jnp.bfloat16)
    grad_w_qkv = jnp.einsum("spd,spe->de", attn_in, grad_qkv, preferred_element_type=jnp.float32)
    grad_b_query = token_sum(grad_qkv[..., :model_width])
    grad_b_value = token_sum(grad_qkv[..., 2 * model_width :])
    grad_norm = jnp.einsum("spe,de->spd", grad_qkv, qkv_back, preferred_element_type=jnp.float32)
    unused, norm_one_pull = jax.vjp(
        layer_norm, hidden, gain_one_back.astype(jnp.float32), bias_one.astype(jnp.float32)
    )
    grad_hidden_part, grad_ln1_gain, grad_ln1_bias = norm_one_pull(grad_norm)
    grad_hidden = grad_hidden_two + grad_hidden_part
    grad_tokens = grad_hidden.astype(jnp.bfloat16)
    grad_embed = jnp.sum(grad_hidden, axis=1)
    grad_w_time = jnp.einsum(
        "sd,se->de", sinus_low.astype(jnp.float32), grad_embed, precision=lax.Precision.HIGHEST
    )
    grad_b_time = jnp.sum(grad_embed, axis=0)
    shares = (
        lax.psum_scatter(
            grad_w_time.astype(jnp.bfloat16), "seq", scatter_dimension=0, tiled=True
        ).astype(jnp.float32),
        lax.psum_scatter(
            grad_b_time.astype(jnp.bfloat16), "seq", scatter_dimension=0, tiled=True
        ).astype(jnp.float32),
        lax.psum_scatter(
            grad_ln1_gain.astype(jnp.bfloat16), "seq", scatter_dimension=0, tiled=True
        ).astype(jnp.float32),
        lax.psum_scatter(
            grad_ln1_bias.astype(jnp.bfloat16), "seq", scatter_dimension=0, tiled=True
        ).astype(jnp.float32),
        lax.psum_scatter(
            grad_w_qkv.astype(jnp.bfloat16), "seq", scatter_dimension=0, tiled=True
        ).astype(jnp.float32),
        lax.psum_scatter(
            grad_b_query.astype(jnp.bfloat16), "seq", scatter_dimension=0, tiled=True
        ).astype(jnp.float32),
        lax.psum_scatter(
            grad_b_value.astype(jnp.bfloat16), "seq", scatter_dimension=0, tiled=True
        ).astype(jnp.float32),
        lax.psum_scatter(
            grad_w_out.astype(jnp.bfloat16), "seq", scatter_dimension=0, tiled=True
        ).astype(jnp.float32),
        lax.psum_scatter(
            grad_b_out.astype(jnp.bfloat16), "seq", scatter_dimension=0, tiled=True
        ).astype(jnp.float32),
        lax.psum_scatter(
            grad_ln2_gain.astype(jnp.bfloat16), "seq", scatter_dimension=0, tiled=True
        ).astype(jnp.float32),
        lax.psum_scatter(
            grad_ln2_bias.astype(jnp.bfloat16), "seq", scatter_dimension=0, tiled=True
        ).astype(jnp.float32),
        lax.psum_scatter(
            grad_w_up.astype(jnp.bfloat16), "seq", scatter_dimension=0, tiled=True
        ).astype(jnp.float32),
        lax.psum_scatter(
            grad_b_up.astype(jnp.bfloat16), "seq", scatter_dimension=0, tiled=True
        ).astype(jnp.float32),
        lax.psum_scatter(
            grad_w_down.astype(jnp.bfloat16), "seq", scatter_dimension=0, tiled=True
        ).astype(jnp.float32),
        lax.psum_scatter(
            grad_b_down.astype(jnp.bfloat16), "seq", scatter_dimension=0, tiled=True
        ).astype(jnp.float32),
    )
    (
        total_w_time,
        total_b_time,
        total_ln1_gain,
        total_ln1_bias,
        total_w_qkv,
        total_b_query,
        total_b_value,
        total_w_out,
        total_b_out,
        total_ln2_gain,
        total_ln2_bias,
        total_w_up,
        total_b_up,
        total_w_down,
        total_b_down,
    ) = lax.psum(
        (
            shares[0],
            shares[1],
            shares[2],
            shares[3],
            shares[4],
            shares[5],
            shares[6],
            shares[7],
            shares[8],
            shares[9],
            shares[10],
            shares[11],
            shares[12],
            shares[13],
            shares[14],
        ),
        "ctx",
    )
    return (
        output,
        grad_tokens,
        total_w_time,
        total_b_time,
        total_ln1_gain,
        total_ln1_bias,
        total_w_qkv,
        total_b_query,
        total_b_value,
        total_w_out,
        total_b_out,
        total_ln2_gain,
        total_ln2_bias,
        total_w_up,
        total_b_up,
        total_w_down,
        total_b_down,
    )


def swap(value, axis):
    return lax.ppermute(value, axis, [(0, 1), (1, 0)])


def pick(value, index):
    return lax.dynamic_index_in_dim(value, index, 0, keepdims=False)


def dot(left, right, dims=((1,), (0,))):
    return lax.dot_general(left, right, (dims, ((), ())), preferred_element_type=F32)


def group_body(
    tokens, grad_out, timestep, w_time, b_time, ln1_gain, ln1_bias, w_qkv, b_query, b_value,
    w_out, b_out, ln2_gain, ln2_bias, w_up, b_up, w_down, b_down,
):
    seqs, piece, width = tokens.shape
    rows = w_qkv.shape[0]
    yi, ci = lax.axis_index("y"), lax.axis_index("c")
    hi, zi, xi = lax.axis_index("h"), lax.axis_index("zl"), lax.axis_index("x")
    si = 2 * yi + ci
    gi = 2 * zi + xi
    heads_here = HEADS // 4
    part = heads_here * HEAD_DIM

    tok_own = jnp.concatenate([pick(tokens, hi), swap(pick(tokens, 1 - hi), "h")])
    own = 2 * piece
    low_bits = (timestep % 64).astype(BF16)
    high_bits = (timestep // 64).astype(BF16)
    steps_row = jnp.zeros((rows,), BF16).at[:seqs].set(high_bits).at[seqs : 2 * seqs].set(low_bits)
    small = jnp.concatenate(
        [jnp.stack([b_time, ln1_gain, ln1_bias, b_query, b_value, b_out, ln2_gain, ln2_bias, b_down,
                    steps_row])]
    )
    small_all = lax.all_gather(small, ("y", "c"))
    vec = jnp.transpose(small_all[:, :9], (1, 0, 2)).reshape(9, width).astype(F32)
    (v_btime, v_ln1g, v_ln1b, v_bq, v_bv, v_bout, v_ln2g, v_ln2b, v_bdown) = [vec[i : i + 1] for i in range(9)]
    steps = (small_all[:, 9, :seqs].astype(F32) * 64 + small_all[:, 9, seqs : 2 * seqs].astype(F32)).reshape(-1)

    half = width // 2
    freq = jnp.exp(-math.log(10000.0) * jnp.arange(half).astype(F32) / half)
    angles = steps[:, None] * freq[None, :]
    sinus = jnp.concatenate([jnp.sin(angles), jnp.cos(angles)], axis=-1).astype(BF16)
    sinus_rows = lax.dynamic_slice_in_dim(sinus, si * rows, rows, 1)
    te = dot(sinus_rows, w_time)
    te = te + swap(te, "y")
    te = te + swap(te, "c")
    time_embed = lax.dynamic_slice_in_dim(te, seqs * si + hi, 1, 0) + v_btime

    def seq_rows(value, axis=0):
        pair = jnp.stack([value, swap(value, "y")])
        pair = jnp.stack([pick(pair, yi), pick(pair, 1 - yi)])
        quad = jnp.stack([pair, swap(pair, "c")])
        quad = jnp.stack([pick(quad, ci), pick(quad, 1 - ci)])
        return jnp.swapaxes(quad, 0, 1).reshape((-1,) + value.shape[1:])

    qkv_cols = pick(jnp.transpose(w_qkv.reshape(rows, 3, 4, part), (2, 0, 1, 3)), gi).reshape(rows, 3 * part)
    w_qkv_g = seq_rows(qkv_cols)
    w_out_f = seq_rows(w_out)
    ff = w_up.shape[1] // 4
    up_blocks = jnp.transpose(w_up.reshape(rows, 2, 2, ff), (2, 1, 0, 3))
    keep, give = pick(up_blocks, ci), pick(up_blocks, 1 - ci)
    got = swap(give, "c")
    both = jnp.stack([keep, got])
    both = jnp.stack([pick(both, ci), pick(both, 1 - ci)])
    both = jnp.swapaxes(both, 0, 1)
    mine, theirs = pick(both, yi), pick(both, 1 - yi)
    got = swap(theirs, "y")
    two = jnp.stack([mine, got])
    w_up_s = jnp.stack([pick(two, yi), pick(two, 1 - yi)]).reshape(width, ff)

    tok_x = swap(tok_own, "x")
    tok_z = swap(tok_own, "zl")
    tok_d = jnp.concatenate([swap(tok_x[:piece], "zl"), swap(tok_z[piece:], "x")])
    go_own = jnp.concatenate([pick(grad_out, hi), swap(pick(grad_out, 1 - hi), "h")])
    go_y = swap(go_own, "y")
    go_pair = jnp.concatenate([go_own, go_y])
    go_all = jnp.concatenate([go_pair, swap(go_pair, "c")])

    tok = jnp.concatenate([tok_own, tok_x, tok_z, tok_d])
    n = tok.shape[0]

    def norm(hidden):
        center = hidden - jnp.mean(hidden, axis=-1, keepdims=True)
        rstd = lax.rsqrt(jnp.mean(center * center, axis=-1, keepdims=True) + norm_eps)
        return center * rstd, rstd

    hidden = tok.astype(F32) + time_embed
    x1, r1 = norm(hidden)
    attn_in = (x1 * v_ln1g + v_ln1b).astype(BF16)
    bias_q = lax.dynamic_slice_in_dim(v_bq, gi * part, part, 1)
    bias_v = lax.dynamic_slice_in_dim(v_bv, gi * part, part, 1)
    qkv_bias = jnp.concatenate([bias_q, jnp.zeros_like(bias_q), bias_v], 1)
    qkv = (dot(attn_in, w_qkv_g) + qkv_bias).astype(BF16)
    split = qkv.reshape(n, 3, heads_here, HEAD_DIM)
    q, k, v = split[:, 0], split[:, 1], split[:, 2]
    scale = 1.0 / math.sqrt(HEAD_DIM)
    scores = scale * jnp.einsum("qhe,khe->hqk", q, k, preferred_element_type=F32)
    top = jnp.max(scores, -1, keepdims=True)
    ex = jnp.exp(scores - top)
    lse = top + jnp.log(jnp.sum(ex, -1, keepdims=True))
    probs = jnp.exp(scores - lse)
    probs_low = probs.astype(BF16)
    attn = jnp.einsum("hqk,khe->qhe", probs_low, v, preferred_element_type=F32).reshape(n, part)

    def to_members(value):
        rel = jnp.stack([pick(value, gi ^ j) for j in range(4)])
        return lax.all_to_all(rel, ("zl", "x"), split_axis=0, concat_axis=0, tiled=True)

    attn_blocks = to_members(attn.astype(BF16).reshape(4, own, part))
    attn_low = jnp.transpose(attn_blocks, (1, 0, 2)).reshape(own, width)
    hidden_two = hidden[:own] + dot(attn_low, w_out_f) + v_bout
    x2, r2 = norm(hidden_two)
    mlp_own = (x2 * v_ln2g + v_ln2b).astype(BF16)
    mlp_y = swap(mlp_own, "y")
    mlp_pair = jnp.concatenate([mlp_own, mlp_y])
    mlp_in = jnp.concatenate([mlp_pair, swap(mlp_pair, "c")])

    pre = dot(mlp_in, w_up_s) + b_up.astype(F32)
    act, gelu_pull = jax.vjp(lambda t: jax.nn.gelu(t, approximate=False), pre)
    act = act.astype(BF16)
    grad_act = dot(go_all, w_down, ((1,), (1,)))
    grad_pre = gelu_pull(grad_act)[0].astype(BF16)
    out_part = dot(act, w_down)
    gm_part = dot(grad_pre, w_up_s, ((1,), (1,)))
    gw_down = dot(act, go_all, ((0,), (0,)))
    gw_up = dot(mlp_in, grad_pre, ((0,), (0,)))
    gb_up = jnp.sum(grad_pre.astype(F32), 0, keepdims=True)
    gb_down = jnp.sum(go_all.astype(F32), 0, keepdims=True)

    def seq_sum(value):
        low = value.astype(BF16)
        pair = value[: 2 * own] + swap(low[2 * own :], "c").astype(F32)
        return pair[:own] + swap(pair[own:].astype(BF16), "y").astype(F32)

    grad_mlp = seq_sum(gm_part)
    out_sum = seq_sum(out_part)
    out_own = (hidden_two + out_sum + v_bdown).astype(BF16)

    def to_sequences(value):
        mine, other = value[:piece], swap(value[piece:], "h")
        two = jnp.stack([mine, other])
        return jnp.stack([pick(two, hi), pick(two, 1 - hi)])

    output = to_sequences(out_own)

    def norm_back(e, x, r):
        return r * (e - jnp.mean(e, -1, keepdims=True) - x * jnp.mean(e * x, -1, keepdims=True))

    grad_two = go_own.astype(F32) + norm_back(grad_mlp * v_ln2g, x2, r2)
    g_ln2g = jnp.sum(grad_mlp * x2, 0, keepdims=True)
    g_ln2b = jnp.sum(grad_mlp, 0, keepdims=True)
    branch = grad_two.astype(BF16)
    g_bout = jnp.sum(branch.astype(F32), 0, keepdims=True)
    gw_out = dot(attn_low, branch, ((0,), (0,)))
    grad_attn_own = dot(branch, w_out_f, ((1,), (1,))).astype(BF16)
    ga_blocks = jnp.transpose(grad_attn_own.reshape(own, 4, part), (1, 0, 2))
    ga_recv = lax.all_to_all(ga_blocks, ("zl", "x"), split_axis=0, concat_axis=0, tiled=True)
    ga = jnp.concatenate([pick(ga_recv, gi ^ j) for j in range(4)]).reshape(n, heads_here, HEAD_DIM)

    delta = jnp.sum(ga.astype(F32) * attn.reshape(n, heads_here, HEAD_DIM), -1)
    dp = jnp.einsum("qhe,khe->hqk", ga, v, preferred_element_type=F32)
    ds = (probs * (dp - jnp.transpose(delta)[..., None])).astype(BF16)
    dv = jnp.einsum("hqk,qhe->khe", probs_low, ga, preferred_element_type=F32)
    dq = scale * jnp.einsum("hqk,khe->qhe", ds, k, preferred_element_type=F32)
    dk = scale * jnp.einsum("hqk,qhe->khe", ds, q, preferred_element_type=F32)
    dqkv = jnp.stack([dq, dk, dv], 1).astype(BF16).reshape(n, 3 * part)
    gw_qkv = dot(attn_in, dqkv, ((0,), (0,)))
    g_bqkv = jnp.sum(dqkv.astype(F32), 0, keepdims=True)
    gn_part = dot(dqkv, w_qkv_g, ((1,), (1,)))
    g_ln1g = jnp.sum(gn_part * x1, 0, keepdims=True)
    g_ln1b = jnp.sum(gn_part, 0, keepdims=True)
    gh_part = norm_back(gn_part * v_ln1g, x1, r1)
    g_embed = jnp.sum(gh_part, 0, keepdims=True) + jnp.sum(grad_two, 0, keepdims=True)

    gh_recv = to_members(gh_part.astype(BF16).reshape(4, own, width))
    grad_hidden = grad_two + jnp.sum(gh_recv.astype(F32), 0)
    grad_tokens = to_sequences(grad_hidden.astype(BF16))

    def ctx_sum(value, first, second):
        def scatter(low, axis, index):
            blocks = low.reshape((2, -1) + low.shape[1:])
            return pick(blocks, index).astype(F32) + swap(pick(blocks, 1 - index), axis).astype(F32)

        def gather(low, axis, index):
            two = jnp.stack([low, swap(low, axis)])
            return jnp.stack([pick(two, index), pick(two, 1 - index)]).reshape((-1,) + low.shape[1:])

        at = {"x": xi, "zl": zi}
        now = scatter(value.astype(BF16), first, at[first]).astype(BF16)
        now = scatter(now, second, at[second]).astype(BF16)
        now = (now.astype(F32) + swap(now, "h").astype(F32)).astype(BF16)
        now = gather(now, second, at[second])
        return gather(now, first, at[first])

    pad = jnp.zeros((64 - 2, width), F32)
    t_down = ctx_sum(jnp.concatenate([gw_down, gb_up, gb_down, pad]), "x", "zl")
    t_up = ctx_sum(gw_up, "zl", "x")
    total_w_down = t_down[:ff].astype(F32)
    total_b_up = t_down[ff].astype(F32)
    total_b_down = lax.dynamic_slice_in_dim(t_down[ff + 1], si * rows, rows, 0).astype(F32)
    ub = t_up.reshape(2, 2, rows, ff)
    keep, give = pick(ub, yi), pick(ub, 1 - yi)
    got = swap(give, "y")
    two = jnp.stack([keep, got])
    two = jnp.stack([pick(two, yi), pick(two, 1 - yi)])
    two = jnp.swapaxes(two, 0, 1)
    got = swap(pick(two, 1 - ci), "c")
    quad = jnp.stack([pick(two, ci), got])
    quad = jnp.stack([pick(quad, ci), pick(quad, 1 - ci)])
    total_w_up = jnp.transpose(quad, (2, 1, 0, 3)).reshape(rows, 4 * ff).astype(F32)

    place = jnp.zeros((1, width), F32)
    g_bq = lax.dynamic_update_slice_in_dim(place, g_bqkv[:, :part], gi * part, 1)
    g_bv = lax.dynamic_update_slice_in_dim(place, g_bqkv[:, 2 * part :], gi * part, 1)
    vecs = jnp.concatenate([g_ln2g, g_ln2b, g_bout, g_bq, g_bv, g_ln1g, g_ln1b])
    vecs = jnp.transpose(vecs.reshape(7, 4, rows), (1, 0, 2))
    vecs = jnp.pad(vecs, ((0, 0), (0, 1), (0, 3 * part - rows)))
    slots = lax.dynamic_update_slice_in_dim(jnp.zeros((4 * seqs, width), F32), g_embed, seqs * si + hi, 0)
    slots = jnp.pad(slots.reshape(8 * seqs, half), ((0, 0), (0, 3 * part - half)))
    slots = jnp.broadcast_to(slots[None], (4,) + slots.shape)
    chain = jnp.concatenate([gw_qkv.reshape(4, rows, 3 * part), vecs, slots], 1).astype(BF16)

    def seq_scatter(value):
        blocks = value.reshape((2, 2) + value.shape[1:])
        blocks = jnp.swapaxes(blocks, 0, 1)
        now = pick(blocks, ci).astype(F32) + swap(pick(blocks, 1 - ci), "c").astype(F32)
        now = now.astype(BF16)
        return (pick(now, yi).astype(F32) + swap(pick(now, 1 - yi), "y").astype(F32)).astype(BF16)

    wo = seq_scatter(gw_out.astype(BF16).reshape(4, rows, width))
    blocks = wo.reshape(2, rows // 2, width)
    wo = (pick(blocks, xi).astype(F32) + swap(pick(blocks, 1 - xi), "x").astype(F32)).astype(BF16)
    blocks = wo.reshape(2, rows // 4, width)
    wo = (pick(blocks, zi).astype(F32) + swap(pick(blocks, 1 - zi), "zl").astype(F32)).astype(BF16)
    wo = wo.reshape(-1, 3 * part)

    now = jnp.concatenate([seq_scatter(chain), wo])
    now = (now.astype(F32) + swap(now, "h").astype(F32)).astype(BF16)
    got_x = swap(now, "x")
    got_z = swap(now, "zl")
    hb = now.shape[0] // 2
    got_d = jnp.concatenate([swap(got_x[:hb], "zl"), swap(got_z[hb:], "x")])
    rel = jnp.stack([now, got_x, got_z, got_d])
    ab = jnp.stack([pick(rel, gi ^ j) for j in range(4)])
    total_w_qkv = jnp.transpose(ab[:, :rows].reshape(4, rows, 3, part), (1, 2, 0, 3)).reshape(rows, 3 * width).astype(F32)
    vsum = jnp.sum(ab[:, rows : rows + 8 + 8 * seqs].astype(F32), 0)
    tv = vsum[:7, :rows]
    embeds = vsum[8 : 8 + 8 * seqs, :half].reshape(4 * seqs, width)
    wo_all = ab[:, rows + 8 + 8 * seqs :].reshape(2, 2, rows // 4, width)
    total_w_out = jnp.transpose(wo_all, (1, 0, 2, 3)).reshape(rows, width).astype(F32)
    total_w_time = lax.dot_general(
        sinus_rows.astype(F32), embeds, (((0,), (0,)), ((), ())), precision=lax.Precision.HIGHEST
    )
    total_b_time = lax.dynamic_slice_in_dim(jnp.sum(embeds, 0), si * rows, rows, 0)
    return (
        output, grad_tokens, total_w_time, total_b_time, tv[5], tv[6], total_w_qkv, tv[3], tv[4],
        total_w_out, tv[2], tv[0], tv[1], total_w_up, total_b_up, total_w_down, total_b_down,
    )


def solution(mesh):
    placed = (
        P("seq", "ctx", None),
        P("seq", "ctx", None),
        P("seq"),
        P("seq", None),
        P("seq"),
        P("seq"),
        P("seq"),
        P("seq", None),
        P("seq"),
        P("seq"),
        P("seq", None),
        P("seq"),
        P("seq"),
        P("seq"),
        P("seq", None),
        P("seq"),
        P("seq", None),
        P("seq"),
    )
    out_placed = (
        P("seq", "ctx", None),
        P("seq", "ctx", None),
        P("seq", None),
        P("seq"),
        P("seq"),
        P("seq"),
        P("seq", None),
        P("seq"),
        P("seq"),
        P("seq", None),
        P("seq"),
        P("seq"),
        P("seq"),
        P("seq", None),
        P("seq"),
        P("seq", None),
        P("seq"),
    )
    sizes = dict(mesh.shape)
    if sizes["seq"] == 4 and sizes["ctx"] == 8:
        fine = Mesh(mesh.devices.reshape((2,) * 5), ("y", "c", "h", "zl", "x"))
        split = {"seq": ("y", "c"), "ctx": ("h", "zl", "x"), None: None}

        def finer(spec):
            return P(*(split[axis] for axis in spec))

        return jax.shard_map(
            group_body,
            mesh=fine,
            in_specs=tuple(finer(spec) for spec in placed),
            out_specs=tuple(finer(spec) for spec in out_placed),
            check_vma=False,
        )
    return jax.shard_map(
        body,
        mesh=mesh,
        in_specs=placed,
        out_specs=out_placed,
        check_vma=False,
    )
```

```python
import math

import jax
import jax.numpy as jnp
from jax import lax
from jax.experimental import pallas as pl
from jax.experimental.pallas import tpu as pltpu
from jax.sharding import Mesh
from jax.sharding import PartitionSpec as P

HEADS = 12
HEAD_DIM = 64


norm_eps = 1e-05
block_keys = 1024


def layer_norm(hidden, norm_gain, offset):
    center = hidden - jnp.mean(hidden, axis=-1, keepdims=True)
    variance = jnp.mean(center * center, axis=-1, keepdims=True)
    return center * lax.rsqrt(variance + norm_eps) * norm_gain + offset


def gelu_exact(values):
    return jax.nn.gelu(values, approximate=False)


def sinusoid(timestep, model_width):
    half_width = model_width // 2
    frequency = jnp.exp(
        -math.log(10000.0) * jnp.arange(half_width).astype(jnp.float32) / half_width
    )
    angles = timestep.astype(jnp.float32)[:, None] * frequency[None, :]
    return jnp.concatenate([jnp.sin(angles), jnp.cos(angles)], axis=-1)


def scores_of(queries, keys_blk, score_scale):
    return score_scale * jnp.einsum(
        "sphe,skhe->shpk", queries, keys_blk, preferred_element_type=jnp.float32
    )


def token_sum(values):
    return jnp.sum(values.astype(jnp.float32), axis=(0, 1))


def softmax_totals(query_low, key_all, score_scale, block_len):
    seq_count, row_count, head_count, head_width = query_low.shape
    blocks = key_all.shape[1] // block_len

    def softmax_block_step(carry, block_index):
        top_now, running = carry
        keys_blk = lax.dynamic_slice_in_dim(key_all, block_index * block_len, block_len, 1)
        scores = scores_of(query_low, keys_blk, score_scale)
        top_new = jnp.maximum(top_now, jnp.max(scores, axis=-1))
        running = running * jnp.exp(top_now - top_new) + jnp.sum(
            jnp.exp(scores - top_new[..., None]), axis=-1
        )
        return ((top_new, running), None)

    initial = (
        jnp.full((seq_count, head_count, row_count), -jnp.inf, jnp.float32),
        jnp.zeros((seq_count, head_count, row_count), jnp.float32),
    )
    (top_now, running), unused = lax.scan(softmax_block_step, initial, jnp.arange(blocks))
    return top_now + jnp.log(running)


def attend(query_low, key_all, value_all, log_totals, score_scale, block_len):
    blocks = key_all.shape[1] // block_len

    def attend_block_step(running, block_index):
        offset = block_index * block_len
        keys_blk = lax.dynamic_slice_in_dim(key_all, offset, block_len, 1)
        values_blk = lax.dynamic_slice_in_dim(value_all, offset, block_len, 1)
        probs_low = jnp.exp(
            scores_of(query_low, keys_blk, score_scale) - log_totals[..., None]
        ).astype(jnp.bfloat16)
        running = running + jnp.einsum(
            "shpk,skhe->sphe", probs_low, values_blk, preferred_element_type=jnp.float32
        )
        return (running, None)

    result, unused = lax.scan(
        attend_block_step, jnp.zeros(query_low.shape, jnp.float32), jnp.arange(blocks)
    )
    return result


def backward_reduce(
    query_low, key_all, value_all, grad_attn, log_totals, delta, score_scale, block_len
):
    blocks = key_all.shape[1] // block_len

    def backward_block_step(carry, block_index):
        grad_query, grad_key, grad_value = carry
        offset = block_index * block_len
        keys_blk = lax.dynamic_slice_in_dim(key_all, offset, block_len, 1)
        values_blk = lax.dynamic_slice_in_dim(value_all, offset, block_len, 1)
        weights = jnp.exp(scores_of(query_low, keys_blk, score_scale) - log_totals[..., None])
        probs_low = weights.astype(jnp.bfloat16)
        value_part = jnp.einsum(
            "shpk,sphe->skhe", probs_low, grad_attn, preferred_element_type=jnp.float32
        )
        grad_probs = jnp.einsum(
            "sphe,skhe->shpk", grad_attn, values_blk, preferred_element_type=jnp.float32
        )
        grad_scores = (weights * (grad_probs - delta[..., None])).astype(jnp.bfloat16)
        grad_query = grad_query + score_scale * jnp.einsum(
            "shpk,skhe->sphe", grad_scores, keys_blk, preferred_element_type=jnp.float32
        )
        key_part = score_scale * jnp.einsum(
            "shpk,sphe->skhe", grad_scores, query_low, preferred_element_type=jnp.float32
        )
        grad_key = lax.dynamic_update_slice_in_dim(grad_key, key_part, offset, 1)
        grad_value = lax.dynamic_update_slice_in_dim(grad_value, value_part, offset, 1)
        return ((grad_query, grad_key, grad_value), None)

    initial = (
        jnp.zeros(query_low.shape, jnp.float32),
        jnp.zeros(key_all.shape, jnp.float32),
        jnp.zeros(value_all.shape, jnp.float32),
    )
    result, unused = lax.scan(backward_block_step, initial, jnp.arange(blocks))
    return result


def body(
    tokens,
    grad_out,
    timestep,
    w_time,
    b_time,
    ln1_gain,
    ln1_bias,
    w_qkv,
    b_query,
    b_value,
    w_out,
    b_out,
    ln2_gain,
    ln2_bias,
    w_up,
    b_up,
    w_down,
    b_down,
):
    (
        time_full,
        time_bias,
        gain_one,
        bias_one,
        qkv_full,
        query_bias,
        value_bias,
        out_full,
        out_bias,
        gain_two,
        bias_two,
        up_full,
        up_bias,
        down_full,
        down_bias,
    ) = (
        lax.all_gather(w_time, "seq", axis=0, tiled=True),
        lax.all_gather(b_time, "seq", axis=0, tiled=True),
        lax.all_gather(ln1_gain, "seq", axis=0, tiled=True),
        lax.all_gather(ln1_bias, "seq", axis=0, tiled=True),
        lax.all_gather(w_qkv, "seq", axis=0, tiled=True),
        lax.all_gather(b_query, "seq", axis=0, tiled=True),
        lax.all_gather(b_value, "seq", axis=0, tiled=True),
        lax.all_gather(w_out, "seq", axis=0, tiled=True),
        lax.all_gather(b_out, "seq", axis=0, tiled=True),
        lax.all_gather(ln2_gain, "seq", axis=0, tiled=True),
        lax.all_gather(ln2_bias, "seq", axis=0, tiled=True),
        lax.all_gather(w_up, "seq", axis=0, tiled=True),
        lax.all_gather(b_up, "seq", axis=0, tiled=True),
        lax.all_gather(w_down, "seq", axis=0, tiled=True),
        lax.all_gather(b_down, "seq", axis=0, tiled=True),
    )
    seq_count, piece_len, model_width = tokens.shape
    score_scale = 1.0 / math.sqrt(HEAD_DIM)
    split_shape = (seq_count, piece_len, HEADS, HEAD_DIM)
    flat_shape = (seq_count, piece_len, model_width)
    sinus_low = sinusoid(timestep, model_width).astype(jnp.bfloat16)
    time_embed = jnp.dot(
        sinus_low, time_full, preferred_element_type=jnp.float32
    ) + time_bias.astype(jnp.float32)
    hidden = tokens.astype(jnp.float32) + time_embed[:, None, :]
    attn_in = layer_norm(hidden, gain_one.astype(jnp.float32), bias_one.astype(jnp.float32)).astype(
        jnp.bfloat16
    )
    qkv_bias = jnp.concatenate([query_bias, jnp.zeros_like(query_bias), value_bias]).astype(
        jnp.float32
    )
    projected = (
        jnp.einsum("spd,de->spe", attn_in, qkv_full, preferred_element_type=jnp.float32) + qkv_bias
    )
    query_low = projected[..., :model_width].astype(jnp.bfloat16).reshape(split_shape)
    key_low = (
        projected[..., model_width : 2 * model_width].astype(jnp.bfloat16).reshape(split_shape)
    )
    value_low = projected[..., 2 * model_width :].astype(jnp.bfloat16).reshape(split_shape)
    key_all, value_all = (
        lax.all_gather(key_low, "ctx", axis=1, tiled=True),
        lax.all_gather(value_low, "ctx", axis=1, tiled=True),
    )
    block_len = min(key_all.shape[1], block_keys)
    log_totals = softmax_totals(query_low, key_all, score_scale, block_len)
    attn = attend(query_low, key_all, value_all, log_totals, score_scale, block_len)
    attn_low = attn.reshape(flat_shape).astype(jnp.bfloat16)
    hidden_two = (
        hidden
        + jnp.einsum("spd,de->spe", attn_low, out_full, preferred_element_type=jnp.float32)
        + out_bias.astype(jnp.float32)
    )
    mlp_in = layer_norm(
        hidden_two, gain_two.astype(jnp.float32), bias_two.astype(jnp.float32)
    ).astype(jnp.bfloat16)
    pre_act = jnp.einsum(
        "spd,df->spf", mlp_in, up_full, preferred_element_type=jnp.float32
    ) + up_bias.astype(jnp.float32)
    act_low = gelu_exact(pre_act).astype(jnp.bfloat16)
    output = (
        hidden_two
        + jnp.einsum("spf,fd->spd", act_low, down_full, preferred_element_type=jnp.float32)
        + down_bias.astype(jnp.float32)
    ).astype(jnp.bfloat16)
    qkv_back, out_back, up_back, down_back, gain_one_back, gain_two_back = (
        lax.all_gather(w_qkv, "seq", axis=0, tiled=True),
        lax.all_gather(w_out, "seq", axis=0, tiled=True),
        lax.all_gather(w_up, "seq", axis=0, tiled=True),
        lax.all_gather(w_down, "seq", axis=0, tiled=True),
        lax.all_gather(ln1_gain, "seq", axis=0, tiled=True),
        lax.all_gather(ln2_gain, "seq", axis=0, tiled=True),
    )
    grad_w_down = jnp.einsum("spf,spd->fd", act_low, grad_out, preferred_element_type=jnp.float32)
    grad_b_down = token_sum(grad_out)
    grad_act = jnp.einsum("spd,fd->spf", grad_out, down_back, preferred_element_type=jnp.float32)
    unused, gelu_pull = jax.vjp(gelu_exact, pre_act)
    grad_pre = gelu_pull(grad_act)[0].astype(jnp.bfloat16)
    grad_w_up = jnp.einsum("spd,spf->df", mlp_in, grad_pre, preferred_element_type=jnp.float32)
    grad_b_up = token_sum(grad_pre)
    grad_mlp = jnp.einsum("spf,df->spd", grad_pre, up_back, preferred_element_type=jnp.float32)
    unused, norm_two_pull = jax.vjp(
        layer_norm, hidden_two, gain_two_back.astype(jnp.float32), bias_two.astype(jnp.float32)
    )
    grad_hidden_two, grad_ln2_gain, grad_ln2_bias = norm_two_pull(grad_mlp)
    grad_hidden_two = grad_hidden_two + grad_out.astype(jnp.float32)
    grad_branch = grad_hidden_two.astype(jnp.bfloat16)
    grad_w_out = jnp.einsum(
        "spd,spe->de", attn_low, grad_branch, preferred_element_type=jnp.float32
    )
    grad_b_out = token_sum(grad_branch)
    grad_attn = (
        jnp.einsum("spe,de->spd", grad_branch, out_back, preferred_element_type=jnp.float32)
        .astype(jnp.bfloat16)
        .reshape(split_shape)
    )
    delta = jnp.transpose(jnp.sum(grad_attn.astype(jnp.float32) * attn, axis=-1), (0, 2, 1))
    grad_query, key_terms, value_terms = backward_reduce(
        query_low, key_all, value_all, grad_attn, log_totals, delta, score_scale, block_len
    )
    grad_key, grad_value = (
        lax.psum_scatter(key_terms, "ctx", scatter_dimension=1, tiled=True),
        lax.psum_scatter(value_terms, "ctx", scatter_dimension=1, tiled=True),
    )
    grad_qkv = jnp.concatenate(
        [
            grad_query.reshape(flat_shape),
            grad_key.reshape(flat_shape),
            grad_value.reshape(flat_shape),
        ],
        axis=-1,
    ).astype(jnp.bfloat16)
    grad_w_qkv = jnp.einsum("spd,spe->de", attn_in, grad_qkv, preferred_element_type=jnp.float32)
    grad_b_query = token_sum(grad_qkv[..., :model_width])
    grad_b_value = token_sum(grad_qkv[..., 2 * model_width :])
    grad_norm = jnp.einsum("spe,de->spd", grad_qkv, qkv_back, preferred_element_type=jnp.float32)
    unused, norm_one_pull = jax.vjp(
        layer_norm, hidden, gain_one_back.astype(jnp.float32), bias_one.astype(jnp.float32)
    )
    grad_hidden_part, grad_ln1_gain, grad_ln1_bias = norm_one_pull(grad_norm)
    grad_hidden = grad_hidden_two + grad_hidden_part
    grad_tokens = grad_hidden.astype(jnp.bfloat16)
    grad_embed = jnp.sum(grad_hidden, axis=1)
    grad_w_time = jnp.einsum(
        "sd,se->de", sinus_low.astype(jnp.float32), grad_embed, precision=lax.Precision.HIGHEST
    )
    grad_b_time = jnp.sum(grad_embed, axis=0)
    shares = (
        lax.psum_scatter(
            grad_w_time.astype(jnp.bfloat16), "seq", scatter_dimension=0, tiled=True
        ).astype(jnp.float32),
        lax.psum_scatter(
            grad_b_time.astype(jnp.bfloat16), "seq", scatter_dimension=0, tiled=True
        ).astype(jnp.float32),
        lax.psum_scatter(
            grad_ln1_gain.astype(jnp.bfloat16), "seq", scatter_dimension=0, tiled=True
        ).astype(jnp.float32),
        lax.psum_scatter(
            grad_ln1_bias.astype(jnp.bfloat16), "seq", scatter_dimension=0, tiled=True
        ).astype(jnp.float32),
        lax.psum_scatter(
            grad_w_qkv.astype(jnp.bfloat16), "seq", scatter_dimension=0, tiled=True
        ).astype(jnp.float32),
        lax.psum_scatter(
            grad_b_query.astype(jnp.bfloat16), "seq", scatter_dimension=0, tiled=True
        ).astype(jnp.float32),
        lax.psum_scatter(
            grad_b_value.astype(jnp.bfloat16), "seq", scatter_dimension=0, tiled=True
        ).astype(jnp.float32),
        lax.psum_scatter(
            grad_w_out.astype(jnp.bfloat16), "seq", scatter_dimension=0, tiled=True
        ).astype(jnp.float32),
        lax.psum_scatter(
            grad_b_out.astype(jnp.bfloat16), "seq", scatter_dimension=0, tiled=True
        ).astype(jnp.float32),
        lax.psum_scatter(
            grad_ln2_gain.astype(jnp.bfloat16), "seq", scatter_dimension=0, tiled=True
        ).astype(jnp.float32),
        lax.psum_scatter(
            grad_ln2_bias.astype(jnp.bfloat16), "seq", scatter_dimension=0, tiled=True
        ).astype(jnp.float32),
        lax.psum_scatter(
            grad_w_up.astype(jnp.bfloat16), "seq", scatter_dimension=0, tiled=True
        ).astype(jnp.float32),
        lax.psum_scatter(
            grad_b_up.astype(jnp.bfloat16), "seq", scatter_dimension=0, tiled=True
        ).astype(jnp.float32),
        lax.psum_scatter(
            grad_w_down.astype(jnp.bfloat16), "seq", scatter_dimension=0, tiled=True
        ).astype(jnp.float32),
        lax.psum_scatter(
            grad_b_down.astype(jnp.bfloat16), "seq", scatter_dimension=0, tiled=True
        ).astype(jnp.float32),
    )
    (
        total_w_time,
        total_b_time,
        total_ln1_gain,
        total_ln1_bias,
        total_w_qkv,
        total_b_query,
        total_b_value,
        total_w_out,
        total_b_out,
        total_ln2_gain,
        total_ln2_bias,
        total_w_up,
        total_b_up,
        total_w_down,
        total_b_down,
    ) = lax.psum(
        (
            shares[0],
            shares[1],
            shares[2],
            shares[3],
            shares[4],
            shares[5],
            shares[6],
            shares[7],
            shares[8],
            shares[9],
            shares[10],
            shares[11],
            shares[12],
            shares[13],
            shares[14],
        ),
        "ctx",
    )
    return (
        output,
        grad_tokens,
        total_w_time,
        total_b_time,
        total_ln1_gain,
        total_ln1_bias,
        total_w_qkv,
        total_b_query,
        total_b_value,
        total_w_out,
        total_b_out,
        total_ln2_gain,
        total_ln2_bias,
        total_w_up,
        total_b_up,
        total_w_down,
        total_b_down,
    )


F32 = jnp.float32
BF16 = jnp.bfloat16
VMEM_BYTES = 56 * 1024 * 1024
RATE = 1.15e9


def swap(value, axis):
    return lax.ppermute(value, axis, [(0, 1), (1, 0)])


def across(value):
    return lax.ppermute(value, ("zl", "x"), [(i, i ^ 3) for i in range(4)])


def pick(value, index):
    return lax.dynamic_index_in_dim(value, index, 0, keepdims=False)


def dot(left, right, left_dim=1, right_dim=0):
    return lax.dot_general(
        left, right, (((left_dim,), (right_dim,)), ((), ())), preferred_element_type=F32
    )


class Steps:
    def __init__(self, ids):
        self.ids = ids
        self.last = None

    def __call__(self, kernel, inputs, outputs, micros, scratch=(), behind=()):
        behind = [*behind] + ([self.last] if self.last is not None else [])
        shapes = [jax.ShapeDtypeStruct(shape, dtype) for shape, dtype in outputs]
        count = 1 + len(inputs)

        def run(*refs):
            kernel(*refs[:count], *refs[count + len(behind) :])

        results = pl.pallas_call(
            run,
            out_shape=shapes,
            in_specs=[pl.BlockSpec(memory_space=pltpu.SMEM)]
            + [pl.BlockSpec(memory_space=pltpu.VMEM)] * len(inputs)
            + [pl.BlockSpec(memory_space=pl.ANY)] * len(behind),
            out_specs=[pl.BlockSpec(memory_space=pltpu.VMEM)] * len(shapes),
            scratch_shapes=list(scratch),
            compiler_params=pltpu.CompilerParams(vmem_limit_bytes=VMEM_BYTES),
            cost_estimate=pl.CostEstimate(
                flops=int(micros * RATE), bytes_accessed=1, transcendentals=0
            ),
            name=kernel.__name__,
        )(self.ids, *inputs, *behind)
        self.last = results[0]
        return results


SEQ, MEMBER, HALF = 0, 1, 2


def normalize(hidden):
    center = hidden - jnp.mean(hidden, axis=-1, keepdims=True)
    rstd = lax.rsqrt(jnp.mean(center * center, axis=-1, keepdims=True) + norm_eps)
    return center * rstd, rstd


def norm_back(e, x, r):
    return r * (e - jnp.mean(e, -1, keepdims=True) - x * jnp.mean(e * x, -1, keepdims=True))


def time_row(ids, te_a, te_b, vec):
    at = pl.ds(2 * ids[SEQ] + ids[HALF], 1)
    return te_a[at, :] + te_b[at, :] + vec[0:1, :]


def token_kernel(ids, tokens, mine, far):
    mine[...] = tokens[ids[HALF]]
    far[...] = tokens[1 - ids[HALF]]


def pick_kernel(ids, grad_out, far):
    far[...] = grad_out[1 - ids[HALF]]


def column_kernel(ids, w_qkv, out):
    part = out.shape[1] // 3
    width = w_qkv.shape[1] // 3
    for member in range(4):

        @pl.when(ids[MEMBER] == member)
        def _():
            for t in range(3):
                at = t * width + member * part
                out[:, t * part : (t + 1) * part] = w_qkv[:, at : at + part]


def up_kernel(ids, w_up, own, y, c, yc):
    ff = own.shape[1]
    for ref, flip in ((own, 0), (y, 2), (c, 1), (yc, 3)):
        ref[...] = w_up[:, pl.ds(pl.multiple_of((ids[SEQ] ^ flip) * ff, ff), ff)]


def add_kernel(ids, left, right, out):
    out[...] = left[...] + right[...]


def own_kernel(ids, grad_out, far, own):
    half = far.shape[0]
    own[:half] = grad_out[ids[HALF]]
    own[half:] = far[...]


def second_kernel(ids, keep, recv, out):
    out[...] = (keep[...] + recv[1].astype(F32)).astype(BF16)


def total4_kernel(ids, a, b, c, d, out):
    total = a[...].astype(F32) + b[...].astype(F32) + c[...].astype(F32) + d[...].astype(F32)
    out[...] = total.astype(BF16)


def both_kernel(ids, left, right, out):
    out[...] = (left[...].astype(F32) + right[...].astype(F32)).astype(BF16)


def chain_kernel(ids, keep, c, first, second):
    first[...] = (keep[0].astype(F32) + c[0].astype(F32)).astype(BF16)
    second[...] = (keep[1].astype(F32) + c[1].astype(F32)).astype(BF16)


def join_kernel(ids, first, y, a, b, c, d, out):
    rows = first.shape[0]
    out[:rows] = (first[...].astype(F32) + y[...].astype(F32)).astype(BF16)
    total = a[...].astype(F32) + b[...].astype(F32) + c[...].astype(F32) + d[...].astype(F32)
    out[rows:] = total.astype(BF16)


def attend_kernel(
    ids, tok_own, tok_x, tok_z, tok_d, far_own, far_x, far_z, far_d, te_a, te_b, vec, small, wq_own, wq_y, wq_c, wq_yc,
    attn_in, qkv_t, o_full, o_send, lse, w_t, w_rows,
):
    part = wq_own.shape[1] // 3
    rows = wq_own.shape[0]
    piece, width = tok_own.shape
    own = 2 * piece
    si, gi = ids[SEQ], ids[MEMBER]
    for ref, flip in ((wq_own, 0), (wq_y, 2), (wq_c, 1), (wq_yc, 3)):
        w_rows[si ^ flip] = ref[...]
    for block in range(4):
        w_t[:, block * rows : (block + 1) * rows] = w_rows[block].T
    te_row = time_row(ids, te_a, te_b, vec)
    gain, offset = vec[1:2, :], vec[2:3, :]
    bias = small[gi].astype(F32).T
    pairs = ((tok_own, far_own), (tok_x, far_x), (tok_z, far_z), (tok_d, far_d))
    for block, (tok, far) in enumerate(pairs):
        normed, _ = normalize(jnp.concatenate([tok[...], far[...]]).astype(F32) + te_row)
        low = (normed * gain + offset).astype(BF16)
        attn_in[block] = low
        qkv = dot(w_t[...], low, 1, 1)
        qkv_t[block, 0:part, :] = (qkv[:part] + bias[:, 3:4]).astype(BF16)
        qkv_t[block, part : 2 * part, :] = qkv[part : 2 * part].astype(BF16)
        qkv_t[block, 2 * part :, :] = (qkv[2 * part :] + bias[:, 4:5]).astype(BF16)

    @pl.loop(0, part // HEAD_DIM)
    def _(head):
        at = pl.multiple_of(head * HEAD_DIM, HEAD_DIM)
        k_t = jnp.concatenate([qkv_t[j, pl.ds(part + at, HEAD_DIM), :] for j in range(4)], 1)
        v_t = jnp.concatenate([qkv_t[j, pl.ds(2 * part + at, HEAD_DIM), :] for j in range(4)], 1)
        for block in range(4):
            q_t = qkv_t[block, pl.ds(at, HEAD_DIM), :] * jnp.asarray(0.125, BF16)
            scores = dot(k_t, q_t, 0, 0)
            top = jnp.max(scores, 0, keepdims=True)
            weights = jnp.exp(scores - top)
            total = jnp.sum(weights, 0, keepdims=True)
            attn = dot(v_t, weights.astype(BF16)) / total
            o_full[block, pl.ds(at, HEAD_DIM), :] = attn
            o_send[gi ^ block, pl.ds(at, HEAD_DIM), :] = attn.astype(BF16)
            lse[head * 4 + block] = jnp.broadcast_to(top + jnp.log(total), (8, own))


def branch_kernel(
    ids, attn, w_out, tok_own, far_own, te_a, te_b, vec, mlp_in, hidden_two, a_own, a_y, a_c, a_yc
):
    rows = attn.shape[1]
    te_row = time_row(ids, te_a, te_b, vec)
    hidden = jnp.concatenate([tok_own[...], far_own[...]]).astype(F32) + te_row + vec[5:6, :]
    for block in range(4):
        hidden = hidden + dot(attn[block], w_out[block * rows : (block + 1) * rows, :], 0, 0)
    hidden_two[...] = hidden
    normed, _ = normalize(hidden)
    mlp_in[...] = (normed * vec[6:7, :] + vec[7:8, :]).astype(BF16)
    for ref, flip in ((a_own, 0), (a_y, 2), (a_c, 1), (a_yc, 3)):
        ref[...] = attn[ids[SEQ] ^ flip]


def feed_kernel(
    ids, m_own, m_y, m_c, m_yc, go_all, u_own, u_y, u_c, u_yc, w_down, b_up,
    gm_own, gm_pair, gm_send, out_own, out_pair, out_send, act_all, gp_all, w_up,
):
    si = ids[SEQ]
    rows = u_own.shape[0]
    for ref, flip in ((u_own, 0), (u_y, 2), (u_c, 1), (u_yc, 3)):
        w_up[pl.ds(pl.multiple_of((si ^ flip) * rows, rows), rows), :] = ref[...]
    for block, (ref, flip) in enumerate(((m_own, 0), (m_y, 2), (m_c, 1), (m_yc, 3))):
        grad_out = go_all[si ^ flip]
        pre = dot(ref[...], w_up[...]) + b_up[...]
        cdf = 0.5 * (1.0 + lax.erf(pre * (0.5**0.5)))
        act = (pre * cdf).astype(BF16)
        grad_act = dot(grad_out, w_down[...], 1, 1)
        slope = cdf + pre * (jnp.exp(-0.5 * pre * pre) * (0.5 / math.pi) ** 0.5)
        grad_pre = (grad_act * slope).astype(BF16)
        act_all[block] = act
        gp_all[block] = grad_pre
        gm = dot(grad_pre, w_up[...], 1, 1)
        out = dot(act, w_down[...])
        if block < 2:
            (gm_own, gm_pair)[block][...] = gm
            (out_own, out_pair)[block][...] = out
        else:
            gm_send[block - 2] = gm.astype(BF16)
            out_send[block - 2] = out.astype(BF16)


def feed_grad_kernel(
    ids, m_own, m_y, m_c, m_yc, go_all, act_all, gp_all, d_own, d_x, d_z, d_d, u_own, u_x, u_z, u_d, grad
):
    si, gi = ids[SEQ], ids[MEMBER]
    width = m_own.shape[1]
    ff = act_all.shape[2]
    part = ff // 4
    rows = width // 4
    fine = rows // 4
    orders = ((m_own, 0), (m_y, 2), (m_c, 1), (m_yc, 3))
    for s in range(4):
        cols = slice(s * part, (s + 1) * part)
        total = jnp.zeros((part, width), F32)
        for block, (_, flip) in enumerate(orders):
            total = total + dot(act_all[block, :, cols], go_all[si ^ flip], 0, 0)
        grad[cols, :] = total.astype(BF16)
    for ref, flip in ((d_own, 0), (d_x, 1), (d_z, 2), (d_d, 3)):
        ref[:part, :] = grad[pl.ds(pl.multiple_of((gi ^ flip) * part, 16), part), :]
    for s in range(4):
        cols = slice(s * rows, (s + 1) * rows)
        total = jnp.zeros((rows, ff), F32)
        for block, (ref, _) in enumerate(orders):
            total = total + dot(ref[:, cols], gp_all[block], 0, 0)
        grad[cols, :] = total.astype(BF16)
    for ref, flip in ((u_own, 0), (u_x, 1), (u_z, 2), (u_d, 3)):
        for s in range(4):
            ref[s] = grad[pl.ds(pl.multiple_of(s * rows + (gi ^ flip) * fine, 16), fine), :]
    b_up = jnp.zeros((1, ff), F32)
    b_down = jnp.zeros((1, width), F32)
    for block in range(4):
        b_up = b_up + jnp.sum(gp_all[block].astype(F32), 0, keepdims=True)
        b_down = b_down + jnp.sum(go_all[block].astype(F32), 0, keepdims=True)
    line = lax.broadcasted_iota(jnp.int32, (16, width), 0)
    extra = jnp.where(line == 0, b_up, jnp.where(line == 1, b_down, 0.0))
    for ref, flip in ((d_own, 0), (d_x, 1), (d_z, 2), (d_d, 3)):
        ref[part:, :] = jnp.where(gi == flip, extra, 0.0).astype(BF16)


def back_kernel(
    ids, gm_keep, gm_c, gm_y, hidden_two, go_own, w_out, vec,
    grad_two, branch, ga_send, sums,
):
    rows = w_out.shape[0] // 4
    grad_mlp = gm_keep[...] + gm_c[0].astype(F32) + gm_y[...].astype(F32)
    normed, rstd = normalize(hidden_two[...])
    grad = go_own[...].astype(F32) + norm_back(grad_mlp * vec[6:7, :], normed, rstd)
    grad_two[...] = grad
    low = grad.astype(BF16)
    branch[...] = low
    for block in range(4):
        ga_send[block] = dot(w_out[block * rows : (block + 1) * rows, :], low, 1, 1).astype(BF16)
    sums[0:1, :] = jnp.sum(grad_mlp * normed, 0, keepdims=True)
    sums[1:2, :] = jnp.sum(grad_mlp, 0, keepdims=True)
    sums[2:3, :] = jnp.sum(low.astype(F32), 0, keepdims=True)
    sums[3:4, :] = jnp.sum(grad, 0, keepdims=True)
    sums[4:8, :] = jnp.zeros((4, sums.shape[1]), F32)


def out_grad_kernel(ids, a_own, a_y, a_c, a_yc, branch, w_own, w_x, w_z, w_d, grads):
    si, gi = ids[SEQ], ids[MEMBER]
    narrow = w_own.shape[1]
    fine = a_own.shape[0] // 4
    third = fine // 3
    grad = jnp.zeros((a_own.shape[0], branch.shape[2]), F32)
    for ref, flip in ((a_own, 0), (a_y, 2), (a_c, 1), (a_yc, 3)):
        grad = grad + dot(ref[...], branch[si ^ flip])
    grads[...] = grad.astype(BF16)
    for ref, flip in ((w_own, 0), (w_x, 1), (w_z, 2), (w_d, 3)):
        lines = grads[pl.ds(pl.multiple_of((gi ^ flip) * fine, 16), fine), :]
        ref[:fine, :] = lines[:, :narrow]
        ref[fine:, :] = jnp.concatenate([lines[i * third : (i + 1) * third, narrow:] for i in range(3)], 1)


def out_kernel(ids, hidden_two, out_keep, out_c, out_y, vec, mine, other):
    out = hidden_two[...] + vec[8:9, :] + out_keep[...] + out_c[0].astype(F32) + out_y[...].astype(F32)
    half = mine.shape[0]
    mine[...] = out[:half].astype(BF16)
    other[...] = out[half:].astype(BF16)


def attend_back_kernel(
    ids, qkv_t, lse, o_full, ga, w_t, tok_own, tok_x, tok_z, tok_d, far_own, far_x, far_z, far_d, te_a, te_b, vec,
    dqkv_t, gh_own, gh_x, gh_z, gh_d, sums, dk, dv,
):
    part = o_full.shape[1]
    own = 2 * tok_own.shape[0]
    si, gi = ids[SEQ], ids[MEMBER]

    @pl.loop(0, part // HEAD_DIM)
    def _(head):
        at = pl.multiple_of(head * HEAD_DIM, HEAD_DIM)
        k_t = jnp.concatenate([qkv_t[j, pl.ds(part + at, HEAD_DIM), :] for j in range(4)], 1)
        v_t = jnp.concatenate([qkv_t[j, pl.ds(2 * part + at, HEAD_DIM), :] for j in range(4)], 1)
        for block in range(4):
            q_t = qkv_t[block, pl.ds(at, HEAD_DIM), :] * jnp.asarray(0.125, BF16)
            do_t = ga[gi ^ block, pl.ds(at, HEAD_DIM), :]
            delta = jnp.sum(do_t.astype(F32) * o_full[block, pl.ds(at, HEAD_DIM), :], 0, keepdims=True)
            weights = jnp.exp(dot(k_t, q_t, 0, 0) - lse[head * 4 + block, 0:1, :])
            grad_probs = dot(v_t, do_t, 0, 0)
            grad_scores = (weights * (grad_probs - delta)).astype(BF16)
            value_part = dot(do_t, weights.astype(BF16), 1, 1)
            key_part = dot(q_t, grad_scores, 1, 1)
            dqkv_t[block, pl.ds(at, HEAD_DIM), :] = (dot(k_t, grad_scores) * 0.125).astype(BF16)
            if block == 0:
                dv[...] = value_part
                dk[...] = key_part
            else:
                dv[...] += value_part
                dk[...] += key_part
        for block in range(4):
            lanes = slice(block * own, (block + 1) * own)
            dqkv_t[block, pl.ds(part + at, HEAD_DIM), :] = dk[:, lanes].astype(BF16)
            dqkv_t[block, pl.ds(2 * part + at, HEAD_DIM), :] = dv[:, lanes].astype(BF16)

    te_row = time_row(ids, te_a, te_b, vec)
    gain = vec[1:2, :]
    sum_gain = jnp.zeros_like(gain)
    sum_bias = jnp.zeros_like(gain)
    sum_hidden = jnp.zeros_like(gain)
    pairs = (
        (tok_own, far_own, gh_own), (tok_x, far_x, gh_x), (tok_z, far_z, gh_z), (tok_d, far_d, gh_d)
    )
    for block, (tok, far, to) in enumerate(pairs):
        normed, rstd = normalize(jnp.concatenate([tok[...], far[...]]).astype(F32) + te_row)
        grad_norm = dot(dqkv_t[block], w_t[...], 0, 0)
        grad = norm_back(grad_norm * gain, normed, rstd)
        to[...] = grad.astype(BF16)
        sum_gain = sum_gain + jnp.sum(grad_norm * normed, 0, keepdims=True)
        sum_bias = sum_bias + jnp.sum(grad_norm, 0, keepdims=True)
        sum_hidden = sum_hidden + jnp.sum(grad, 0, keepdims=True)
    sums[0:1, :] = sum_gain
    sums[1:2, :] = sum_bias
    sums[2:3, :] = sum_hidden
    sums[3:8, :] = jnp.zeros((5, sums.shape[1]), F32)


def qkv_grad_kernel(ids, attn_in, dqkv_t, sums_two, sums_one, keep, give):
    si, gi = ids[SEQ], ids[MEMBER]
    cols = dqkv_t.shape[1]
    part = cols // 3
    rows = part
    width = attn_in.shape[2]
    half = width // 2
    grad = jnp.zeros((cols, width), F32)
    tok_sum = jnp.zeros((16, cols), F32)
    for block in range(4):
        grad = grad + dot(dqkv_t[block], attn_in[block])
        tok_sum = tok_sum + dot(jnp.ones((16, dqkv_t.shape[2]), BF16), dqkv_t[block], 1, 1)
    grad = grad.astype(BF16)
    line = lax.broadcasted_iota(jnp.int32, (32, cols), 0)
    embed = sums_one[2:3, :] + sums_two[3:4, :]
    slot = 8 + 2 * (2 * si + ids[HALF])
    lanes = lax.broadcasted_iota(jnp.int32, (1, cols), 1)
    wide = [jnp.concatenate([e, jnp.zeros((1, cols - half), F32)], 1) for e in (embed[:, :half], embed[:, half:])]
    common = jnp.where(line == slot, wide[0], jnp.where(line == slot + 1, wide[1], 0.0))
    for s in range(4):
        here = slice(s * rows, (s + 1) * rows)
        extra = common
        vectors = (
            sums_two[0:1, here], sums_two[1:2, here], sums_two[2:3, here], sums_one[0:1, here], sums_one[1:2, here],
        )
        for i, vector in enumerate(vectors):
            full = jnp.concatenate([vector, jnp.zeros((1, cols - rows), F32)], 1)
            extra = jnp.where(line == i, full, extra)
        extra = jnp.where((line == 5) & (gi == s), tok_sum[0:1, :], extra)
        block = grad[:, here].T
        flip = si ^ s

        @pl.when(flip % 2 == 0)
        def _():
            keep[flip // 2, :rows, :] = block
            keep[flip // 2, rows:, :] = extra.astype(BF16)

        @pl.when(flip % 2 == 1)
        def _():
            give[flip // 2, :rows, :] = block
            give[flip // 2, rows:, :] = extra.astype(BF16)


def hidden_grad_kernel(ids, grad_two, a, b, c, d, mine, other):
    half = mine.shape[0]
    grad = grad_two[...]
    for ref in (a, b, c, d):
        grad = grad + ref[...].astype(F32)
    mine[...] = grad[:half].astype(BF16)
    other[...] = grad[half:].astype(BF16)


def feed_total_kernel(ids, d_own, d_x, d_z, d_d, u_own, u_x, u_z, u_d, w_down, w_up, small):
    gi = ids[MEMBER]
    quarter = w_down.shape[1]
    fine = w_up.shape[1]
    ff = w_down.shape[2]
    for ref, flip in ((d_own, 0), (d_x, 1), (d_z, 2), (d_d, 3)):
        w_down[gi ^ flip] = ref[:quarter, :].astype(F32)

        @pl.when(gi == flip)
        def _():
            small[...] = ref[quarter:, :].astype(F32)

    for ref, flip in ((u_own, 0), (u_x, 1), (u_z, 2), (u_d, 3)):
        for s in range(4):
            w_up[gi ^ flip, :, s * ff : (s + 1) * ff] = ref[s].astype(F32)


def total_kernel(ids, g_own, g_x, g_z, g_d, sinus, w_qkv, w_out, w_time, vectors, embeds, totals):
    si, gi = ids[SEQ], ids[MEMBER]
    rows = w_qkv.shape[0]
    cols = g_own.shape[1]
    width = w_qkv.shape[1] // 3
    part = cols // 3
    fine = rows // 4
    third = fine // 3
    for member in range(4):
        for ref, flip in ((g_own, 0), (g_x, 1), (g_z, 2), (g_d, 3)):

            @pl.when(gi ^ flip == member)
            def _():
                for t in range(3):
                    at = t * width + member * part
                    w_qkv[:, at : at + part] = ref[:rows, t * part : (t + 1) * part].astype(F32)
                lines = ref[rows + 32 :, :].astype(F32)
                w_out[member, :, :cols] = lines[:fine]
                for i in range(3):
                    w_out[member, i * third : (i + 1) * third, cols:] = lines[fine:, i * part : (i + 1) * part]

    small = jnp.zeros((32, cols), F32)
    for ref in (g_own, g_x, g_z, g_d):
        small = small + ref[rows : rows + 32, :].astype(F32)
    vectors[...] = small[:8]
    half = width // 2
    totals[...] = small
    for b in range(8):
        embeds[b : b + 1, :half] = totals[8 + 2 * b : 9 + 2 * b, :half]
        embeds[b : b + 1, half:] = totals[9 + 2 * b : 10 + 2 * b, :half]
    w_time[...] = lax.dot_general(
        sinus[...], embeds[...], (((0,), (0,)), ((), ())), precision=lax.Precision.HIGHEST,
        preferred_element_type=F32,
    )


def pair_kernel(ids, mine, other, out):
    out[ids[HALF]] = mine[...]
    out[1 - ids[HALF]] = other[...]


def group_body(
    tokens, grad_out, timestep, w_time, b_time, ln1_gain, ln1_bias, w_qkv, b_query, b_value,
    w_out, b_out, ln2_gain, ln2_bias, w_up, b_up, w_down, b_down,
):
    seqs, piece, width = tokens.shape
    rows = w_qkv.shape[0]
    ff = w_down.shape[0]
    own = 2 * piece
    part = width // 4
    heads = part // HEAD_DIM
    yi, ci = lax.axis_index("y"), lax.axis_index("c")
    hi, zi, xi = lax.axis_index("h"), lax.axis_index("zl"), lax.axis_index("x")
    si = 2 * yi + ci
    gi = 2 * zi + xi
    step = Steps(jnp.stack([si, gi, hi]).astype(jnp.int32))

    def members(value):
        return lax.all_to_all(value, ("zl", "x"), split_axis=0, concat_axis=0, tiled=True)

    def gather4(value):
        return [value, swap(value, "x"), swap(value, "zl"), across(value)]

    def trade4(keep, x, z, d):
        return [keep, swap(x, "x"), swap(z, "zl"), across(d)]

    def across_seq(value):
        return lax.ppermute(value, ("y", "c"), [(i, i ^ 3) for i in range(4)])

    w_out_f = lax.all_gather(w_out, ("y", "c"), axis=0, tiled=True)
    tok_own, tok_far = step(token_kernel, [tokens], [((piece, width), BF16)] * 2, 1)
    far_own = swap(tok_far, "h")
    toks = gather4(tok_own)
    fars = gather4(far_own)
    (wq_own,) = step(column_kernel, [w_qkv], [((rows, 3 * part), BF16)], 2)
    wq_y = swap(wq_own, "y")
    wq_c = swap(wq_own, "c")
    wq_yc = swap(wq_y, "c")
    low_bits = (timestep % 64).astype(BF16)
    high_bits = (timestep // 64).astype(BF16)
    steps_row = jnp.concatenate([high_bits, low_bits, jnp.zeros((rows - 2 * seqs,), BF16)])
    blank = jnp.zeros((rows,), BF16)
    small = jnp.stack(
        [b_time, ln1_gain, ln1_bias, b_query, b_value, b_out, ln2_gain, ln2_bias, b_down, steps_row] + [blank] * 6
    )
    small_all = lax.all_gather(small, ("y", "c"))
    vec = jnp.transpose(small_all, (1, 0, 2)).reshape(16, width).astype(F32)
    steps = (small_all[:, 9, :seqs].astype(F32) * 64 + small_all[:, 9, seqs : 2 * seqs].astype(F32)).reshape(-1)
    half = width // 2
    place = si * rows + jnp.arange(rows)
    freq = jnp.exp(-math.log(10000.0) * (place % half).astype(F32) / half)
    angles = steps[:, None] * freq[None, :]
    sinus_rows = jnp.where(place < half, jnp.sin(angles), jnp.cos(angles)).astype(BF16)
    te = dot(sinus_rows, w_time)
    up_own, up_y, up_c, up_yc = step(up_kernel, [w_up], [((rows, ff), BF16)] * 4, 2)
    ups = [up_own, swap(up_y, "y"), swap(up_c, "c"), across_seq(up_yc)]
    (te_a,) = step(add_kernel, [te, swap(te, "y")], [((4 * seqs, width), F32)], 1, behind=[far_own])
    te_b = swap(te_a, "c")
    (go_send,) = step(pick_kernel, [grad_out], [((piece, width), BF16)], 1)
    go_far = swap(go_send, "h")

    attn_in, qkv_t, o_full, o_send, lse, w_t = step(
        attend_kernel, [*toks, *fars, te_a, te_b, vec, small_all, wq_own, wq_y, wq_c, wq_yc],
        [((4, own, width), BF16), ((4, 3 * part, own), BF16), ((4, part, own), F32), ((4, part, own), BF16),
         ((4 * heads, 8, own), F32), ((3 * part, width), BF16)],
        15, [pltpu.VMEM((4, rows, 3 * part), BF16)], ups[1:],
    )
    attn = members(o_send)
    (go_own,) = step(own_kernel, [grad_out, go_far], [((own, width), BF16)], 1)
    go_all = lax.all_gather(go_own, ("y", "c"))
    mlp_own, hidden_two, a_own, a_y, a_c, a_yc = step(
        branch_kernel, [attn, w_out_f, tok_own, far_own, te_a, te_b, vec],
        [((own, width), BF16), ((own, width), F32)] + [((part, own), BF16)] * 4, 3,
    )
    mlp_y = swap(mlp_own, "y")
    mlp_c = swap(mlp_own, "c")
    mlp_yc = swap(mlp_y, "c")
    mlps = [mlp_own, mlp_y, mlp_c, mlp_yc]
    a_s = [a_own, swap(a_y, "y"), swap(a_c, "c"), across_seq(a_yc)]
    two = (2, own, width)
    gm_own, gm_far, gm_send, out_own, out_far, out_send, act_all, gp_all = step(
        feed_kernel, [*mlps, go_all, *ups, w_down, b_up.astype(F32).reshape(1, ff)],
        [*[((own, width), F32)] * 2, (two, BF16), *[((own, width), F32)] * 2, (two, BF16), *[((4, own, ff), BF16)] * 2], 10,
        [pltpu.VMEM((width, ff), BF16)], a_s[1:],
    )
    gm_c = swap(gm_send, "c")
    out_c = swap(out_send, "c")
    (gm_pair,) = step(second_kernel, [gm_far, gm_c], [((own, width), BF16)], 1)
    gm_y = swap(gm_pair, "y")
    quarters = [((ff // 4 + 16, width), BF16)] * 4 + [((4, rows // 4, ff), BF16)] * 4
    *gd, gu_own, gu_x, gu_z, gu_d = step(
        feed_grad_kernel, [*mlps, go_all, act_all, gp_all], quarters, 7, [pltpu.VMEM((width, width), BF16)]
    )
    gds = trade4(*gd)
    grad_two, branch, ga_send, sums_two = step(
        back_kernel, [gm_own, gm_c, gm_y, hidden_two, go_own, w_out_f, vec],
        [((own, width), F32), ((own, width), BF16), ((4, part, own), BF16), ((8, width), F32)], 4,
    )
    ga = members(ga_send)
    branch_s = lax.all_gather(branch, ("y", "c"))
    (out_pair,) = step(second_kernel, [out_far, out_c], [((own, width), BF16)], 1)
    out_y = swap(out_pair, "y")
    gus = trade4(gu_own, gu_x, gu_z, gu_d)

    dqkv_t, gh_own, gh_x, gh_z, gh_d, sums_one = step(
        attend_back_kernel, [qkv_t, lse, o_full, ga, w_t, *toks, *fars, te_a, te_b, vec],
        [((4, 3 * part, own), BF16)] + [((own, width), BF16)] * 4 + [((8, width), F32)],
        15, [pltpu.VMEM((HEAD_DIM, 4 * own), F32)] * 2,
    )
    ghs = trade4(gh_own, gh_x, gh_z, gh_d)
    (gd_sum,) = step(total4_kernel, gds, [((ff // 4 + 16, width), BF16)], 1)
    gd_h = swap(gd_sum, "h")
    chain = (2, rows + 32, 3 * part)
    ch_keep, ch_give = step(qkv_grad_kernel, [attn_in, dqkv_t, sums_two, sums_one], [(chain, BF16), (chain, BF16)], 5)
    ch_c = swap(ch_give, "c")
    (gu_sum,) = step(total4_kernel, gus, [((4, rows // 4, ff), BF16)], 1)
    gu_h = swap(gu_sum, "h")
    folded = ((rows // 4 + rows // 12, 3 * part), BF16)
    wo = step(out_grad_kernel, [*a_s, branch_s], [folded] * 4, 2, [pltpu.VMEM((rows, width), BF16)])
    wos = trade4(*wo)
    first, second = step(chain_kernel, [ch_keep, ch_c], [(chain[1:], BF16)] * 2, 1)
    ch_y = swap(second, "y")
    (gd_sum,) = step(both_kernel, [gd_sum, gd_h], [((ff // 4 + 16, width), BF16)], 1)
    gds = gather4(gd_sum)
    out_mine, out_other = step(
        out_kernel, [hidden_two, out_own, out_c, out_y, vec], [((piece, width), BF16), ((piece, width), BF16)], 2
    )
    out_recv = swap(out_other, "h")
    joined = ((rows + 32 + rows // 3, 3 * part), BF16)
    (now,) = step(join_kernel, [first, ch_y, *wos], [joined], 1)
    ch_h = swap(now, "h")
    (gu_sum,) = step(both_kernel, [gu_sum, gu_h], [((4, rows // 4, ff), BF16)], 1)
    gu_s = lax.all_to_all(gu_sum, ("y", "c"), split_axis=0, concat_axis=0, tiled=True)
    gt_mine, gt_other = step(
        hidden_grad_kernel, [grad_two, *ghs], [((piece, width), BF16), ((piece, width), BF16)], 2
    )
    gt_recv = swap(gt_other, "h")
    (now,) = step(both_kernel, [now, ch_h], [joined], 1)
    gqs = gather4(now)
    gus = gather4(gu_s)
    (output,) = step(pair_kernel, [out_mine, out_recv], [((seqs, piece, width), BF16)], 1.5)
    (grad_tokens,) = step(pair_kernel, [gt_mine, gt_recv], [((seqs, piece, width), BF16)], 1.5)
    t_qkv, t_out, total_w_time, tv, embeds = step(
        total_kernel, [*gqs, sinus_rows.astype(F32)],
        [((rows, 3 * width), F32), ((4, rows // 4, width), F32), ((rows, width), F32), ((8, 3 * part), F32),
         ((8, width), F32)],
        3, [pltpu.VMEM((32, 3 * part), F32)],
    )
    t_down, t_up, t_small = step(
        feed_total_kernel, [*gds, *gus],
        [((4, ff // 4, width), F32), ((4, rows // 4, 4 * ff), F32), ((16, width), F32)], 4,
    )
    total_b_time = lax.dynamic_slice_in_dim(jnp.sum(embeds, 0), si * rows, rows, 0)
    total_b_down = lax.dynamic_slice_in_dim(t_small[1], si * rows, rows, 0)
    return (
        output, grad_tokens, total_w_time, total_b_time, tv[3, :rows], tv[4, :rows], t_qkv,
        tv[5, :part], tv[5, 2 * part :], t_out.reshape(rows, width), tv[2, :rows], tv[0, :rows], tv[1, :rows],
        t_up.reshape(rows, 4 * ff), t_small[0], t_down.reshape(ff, width), total_b_down,
    )


def solution(mesh):
    placed = (
        P("seq", "ctx", None),
        P("seq", "ctx", None),
        P("seq"),
        P("seq", None),
        P("seq"),
        P("seq"),
        P("seq"),
        P("seq", None),
        P("seq"),
        P("seq"),
        P("seq", None),
        P("seq"),
        P("seq"),
        P("seq"),
        P("seq", None),
        P("seq"),
        P("seq", None),
        P("seq"),
    )
    out_placed = (
        P("seq", "ctx", None),
        P("seq", "ctx", None),
        P("seq", None),
        P("seq"),
        P("seq"),
        P("seq"),
        P("seq", None),
        P("seq"),
        P("seq"),
        P("seq", None),
        P("seq"),
        P("seq"),
        P("seq"),
        P("seq", None),
        P("seq"),
        P("seq", None),
        P("seq"),
    )
    sizes = dict(mesh.shape)
    if sizes["seq"] == 4 and sizes["ctx"] == 8:
        fine = Mesh(mesh.devices.reshape((2,) * 5), ("y", "c", "h", "zl", "x"))
        split = {"seq": ("y", "c"), "ctx": ("h", "zl", "x"), None: None}

        def finer(spec):
            return P(*(split[axis] for axis in spec))

        return jax.shard_map(
            group_body,
            mesh=fine,
            in_specs=tuple(finer(spec) for spec in placed),
            out_specs=tuple(finer(spec) for spec in out_placed),
            check_vma=False,
        )
    return jax.shard_map(
        body,
        mesh=mesh,
        in_specs=placed,
        out_specs=out_placed,
        check_vma=False,
    )
```

```python
import math

import jax
import jax.numpy as jnp
from jax import lax
from jax.experimental import pallas as pl
from jax.experimental.pallas import tpu as pltpu
from jax.sharding import Mesh
from jax.sharding import PartitionSpec as P

HEADS = 12
HEAD_DIM = 64


norm_eps = 1e-05
block_keys = 1024


def layer_norm(hidden, norm_gain, offset):
    center = hidden - jnp.mean(hidden, axis=-1, keepdims=True)
    variance = jnp.mean(center * center, axis=-1, keepdims=True)
    return center * lax.rsqrt(variance + norm_eps) * norm_gain + offset


def gelu_exact(values):
    return jax.nn.gelu(values, approximate=False)


def sinusoid(timestep, model_width):
    half_width = model_width // 2
    frequency = jnp.exp(
        -math.log(10000.0) * jnp.arange(half_width).astype(jnp.float32) / half_width
    )
    angles = timestep.astype(jnp.float32)[:, None] * frequency[None, :]
    return jnp.concatenate([jnp.sin(angles), jnp.cos(angles)], axis=-1)


def scores_of(queries, keys_blk, score_scale):
    return score_scale * jnp.einsum(
        "sphe,skhe->shpk", queries, keys_blk, preferred_element_type=jnp.float32
    )


def token_sum(values):
    return jnp.sum(values.astype(jnp.float32), axis=(0, 1))


def softmax_totals(query_low, key_all, score_scale, block_len):
    seq_count, row_count, head_count, head_width = query_low.shape
    blocks = key_all.shape[1] // block_len

    def softmax_block_step(carry, block_index):
        top_now, running = carry
        keys_blk = lax.dynamic_slice_in_dim(key_all, block_index * block_len, block_len, 1)
        scores = scores_of(query_low, keys_blk, score_scale)
        top_new = jnp.maximum(top_now, jnp.max(scores, axis=-1))
        running = running * jnp.exp(top_now - top_new) + jnp.sum(
            jnp.exp(scores - top_new[..., None]), axis=-1
        )
        return ((top_new, running), None)

    initial = (
        jnp.full((seq_count, head_count, row_count), -jnp.inf, jnp.float32),
        jnp.zeros((seq_count, head_count, row_count), jnp.float32),
    )
    (top_now, running), unused = lax.scan(softmax_block_step, initial, jnp.arange(blocks))
    return top_now + jnp.log(running)


def attend(query_low, key_all, value_all, log_totals, score_scale, block_len):
    blocks = key_all.shape[1] // block_len

    def attend_block_step(running, block_index):
        offset = block_index * block_len
        keys_blk = lax.dynamic_slice_in_dim(key_all, offset, block_len, 1)
        values_blk = lax.dynamic_slice_in_dim(value_all, offset, block_len, 1)
        probs_low = jnp.exp(
            scores_of(query_low, keys_blk, score_scale) - log_totals[..., None]
        ).astype(jnp.bfloat16)
        running = running + jnp.einsum(
            "shpk,skhe->sphe", probs_low, values_blk, preferred_element_type=jnp.float32
        )
        return (running, None)

    result, unused = lax.scan(
        attend_block_step, jnp.zeros(query_low.shape, jnp.float32), jnp.arange(blocks)
    )
    return result


def backward_reduce(
    query_low, key_all, value_all, grad_attn, log_totals, delta, score_scale, block_len
):
    blocks = key_all.shape[1] // block_len

    def backward_block_step(carry, block_index):
        grad_query, grad_key, grad_value = carry
        offset = block_index * block_len
        keys_blk = lax.dynamic_slice_in_dim(key_all, offset, block_len, 1)
        values_blk = lax.dynamic_slice_in_dim(value_all, offset, block_len, 1)
        weights = jnp.exp(scores_of(query_low, keys_blk, score_scale) - log_totals[..., None])
        probs_low = weights.astype(jnp.bfloat16)
        value_part = jnp.einsum(
            "shpk,sphe->skhe", probs_low, grad_attn, preferred_element_type=jnp.float32
        )
        grad_probs = jnp.einsum(
            "sphe,skhe->shpk", grad_attn, values_blk, preferred_element_type=jnp.float32
        )
        grad_scores = (weights * (grad_probs - delta[..., None])).astype(jnp.bfloat16)
        grad_query = grad_query + score_scale * jnp.einsum(
            "shpk,skhe->sphe", grad_scores, keys_blk, preferred_element_type=jnp.float32
        )
        key_part = score_scale * jnp.einsum(
            "shpk,sphe->skhe", grad_scores, query_low, preferred_element_type=jnp.float32
        )
        grad_key = lax.dynamic_update_slice_in_dim(grad_key, key_part, offset, 1)
        grad_value = lax.dynamic_update_slice_in_dim(grad_value, value_part, offset, 1)
        return ((grad_query, grad_key, grad_value), None)

    initial = (
        jnp.zeros(query_low.shape, jnp.float32),
        jnp.zeros(key_all.shape, jnp.float32),
        jnp.zeros(value_all.shape, jnp.float32),
    )
    result, unused = lax.scan(backward_block_step, initial, jnp.arange(blocks))
    return result


def body(
    tokens,
    grad_out,
    timestep,
    w_time,
    b_time,
    ln1_gain,
    ln1_bias,
    w_qkv,
    b_query,
    b_value,
    w_out,
    b_out,
    ln2_gain,
    ln2_bias,
    w_up,
    b_up,
    w_down,
    b_down,
):
    (
        time_full,
        time_bias,
        gain_one,
        bias_one,
        qkv_full,
        query_bias,
        value_bias,
        out_full,
        out_bias,
        gain_two,
        bias_two,
        up_full,
        up_bias,
        down_full,
        down_bias,
    ) = (
        lax.all_gather(w_time, "seq", axis=0, tiled=True),
        lax.all_gather(b_time, "seq", axis=0, tiled=True),
        lax.all_gather(ln1_gain, "seq", axis=0, tiled=True),
        lax.all_gather(ln1_bias, "seq", axis=0, tiled=True),
        lax.all_gather(w_qkv, "seq", axis=0, tiled=True),
        lax.all_gather(b_query, "seq", axis=0, tiled=True),
        lax.all_gather(b_value, "seq", axis=0, tiled=True),
        lax.all_gather(w_out, "seq", axis=0, tiled=True),
        lax.all_gather(b_out, "seq", axis=0, tiled=True),
        lax.all_gather(ln2_gain, "seq", axis=0, tiled=True),
        lax.all_gather(ln2_bias, "seq", axis=0, tiled=True),
        lax.all_gather(w_up, "seq", axis=0, tiled=True),
        lax.all_gather(b_up, "seq", axis=0, tiled=True),
        lax.all_gather(w_down, "seq", axis=0, tiled=True),
        lax.all_gather(b_down, "seq", axis=0, tiled=True),
    )
    seq_count, piece_len, model_width = tokens.shape
    score_scale = 1.0 / math.sqrt(HEAD_DIM)
    split_shape = (seq_count, piece_len, HEADS, HEAD_DIM)
    flat_shape = (seq_count, piece_len, model_width)
    sinus_low = sinusoid(timestep, model_width).astype(jnp.bfloat16)
    time_embed = jnp.dot(
        sinus_low, time_full, preferred_element_type=jnp.float32
    ) + time_bias.astype(jnp.float32)
    hidden = tokens.astype(jnp.float32) + time_embed[:, None, :]
    attn_in = layer_norm(hidden, gain_one.astype(jnp.float32), bias_one.astype(jnp.float32)).astype(
        jnp.bfloat16
    )
    qkv_bias = jnp.concatenate([query_bias, jnp.zeros_like(query_bias), value_bias]).astype(
        jnp.float32
    )
    projected = (
        jnp.einsum("spd,de->spe", attn_in, qkv_full, preferred_element_type=jnp.float32) + qkv_bias
    )
    query_low = projected[..., :model_width].astype(jnp.bfloat16).reshape(split_shape)
    key_low = (
        projected[..., model_width : 2 * model_width].astype(jnp.bfloat16).reshape(split_shape)
    )
    value_low = projected[..., 2 * model_width :].astype(jnp.bfloat16).reshape(split_shape)
    key_all, value_all = (
        lax.all_gather(key_low, "ctx", axis=1, tiled=True),
        lax.all_gather(value_low, "ctx", axis=1, tiled=True),
    )
    block_len = min(key_all.shape[1], block_keys)
    log_totals = softmax_totals(query_low, key_all, score_scale, block_len)
    attn = attend(query_low, key_all, value_all, log_totals, score_scale, block_len)
    attn_low = attn.reshape(flat_shape).astype(jnp.bfloat16)
    hidden_two = (
        hidden
        + jnp.einsum("spd,de->spe", attn_low, out_full, preferred_element_type=jnp.float32)
        + out_bias.astype(jnp.float32)
    )
    mlp_in = layer_norm(
        hidden_two, gain_two.astype(jnp.float32), bias_two.astype(jnp.float32)
    ).astype(jnp.bfloat16)
    pre_act = jnp.einsum(
        "spd,df->spf", mlp_in, up_full, preferred_element_type=jnp.float32
    ) + up_bias.astype(jnp.float32)
    act_low = gelu_exact(pre_act).astype(jnp.bfloat16)
    output = (
        hidden_two
        + jnp.einsum("spf,fd->spd", act_low, down_full, preferred_element_type=jnp.float32)
        + down_bias.astype(jnp.float32)
    ).astype(jnp.bfloat16)
    qkv_back, out_back, up_back, down_back, gain_one_back, gain_two_back = (
        lax.all_gather(w_qkv, "seq", axis=0, tiled=True),
        lax.all_gather(w_out, "seq", axis=0, tiled=True),
        lax.all_gather(w_up, "seq", axis=0, tiled=True),
        lax.all_gather(w_down, "seq", axis=0, tiled=True),
        lax.all_gather(ln1_gain, "seq", axis=0, tiled=True),
        lax.all_gather(ln2_gain, "seq", axis=0, tiled=True),
    )
    grad_w_down = jnp.einsum("spf,spd->fd", act_low, grad_out, preferred_element_type=jnp.float32)
    grad_b_down = token_sum(grad_out)
    grad_act = jnp.einsum("spd,fd->spf", grad_out, down_back, preferred_element_type=jnp.float32)
    unused, gelu_pull = jax.vjp(gelu_exact, pre_act)
    grad_pre = gelu_pull(grad_act)[0].astype(jnp.bfloat16)
    grad_w_up = jnp.einsum("spd,spf->df", mlp_in, grad_pre, preferred_element_type=jnp.float32)
    grad_b_up = token_sum(grad_pre)
    grad_mlp = jnp.einsum("spf,df->spd", grad_pre, up_back, preferred_element_type=jnp.float32)
    unused, norm_two_pull = jax.vjp(
        layer_norm, hidden_two, gain_two_back.astype(jnp.float32), bias_two.astype(jnp.float32)
    )
    grad_hidden_two, grad_ln2_gain, grad_ln2_bias = norm_two_pull(grad_mlp)
    grad_hidden_two = grad_hidden_two + grad_out.astype(jnp.float32)
    grad_branch = grad_hidden_two.astype(jnp.bfloat16)
    grad_w_out = jnp.einsum(
        "spd,spe->de", attn_low, grad_branch, preferred_element_type=jnp.float32
    )
    grad_b_out = token_sum(grad_branch)
    grad_attn = (
        jnp.einsum("spe,de->spd", grad_branch, out_back, preferred_element_type=jnp.float32)
        .astype(jnp.bfloat16)
        .reshape(split_shape)
    )
    delta = jnp.transpose(jnp.sum(grad_attn.astype(jnp.float32) * attn, axis=-1), (0, 2, 1))
    grad_query, key_terms, value_terms = backward_reduce(
        query_low, key_all, value_all, grad_attn, log_totals, delta, score_scale, block_len
    )
    grad_key, grad_value = (
        lax.psum_scatter(key_terms, "ctx", scatter_dimension=1, tiled=True),
        lax.psum_scatter(value_terms, "ctx", scatter_dimension=1, tiled=True),
    )
    grad_qkv = jnp.concatenate(
        [
            grad_query.reshape(flat_shape),
            grad_key.reshape(flat_shape),
            grad_value.reshape(flat_shape),
        ],
        axis=-1,
    ).astype(jnp.bfloat16)
    grad_w_qkv = jnp.einsum("spd,spe->de", attn_in, grad_qkv, preferred_element_type=jnp.float32)
    grad_b_query = token_sum(grad_qkv[..., :model_width])
    grad_b_value = token_sum(grad_qkv[..., 2 * model_width :])
    grad_norm = jnp.einsum("spe,de->spd", grad_qkv, qkv_back, preferred_element_type=jnp.float32)
    unused, norm_one_pull = jax.vjp(
        layer_norm, hidden, gain_one_back.astype(jnp.float32), bias_one.astype(jnp.float32)
    )
    grad_hidden_part, grad_ln1_gain, grad_ln1_bias = norm_one_pull(grad_norm)
    grad_hidden = grad_hidden_two + grad_hidden_part
    grad_tokens = grad_hidden.astype(jnp.bfloat16)
    grad_embed = jnp.sum(grad_hidden, axis=1)
    grad_w_time = jnp.einsum(
        "sd,se->de", sinus_low.astype(jnp.float32), grad_embed, precision=lax.Precision.HIGHEST
    )
    grad_b_time = jnp.sum(grad_embed, axis=0)
    shares = (
        lax.psum_scatter(
            grad_w_time.astype(jnp.bfloat16), "seq", scatter_dimension=0, tiled=True
        ).astype(jnp.float32),
        lax.psum_scatter(
            grad_b_time.astype(jnp.bfloat16), "seq", scatter_dimension=0, tiled=True
        ).astype(jnp.float32),
        lax.psum_scatter(
            grad_ln1_gain.astype(jnp.bfloat16), "seq", scatter_dimension=0, tiled=True
        ).astype(jnp.float32),
        lax.psum_scatter(
            grad_ln1_bias.astype(jnp.bfloat16), "seq", scatter_dimension=0, tiled=True
        ).astype(jnp.float32),
        lax.psum_scatter(
            grad_w_qkv.astype(jnp.bfloat16), "seq", scatter_dimension=0, tiled=True
        ).astype(jnp.float32),
        lax.psum_scatter(
            grad_b_query.astype(jnp.bfloat16), "seq", scatter_dimension=0, tiled=True
        ).astype(jnp.float32),
        lax.psum_scatter(
            grad_b_value.astype(jnp.bfloat16), "seq", scatter_dimension=0, tiled=True
        ).astype(jnp.float32),
        lax.psum_scatter(
            grad_w_out.astype(jnp.bfloat16), "seq", scatter_dimension=0, tiled=True
        ).astype(jnp.float32),
        lax.psum_scatter(
            grad_b_out.astype(jnp.bfloat16), "seq", scatter_dimension=0, tiled=True
        ).astype(jnp.float32),
        lax.psum_scatter(
            grad_ln2_gain.astype(jnp.bfloat16), "seq", scatter_dimension=0, tiled=True
        ).astype(jnp.float32),
        lax.psum_scatter(
            grad_ln2_bias.astype(jnp.bfloat16), "seq", scatter_dimension=0, tiled=True
        ).astype(jnp.float32),
        lax.psum_scatter(
            grad_w_up.astype(jnp.bfloat16), "seq", scatter_dimension=0, tiled=True
        ).astype(jnp.float32),
        lax.psum_scatter(
            grad_b_up.astype(jnp.bfloat16), "seq", scatter_dimension=0, tiled=True
        ).astype(jnp.float32),
        lax.psum_scatter(
            grad_w_down.astype(jnp.bfloat16), "seq", scatter_dimension=0, tiled=True
        ).astype(jnp.float32),
        lax.psum_scatter(
            grad_b_down.astype(jnp.bfloat16), "seq", scatter_dimension=0, tiled=True
        ).astype(jnp.float32),
    )
    (
        total_w_time,
        total_b_time,
        total_ln1_gain,
        total_ln1_bias,
        total_w_qkv,
        total_b_query,
        total_b_value,
        total_w_out,
        total_b_out,
        total_ln2_gain,
        total_ln2_bias,
        total_w_up,
        total_b_up,
        total_w_down,
        total_b_down,
    ) = lax.psum(
        (
            shares[0],
            shares[1],
            shares[2],
            shares[3],
            shares[4],
            shares[5],
            shares[6],
            shares[7],
            shares[8],
            shares[9],
            shares[10],
            shares[11],
            shares[12],
            shares[13],
            shares[14],
        ),
        "ctx",
    )
    return (
        output,
        grad_tokens,
        total_w_time,
        total_b_time,
        total_ln1_gain,
        total_ln1_bias,
        total_w_qkv,
        total_b_query,
        total_b_value,
        total_w_out,
        total_b_out,
        total_ln2_gain,
        total_ln2_bias,
        total_w_up,
        total_b_up,
        total_w_down,
        total_b_down,
    )


F32 = jnp.float32
BF16 = jnp.bfloat16
VMEM_BYTES = 56 * 1024 * 1024
RATE = 1.15e9


def swap(value, axis):
    return lax.ppermute(value, axis, [(0, 1), (1, 0)])


def across(value):
    return lax.ppermute(value, ("zl", "x"), [(i, i ^ 3) for i in range(4)])


def pick(value, index):
    return lax.dynamic_index_in_dim(value, index, 0, keepdims=False)


def dot(left, right, left_dim=1, right_dim=0):
    return lax.dot_general(
        left, right, (((left_dim,), (right_dim,)), ((), ())), preferred_element_type=F32
    )


class Values:
    pass


class Steps:
    def __init__(self, ids):
        self.ids = ids
        self.last = None

    def __call__(self, kernel, micros, inputs, outputs, scratch=(), behind=()):
        behind = [*behind] + ([self.last] if self.last is not None else [])
        shapes = [jax.ShapeDtypeStruct(shape, dtype) for shape, dtype in outputs]
        count = 1 + len(inputs)

        def run(*refs):
            kernel(*refs[:count], *refs[count + len(behind) :])

        results = pl.pallas_call(
            run,
            out_shape=shapes,
            in_specs=[pl.BlockSpec(memory_space=pltpu.SMEM)]
            + [pl.BlockSpec(memory_space=pltpu.VMEM)] * len(inputs)
            + [pl.BlockSpec(memory_space=pl.ANY)] * len(behind),
            out_specs=[pl.BlockSpec(memory_space=pltpu.VMEM)] * len(shapes),
            scratch_shapes=list(scratch),
            compiler_params=pltpu.CompilerParams(vmem_limit_bytes=VMEM_BYTES),
            cost_estimate=pl.CostEstimate(
                flops=int(micros * RATE), bytes_accessed=1, transcendentals=0
            ),
            name=kernel.__name__,
        )(self.ids, *inputs, *behind)
        self.last = results[0]
        return results


SEQ, MEMBER, HALF = 0, 1, 2


def normalize(hidden):
    center = hidden - jnp.mean(hidden, axis=-1, keepdims=True)
    rstd = lax.rsqrt(jnp.mean(center * center, axis=-1, keepdims=True) + norm_eps)
    return center * rstd, rstd


def norm_back(e, x, r):
    return r * (e - jnp.mean(e, -1, keepdims=True) - x * jnp.mean(e * x, -1, keepdims=True))


def token_kernel(ids, tokens, mine, far, blank):
    blank[...] = jnp.zeros(blank.shape, blank.dtype)
    mine[...] = tokens[ids[HALF]]
    far[...] = tokens[1 - ids[HALF]]


def pick_kernel(ids, grad_out, far):
    far[...] = grad_out[1 - ids[HALF]]


def column_kernel(ids, w_qkv, out):
    part = w_qkv.shape[1] // 12
    width = w_qkv.shape[1] // 3
    for member in range(4):

        @pl.when(ids[MEMBER] == member)
        def _():
            for t in range(3):
                at = t * width + member * part
                value = w_qkv[:, at : at + part]
                for block in range(4):
                    out[block, :, t * part : (t + 1) * part] = value


def up_kernel(ids, w_up, own, y, c, yc):
    ff = own.shape[1]
    for ref, flip in ((own, 0), (y, 2), (c, 1), (yc, 3)):
        ref[...] = w_up[:, pl.ds(pl.multiple_of((ids[SEQ] ^ flip) * ff, ff), ff)]


def own_kernel(ids, grad_out, far, w_out, own, copy):
    copy[...] = w_out[...]
    half = far.shape[0]
    own[:half] = grad_out[ids[HALF]]
    own[half:] = far[...]


def second_kernel(ids, keep, recv, out):
    out[...] = (keep[...].astype(F32) + recv[1].astype(F32)).astype(BF16)


def both_kernel(ids, left, right, out):
    out[...] = (left[...].astype(F32) + right[...].astype(F32)).astype(BF16)


def chain_kernel(ids, keep, c, first, second):
    first[...] = (keep[0].astype(F32) + c[0].astype(F32)).astype(BF16)
    second[...] = (keep[1].astype(F32) + c[1].astype(F32)).astype(BF16)


def join_kernel(ids, first, y, a, b, c, d, out):
    rows = first.shape[0]
    out[:rows] = (first[...].astype(F32) + y[...].astype(F32)).astype(BF16)
    total = a[...].astype(F32) + b[...].astype(F32) + c[...].astype(F32) + d[...].astype(F32)
    out[rows:] = total.astype(BF16)


def pieces_kernel(ids, a, b, c, d, down, up):
    total = a[...].astype(F32) + b[...].astype(F32) + c[...].astype(F32) + d[...].astype(F32)
    low = total.astype(BF16)
    rows = down.shape[0]
    fine = up.shape[1]
    down[...] = low[:rows]
    for s in range(4):
        up[s] = low[rows + s * fine : rows + (s + 1) * fine]


def attend_kernel(
    ids, tok_own, tok_x, tok_z, tok_d, far_own, far_x, far_z, far_d, sinus, w_time, vec, small, wq,
    attn_in, qkv_t, o_full, o_send, lse, w_t, te,
):
    piece, width = tok_own.shape
    part = width // 4
    rows = wq.shape[1]
    own = 2 * piece
    gi = ids[MEMBER]
    for block in range(4):
        w_t[:, block * rows : (block + 1) * rows] = wq[block].T
    te[...] = dot(sinus[...], w_time[...]) + vec[0:1, :]
    te_row = te[0:1, :]
    gain, offset = vec[1:2, :], vec[2:3, :]
    bias = small[gi].astype(F32).T
    pairs = ((tok_own, far_own), (tok_x, far_x), (tok_z, far_z), (tok_d, far_d))
    for block, (tok, far) in enumerate(pairs):
        normed, _ = normalize(jnp.concatenate([tok[...], far[...]]).astype(F32) + te_row)
        low = (normed * gain + offset).astype(BF16)
        attn_in[block] = low
        qkv = dot(w_t[...], low, 1, 1)
        qkv_t[block, 0:part, :] = (qkv[:part] + bias[:, 3:4]).astype(BF16)
        qkv_t[block, part : 2 * part, :] = qkv[part : 2 * part].astype(BF16)
        qkv_t[block, 2 * part :, :] = (qkv[2 * part :] + bias[:, 4:5]).astype(BF16)

    @pl.loop(0, part // HEAD_DIM)
    def _(head):
        at = pl.multiple_of(head * HEAD_DIM, HEAD_DIM)
        k_t = jnp.concatenate([qkv_t[j, pl.ds(part + at, HEAD_DIM), :] for j in range(4)], 1)
        v_t = jnp.concatenate([qkv_t[j, pl.ds(2 * part + at, HEAD_DIM), :] for j in range(4)], 1)
        for block in range(4):
            q_t = qkv_t[block, pl.ds(at, HEAD_DIM), :] * jnp.asarray(0.125, BF16)
            scores = dot(k_t, q_t, 0, 0)
            top = jnp.max(scores, 0, keepdims=True)
            weights = jnp.exp(scores - top)
            total = jnp.sum(weights, 0, keepdims=True)
            attn = dot(v_t, weights.astype(BF16)) / total
            o_full[block, pl.ds(at, HEAD_DIM), :] = attn
            o_send[gi ^ block, pl.ds(at, HEAD_DIM), :] = attn.astype(BF16)
            lse[head * 4 + block] = jnp.broadcast_to(top + jnp.log(total), (8, own))


def fold(value):
    third = value.shape[0] // 3
    return jnp.concatenate([value[i * third : (i + 1) * third] for i in range(3)], 1)


def unfold(value):
    wide = value.shape[1] // 3
    return jnp.concatenate([value[:, i * wide : (i + 1) * wide] for i in range(3)], 0)


def branch_kernel(
    ids, attn, w_out, tok_own, far_own, te, vec, mlp_in, hidden_two, folds
):
    rows = attn.shape[1]
    te_row = te[0:1, :]
    hidden = jnp.concatenate([tok_own[...], far_own[...]]).astype(F32) + te_row + vec[5:6, :]
    for block in range(4):
        hidden = hidden + dot(attn[block], w_out[block * rows : (block + 1) * rows, :], 0, 0)
    hidden_two[...] = hidden
    normed, _ = normalize(hidden)
    mlp_in[...] = (normed * vec[6:7, :] + vec[7:8, :]).astype(BF16)
    for block in range(4):
        folds[block] = fold(attn[ids[SEQ] ^ block])


def feed_kernel(
    ids, m_own, m_y, m_c, m_yc, go_all, u_own, u_y, u_c, u_yc, w_down, b_up, folds,
    gm_own, gm_pair, gm_send, out_own, out_pair, out_send, act_all, gp_all, w_up,
):
    si = ids[SEQ]
    rows = u_own.shape[0]
    own = m_own.shape[0]
    for ref, flip in ((u_own, 0), (u_y, 2), (u_c, 1), (u_yc, 3)):
        w_up[pl.ds(pl.multiple_of((si ^ flip) * rows, rows), rows), :] = ref[...]
    fine = folds.shape[1]
    out_send[2 * own : 2 * own + fine, :] = folds[1]
    out_send[2 * own + fine :, :] = folds[3]
    for block, (ref, flip) in enumerate(((m_own, 0), (m_y, 2), (m_c, 1), (m_yc, 3))):
        grad_out = go_all[si ^ flip]
        pre = dot(ref[...], w_up[...]) + b_up[...]
        cdf = 0.5 * (1.0 + lax.erf(pre * (0.5**0.5)))
        act = (pre * cdf).astype(BF16)
        grad_act = dot(grad_out, w_down[...], 1, 1)
        slope = cdf + pre * (jnp.exp(-0.5 * pre * pre) * (0.5 / math.pi) ** 0.5)
        grad_pre = (grad_act * slope).astype(BF16)
        act_all[block] = act
        gp_all[block] = grad_pre
        gm = dot(grad_pre, w_up[...], 1, 1)
        out = dot(act, w_down[...])
        if block < 2:
            (gm_own, gm_pair)[block][...] = gm.astype(gm_pair.dtype if block else F32)
            (out_own, out_pair)[block][...] = out.astype(out_pair.dtype if block else F32)
        else:
            gm_send[block - 2] = gm.astype(BF16)
            out_send[(block - 2) * own : (block - 1) * own, :] = out.astype(BF16)


def feed_grad_kernel(
    ids, m_own, m_y, m_c, m_yc, go_all, act_all, gp_all, p_own, p_x, p_z, p_d, grad
):
    si, gi = ids[SEQ], ids[MEMBER]
    width = m_own.shape[1]
    ff = act_all.shape[2]
    part = ff // 4
    rows = width // 4
    fine = rows // 4
    pieces = ((p_own, 0), (p_x, 1), (p_z, 2), (p_d, 3))
    orders = ((m_own, 0), (m_y, 2), (m_c, 1), (m_yc, 3))
    for s in range(4):
        cols = slice(s * part, (s + 1) * part)
        total = jnp.zeros((part, width), F32)
        for block, (_, flip) in enumerate(orders):
            total = total + dot(act_all[block, :, cols], go_all[si ^ flip], 0, 0)
        grad[cols, :] = total.astype(BF16)
    for ref, flip in pieces:
        ref[:part, :] = grad[pl.ds(pl.multiple_of((gi ^ flip) * part, 16), part), :]
    for s in range(4):
        cols = slice(s * rows, (s + 1) * rows)
        total = jnp.zeros((rows, ff), F32)
        for block, (ref, _) in enumerate(orders):
            total = total + dot(ref[:, cols], gp_all[block], 0, 0)
        grad[cols, :] = total.astype(BF16)
    for ref, flip in pieces:
        for s in range(4):
            at = part + 16 + s * fine
            ref[at : at + fine, :] = grad[pl.ds(pl.multiple_of(s * rows + (gi ^ flip) * fine, 16), fine), :]
    b_up = jnp.zeros((1, ff), F32)
    b_down = jnp.zeros((1, width), F32)
    for block in range(4):
        b_up = b_up + jnp.sum(gp_all[block].astype(F32), 0, keepdims=True)
        b_down = b_down + jnp.sum(go_all[block].astype(F32), 0, keepdims=True)
    line = lax.broadcasted_iota(jnp.int32, (16, width), 0)
    extra = jnp.where(line == 0, b_up, jnp.where(line == 1, b_down, 0.0))
    for ref, flip in pieces:
        ref[part : part + 16, :] = jnp.where(gi == flip, extra, 0.0).astype(BF16)


def back_kernel(
    ids, gm_keep, gm_c, gm_y, hidden_two, go_own, w_out, vec, out_far, out_c, folds,
    grad_two, branch, ga_send, sums, out_pair,
):
    rows = w_out.shape[0] // 4
    grad_mlp = gm_keep[...] + gm_c[0].astype(F32) + gm_y[...].astype(F32)
    normed, rstd = normalize(hidden_two[...])
    grad = go_own[...].astype(F32) + norm_back(grad_mlp * vec[6:7, :], normed, rstd)
    grad_two[...] = grad
    low = grad.astype(BF16)
    branch[...] = low
    for block in range(4):
        ga_send[block] = dot(w_out[block * rows : (block + 1) * rows, :], low, 1, 1).astype(BF16)
    sums[0:1, :] = jnp.sum(grad_mlp * normed, 0, keepdims=True)
    sums[1:2, :] = jnp.sum(grad_mlp, 0, keepdims=True)
    sums[2:3, :] = jnp.sum(low.astype(F32), 0, keepdims=True)
    sums[3:4, :] = jnp.sum(grad, 0, keepdims=True)
    sums[4:8, :] = jnp.zeros((4, sums.shape[1]), F32)
    own = out_far.shape[0]
    fine = folds.shape[1]
    out_pair[:own, :] = (out_far[...].astype(F32) + out_c[own : 2 * own, :].astype(F32)).astype(BF16)
    out_pair[own : own + fine, :] = folds[2]
    out_pair[own + fine :, :] = out_c[2 * own + fine :, :]


def attend_back_kernel(
    ids, qkv_t, lse, o_full, ga, w_t, tok_own, tok_x, tok_z, tok_d, far_own, far_x, far_z, far_d, te, vec,
    dqkv_t, gh_send, sums, dk, dv,
):
    part = o_full.shape[1]
    own = 2 * tok_own.shape[0]
    si, gi = ids[SEQ], ids[MEMBER]

    @pl.loop(0, part // HEAD_DIM)
    def _(head):
        at = pl.multiple_of(head * HEAD_DIM, HEAD_DIM)
        k_t = jnp.concatenate([qkv_t[j, pl.ds(part + at, HEAD_DIM), :] for j in range(4)], 1)
        v_t = jnp.concatenate([qkv_t[j, pl.ds(2 * part + at, HEAD_DIM), :] for j in range(4)], 1)
        for block in range(4):
            q_t = qkv_t[block, pl.ds(at, HEAD_DIM), :] * jnp.asarray(0.125, BF16)
            do_t = ga[gi ^ block, pl.ds(at, HEAD_DIM), :]
            delta = jnp.sum(do_t.astype(F32) * o_full[block, pl.ds(at, HEAD_DIM), :], 0, keepdims=True)
            weights = jnp.exp(dot(k_t, q_t, 0, 0) - lse[head * 4 + block, 0:1, :])
            grad_probs = dot(v_t, do_t, 0, 0)
            grad_scores = (weights * (grad_probs - delta)).astype(BF16)
            value_part = dot(do_t, weights.astype(BF16), 1, 1)
            key_part = dot(q_t, grad_scores, 1, 1)
            dqkv_t[block, pl.ds(at, HEAD_DIM), :] = (dot(k_t, grad_scores) * 0.125).astype(BF16)
            if block == 0:
                dv[...] = value_part
                dk[...] = key_part
            else:
                dv[...] += value_part
                dk[...] += key_part
        for block in range(4):
            lanes = slice(block * own, (block + 1) * own)
            dqkv_t[block, pl.ds(part + at, HEAD_DIM), :] = dk[:, lanes].astype(BF16)
            dqkv_t[block, pl.ds(2 * part + at, HEAD_DIM), :] = dv[:, lanes].astype(BF16)

    te_row = te[0:1, :]
    gain = vec[1:2, :]
    sum_gain = jnp.zeros_like(gain)
    sum_bias = jnp.zeros_like(gain)
    sum_hidden = jnp.zeros_like(gain)
    pairs = ((tok_own, far_own), (tok_x, far_x), (tok_z, far_z), (tok_d, far_d))
    for block, (tok, far) in enumerate(pairs):
        normed, rstd = normalize(jnp.concatenate([tok[...], far[...]]).astype(F32) + te_row)
        grad_norm = dot(dqkv_t[block], w_t[...], 0, 0)
        grad = norm_back(grad_norm * gain, normed, rstd)
        gh_send[gi ^ block] = grad.astype(BF16)
        sum_gain = sum_gain + jnp.sum(grad_norm * normed, 0, keepdims=True)
        sum_bias = sum_bias + jnp.sum(grad_norm, 0, keepdims=True)
        sum_hidden = sum_hidden + jnp.sum(grad, 0, keepdims=True)
    sums[0:1, :] = sum_gain
    sums[1:2, :] = sum_bias
    sums[2:3, :] = sum_hidden
    sums[3:8, :] = jnp.zeros((5, sums.shape[1]), F32)


def qkv_grad_kernel(ids, attn_in, dqkv_t, sums_two, sums_one, keep, give):
    si, gi = ids[SEQ], ids[MEMBER]
    cols = dqkv_t.shape[1]
    part = cols // 3
    rows = part
    width = attn_in.shape[2]
    half = width // 2
    grad = jnp.zeros((cols, width), F32)
    tok_sum = jnp.zeros((16, cols), F32)
    for block in range(4):
        grad = grad + dot(dqkv_t[block], attn_in[block])
        tok_sum = tok_sum + dot(jnp.ones((16, dqkv_t.shape[2]), BF16), dqkv_t[block], 1, 1)
    grad = grad.astype(BF16)
    line = lax.broadcasted_iota(jnp.int32, (32, cols), 0)
    embed = sums_one[2:3, :] + sums_two[3:4, :]
    slot = 8 + 2 * (2 * si + ids[HALF])
    lanes = lax.broadcasted_iota(jnp.int32, (1, cols), 1)
    wide = [jnp.concatenate([e, jnp.zeros((1, cols - half), F32)], 1) for e in (embed[:, :half], embed[:, half:])]
    common = jnp.where(line == slot, wide[0], jnp.where(line == slot + 1, wide[1], 0.0))
    for s in range(4):
        here = slice(s * rows, (s + 1) * rows)
        extra = common
        vectors = (
            sums_two[0:1, here], sums_two[1:2, here], sums_two[2:3, here], sums_one[0:1, here], sums_one[1:2, here],
        )
        for i, vector in enumerate(vectors):
            full = jnp.concatenate([vector, jnp.zeros((1, cols - rows), F32)], 1)
            extra = jnp.where(line == i, full, extra)
        extra = jnp.where((line == 5) & (gi == s), tok_sum[0:1, :], extra)
        block = grad[:, here].T
        flip = si ^ s

        @pl.when(flip % 2 == 0)
        def _():
            keep[flip // 2, :rows, :] = block
            keep[flip // 2, rows:, :] = extra.astype(BF16)

        @pl.when(flip % 2 == 1)
        def _():
            give[flip // 2, :rows, :] = block
            give[flip // 2, rows:, :] = extra.astype(BF16)


def out_grad_kernel(ids, folds, out_c, out_y, branch_s, w_own, w_x, w_z, w_d, low):
    si, gi = ids[SEQ], ids[MEMBER]
    rows = low.shape[0]
    cols = w_own.shape[1]
    fine = rows // 4
    third = fine // 3
    own = branch_s.shape[1]
    third_rows = folds.shape[1]
    grad = dot(unfold(folds[0]), branch_s[si])
    grad = grad + dot(unfold(out_c[2 * own : 2 * own + third_rows, :]), branch_s[si ^ 1])
    grad = grad + dot(unfold(out_y[own : own + third_rows, :]), branch_s[si ^ 2])
    grad = grad + dot(unfold(out_y[own + third_rows :, :]), branch_s[si ^ 3])
    low[...] = grad.astype(BF16)
    for ref, flip in ((w_own, 0), (w_x, 1), (w_z, 2), (w_d, 3)):
        lines = low[pl.ds(pl.multiple_of((gi ^ flip) * fine, 16), fine), :]
        ref[:fine, :] = lines[:, :cols]
        ref[fine:, :] = jnp.concatenate([lines[i * third : (i + 1) * third, cols:] for i in range(3)], 1)


def out_kernel(ids, hidden_two, out_keep, out_c, out_y, vec, mine, other):
    half = mine.shape[0]
    out = hidden_two[...] + vec[8:9, :] + out_keep[...] + out_c[: 2 * half].astype(F32) + out_y[: 2 * half].astype(F32)
    mine[...] = out[:half].astype(BF16)
    other[...] = out[half:].astype(BF16)


def hidden_grad_kernel(ids, grad_two, recv, mine, other):
    half = mine.shape[0]
    grad = grad_two[...]
    for member in range(4):
        grad = grad + recv[member].astype(F32)
    mine[...] = grad[:half].astype(BF16)
    other[...] = grad[half:].astype(BF16)


def down_total_kernel(ids, own, x, z, d, w_down, b_up, b_down):
    gi = ids[MEMBER]
    quarter = w_down.shape[1]
    for ref, flip in ((own, 0), (x, 1), (z, 2), (d, 3)):
        w_down[gi ^ flip] = ref[:quarter, :].astype(F32)

        @pl.when(gi == flip)
        def _():
            b_up[...] = ref[quarter : quarter + 1, :].astype(F32)
            full = ref[quarter : quarter + 2, :].astype(F32)
            rows = b_down.shape[1]
            for s in range(4):

                @pl.when(ids[SEQ] == s)
                def _():
                    b_down[...] = full[1:2, s * rows : (s + 1) * rows]


def up_total_kernel(ids, own, x, z, d, w_up):
    gi = ids[MEMBER]
    ff = own.shape[2]
    for ref, flip in ((own, 0), (x, 1), (z, 2), (d, 3)):
        for s in range(4):
            w_up[gi ^ flip, :, s * ff : (s + 1) * ff] = ref[s].astype(F32)


def total_kernel(ids, g_own, g_x, g_z, g_d, sinus, w_qkv, w_out, w_time, vectors, b_time, totals, embeds):
    si, gi = ids[SEQ], ids[MEMBER]
    rows = w_qkv.shape[0]
    cols = g_own.shape[1]
    width = w_qkv.shape[1] // 3
    part = cols // 3
    fine = rows // 4
    third = fine // 3
    for member in range(4):
        for ref, flip in ((g_own, 0), (g_x, 1), (g_z, 2), (g_d, 3)):

            @pl.when(gi ^ flip == member)
            def _():
                for t in range(3):
                    at = t * width + member * part
                    w_qkv[:, at : at + part] = ref[:rows, t * part : (t + 1) * part].astype(F32)
                lines = ref[rows + 32 :, :].astype(F32)
                w_out[member, :, :cols] = lines[:fine]
                for i in range(3):
                    w_out[member, i * third : (i + 1) * third, cols:] = lines[fine:, i * part : (i + 1) * part]

    small = jnp.zeros((32, cols), F32)
    for ref in (g_own, g_x, g_z, g_d):
        small = small + ref[rows : rows + 32, :].astype(F32)
    vectors[...] = small[:8]
    half = width // 2
    totals[...] = small
    for b in range(8):
        embeds[b : b + 1, :half] = totals[8 + 2 * b : 9 + 2 * b, :half]
        embeds[b : b + 1, half:] = totals[9 + 2 * b : 10 + 2 * b, :half]
    full = jnp.sum(embeds[...], 0, keepdims=True)
    for s in range(4):

        @pl.when(si == s)
        def _():
            b_time[...] = full[:, s * rows : (s + 1) * rows]

    w_time[...] = lax.dot_general(
        sinus[...], embeds[...], (((0,), (0,)), ((), ())), precision=lax.Precision.HIGHEST,
        preferred_element_type=F32,
    )


def pair_kernel(ids, grad_mine, out_mine, grad_other, out_other, grad_tokens, output):
    grad_tokens[ids[HALF]] = grad_mine[...]
    grad_tokens[1 - ids[HALF]] = grad_other[...]
    output[ids[HALF]] = out_mine[...]
    output[1 - ids[HALF]] = out_other[...]


def group_body(
    tokens, grad_out, timestep, w_time, b_time, ln1_gain, ln1_bias, w_qkv, b_query, b_value,
    w_out, b_out, ln2_gain, ln2_bias, w_up, b_up, w_down, b_down,
):
    seqs, piece, width = tokens.shape
    rows = w_qkv.shape[0]
    ff = w_down.shape[0]
    own = 2 * piece
    part = width // 4
    heads = part // HEAD_DIM
    yi, ci = lax.axis_index("y"), lax.axis_index("c")
    hi, zi, xi = lax.axis_index("h"), lax.axis_index("zl"), lax.axis_index("x")
    si = 2 * yi + ci
    gi = 2 * zi + xi
    step = Steps(jnp.stack([si, gi, hi]).astype(jnp.int32))

    def members(value):
        return lax.all_to_all(value, ("zl", "x"), split_axis=0, concat_axis=0, tiled=True)

    def shards(value):
        return lax.all_to_all(value, ("y", "c"), split_axis=0, concat_axis=0, tiled=True)

    def gather4(value):
        return [value, swap(value, "x"), swap(value, "zl"), across(value)]

    def trade4(keep, x, z, d):
        return [keep, swap(x, "x"), swap(z, "zl"), across(d)]

    def across_seq(value):
        return lax.ppermute(value, ("y", "c"), [(i, i ^ 3) for i in range(4)])

    half = width // 2
    hidden_low = ((own, width), BF16)
    hidden_full = ((own, width), F32)
    down = ((ff // 4 + 16, width), BF16)
    up = ((4, rows // 4, ff), BF16)
    packed = ((ff // 4 + 16 + rows, width), BF16)
    chain = (2, rows + 32, 3 * part)
    joined = ((rows + 32 + rows // 3, 3 * part), BF16)
    v = Values()

    def sinusoid_at(steps, place):
        freq = jnp.exp(-math.log(10000.0) * (place % half).astype(F32) / half)
        angles = steps[:, None] * freq[None, :]
        return jnp.where(place < half, jnp.sin(angles), jnp.cos(angles)).astype(BF16)

    w_time_f = lax.all_gather(w_time, ("y", "c"), axis=0, tiled=True)
    here = jnp.broadcast_to(pick(timestep, hi).astype(F32), (8,))
    sinus_here = sinusoid_at(here, jnp.arange(width))

    def token():
        tok_own, tok_far, blank = step(token_kernel, 2, [tokens], [((piece, width), BF16)] * 2 + [((1, rows), BF16)])
        v.blank = blank.reshape(rows)
        v.far_own = swap(tok_far, "h")
        v.toks = gather4(tok_own)
        v.fars = gather4(v.far_own)

    def small_parameters():
        low_bits = (timestep % 64).astype(BF16)
        high_bits = (timestep // 64).astype(BF16)
        steps_row = jnp.concatenate([high_bits, low_bits, jnp.zeros((rows - 2 * seqs,), BF16)])
        small = jnp.stack(
            [b_time, ln1_gain, ln1_bias, b_query, b_value, b_out, ln2_gain, ln2_bias, b_down, steps_row] + [v.blank] * 6
        )
        v.small = lax.all_gather(small, ("y", "c"))
        v.vec = jnp.transpose(v.small, (1, 0, 2)).reshape(16, width).astype(F32)

    def column():
        (blocks,) = step(column_kernel, 2, [w_qkv], [((4, rows, 3 * part), BF16)], behind=[v.small])
        v.wq = shards(blocks)

    def up_weights():
        pieces = step(up_kernel, 2, [w_up], [((rows, ff), BF16)] * 4)
        v.ups = [pieces[0], swap(pieces[1], "y"), swap(pieces[2], "c"), across_seq(pieces[3])]

    def pick_grad():
        (send,) = step(pick_kernel, 2, [grad_out], [((piece, width), BF16)])
        v.go_far = swap(send, "h")

    def attend():
        v.attn_in, v.qkv_t, v.o_full, send, v.lse, v.w_t, v.te = step(attend_kernel, 15, [*v.toks, *v.fars, sinus_here, w_time_f, v.vec, v.small, v.wq],
            [((4, own, width), BF16), ((4, 3 * part, own), BF16), ((4, part, own), F32), ((4, part, own), BF16),
             ((4 * heads, 8, own), F32), ((3 * part, width), BF16), ((8, width), F32)], behind=[v.wq])
        v.attn = members(send)

    def own_grad():
        v.go_own, copy = step(own_kernel, 2, [grad_out, v.go_far, w_out], [hidden_low, ((rows, width), BF16)])
        v.w_out = lax.all_gather(copy, ("y", "c"), axis=0, tiled=True)
        v.go_all = lax.all_gather(v.go_own, ("y", "c"))

    def branch():
        mlp, v.hidden_two, v.folds = step(branch_kernel, 30, [v.attn, v.w_out, v.toks[0], v.far_own, v.te, v.vec],
            [hidden_low, hidden_full, ((4, part // 3, width), BF16)], behind=[*v.ups[1:]])
        y = swap(mlp, "y")
        v.mlps = [mlp, y, swap(mlp, "c"), swap(y, "c")]

    def feed():
        v.gm_own, v.gm_far, gm_send, v.out_own, v.out_far, out_send, v.act, v.gp = step(feed_kernel, 10,
            [*v.mlps, v.go_all, *v.ups, w_down, b_up.astype(F32).reshape(1, ff), v.folds],
            [hidden_full, hidden_low, ((2, own, width), BF16), hidden_full, hidden_low,
             ((2 * own + 2 * part // 3, width), BF16), *[((4, own, ff), BF16)] * 2],
            [pltpu.VMEM((width, ff), BF16)],
        )
        v.gm_c = swap(gm_send, "c")
        v.out_c = swap(out_send, "c")

    def gm_add():
        (pair,) = step(second_kernel, 2, [v.gm_far, v.gm_c], [hidden_low])
        v.gm_y = swap(pair, "y")

    def feed_grad():
        v.ps = trade4(*step(feed_grad_kernel, 7, [*v.mlps, v.go_all, v.act, v.gp], [packed] * 4,
            [pltpu.VMEM((width, width), BF16)],
        ))

    def back():
        v.grad_two, branch_low, send, v.sums_two, pair = step(back_kernel, 5,
            [v.gm_own, v.gm_c, v.gm_y, v.hidden_two, v.go_own, v.w_out, v.vec, v.out_far, v.out_c,
             v.folds],
            [hidden_full, hidden_low, ((4, part, own), BF16), ((8, width), F32), ((own + 2 * part // 3, width), BF16)],
        )
        v.ga = members(send)
        v.branch_s = lax.all_gather(branch_low, ("y", "c"))
        v.out_y = swap(pair, "y")

    def attend_back():
        v.dqkv, gh, v.sums_one = step(attend_back_kernel, 15,
            [v.qkv_t, v.lse, v.o_full, v.ga, v.w_t, *v.toks, *v.fars, v.te, v.vec],
            [((4, 3 * part, own), BF16), ((4, own, width), BF16), ((8, width), F32)],
            [pltpu.VMEM((HEAD_DIM, 4 * own), F32)] * 2,
        )
        v.gh = members(gh)

    def p_sum():
        v.d_low, v.u_low = step(pieces_kernel, 2, v.ps, [down, up])
        v.d_h = swap(v.d_low, "h")
        v.u_h = swap(v.u_low, "h")

    def qkv_grad():
        v.ch_keep, give = step(qkv_grad_kernel, 5, [v.attn_in, v.dqkv, v.sums_two, v.sums_one], [(chain, BF16)] * 2
        )
        v.ch_c = swap(give, "c")

    def out_grad():
        pieces = step(out_grad_kernel, 3, [v.folds, v.out_c, v.out_y, v.branch_s],
            [((rows // 3, 3 * part), BF16)] * 4, [pltpu.VMEM((rows, width), BF16)],
        )
        v.wos = trade4(*pieces)

    def chain_add():
        v.first, second = step(chain_kernel, 2, [v.ch_keep, v.ch_c], [(chain[1:], BF16)] * 2)
        v.ch_y = swap(second, "y")

    def join():
        (v.now,) = step(join_kernel, 2, [v.first, v.ch_y, *v.wos], [joined])
        v.ch_h = swap(v.now, "h")

    def out():
        v.out_mine, other = step(out_kernel, 2, [v.hidden_two, v.out_own, v.out_c, v.out_y, v.vec],
            [((piece, width), BF16)] * 2,
        )
        v.out_h = swap(other, "h")

    def hidden():
        v.gt_mine, other = step(hidden_grad_kernel, 3, [v.grad_two, v.gh], [((piece, width), BF16)] * 2)
        v.gt_h = swap(other, "h")

    def d_add():
        (value,) = step(both_kernel, 2, [v.d_low, v.d_h], [down])
        v.dg = gather4(value)

    def u_add():
        (value,) = step(both_kernel, 2, [v.u_low, v.u_h], [up])
        v.gu_s = shards(value)
        v.ug = gather4(v.gu_s)

    def now_add():
        (value,) = step(both_kernel, 2, [v.now, v.ch_h], [joined])
        v.qg = gather4(value)

    def pair():
        v.grad_tokens, v.output = step(pair_kernel, 2, [v.gt_mine, v.out_mine, v.gt_h, v.out_h], [((seqs, piece, width), BF16)] * 2
        )

    def total():
        steps = (v.small[:, 9, :seqs].astype(F32) * 64 + v.small[:, 9, seqs : 2 * seqs].astype(F32)).reshape(-1)
        sinus_rows = sinusoid_at(steps, si * rows + jnp.arange(rows)).astype(F32)
        v.w_qkv, v.t_out, v.w_time, v.tv, v.b_time = step(total_kernel, 3, [*v.qg, sinus_rows],
            [((rows, 3 * width), F32), ((4, rows // 4, width), F32), ((rows, width), F32), ((8, 3 * part), F32),
             ((1, rows), F32)],
            [pltpu.VMEM((32, 3 * part), F32), pltpu.VMEM((8, width), F32)],
        )

    def down_total():
        v.w_down, v.b_up, v.b_down = step(down_total_kernel, 3, v.dg, [((4, ff // 4, width), F32), ((1, ff), F32), ((1, rows), F32)]
        )

    def up_total():
        (v.w_up,) = step(up_total_kernel, 3, v.ug, [((4, rows // 4, 4 * ff), F32)])

    for run in (
        token, small_parameters, pick_grad, column, up_weights, own_grad, attend, branch, feed, gm_add, feed_grad,
        back, attend_back, out, p_sum, qkv_grad, chain_add, out_grad, join, d_add, hidden, u_add, now_add, down_total,
        total, pair, up_total,
    ):
        run()
    tv = v.tv
    return (
        v.output, v.grad_tokens, v.w_time, v.b_time.reshape(rows), tv[3, :rows], tv[4, :rows], v.w_qkv,
        tv[5, :part], tv[5, 2 * part :], v.t_out.reshape(rows, width), tv[2, :rows], tv[0, :rows], tv[1, :rows],
        v.w_up.reshape(rows, 4 * ff), v.b_up.reshape(ff), v.w_down.reshape(ff, width), v.b_down.reshape(rows),
    )


def solution(mesh):
    placed = (
        P("seq", "ctx", None),
        P("seq", "ctx", None),
        P("seq"),
        P("seq", None),
        P("seq"),
        P("seq"),
        P("seq"),
        P("seq", None),
        P("seq"),
        P("seq"),
        P("seq", None),
        P("seq"),
        P("seq"),
        P("seq"),
        P("seq", None),
        P("seq"),
        P("seq", None),
        P("seq"),
    )
    out_placed = (
        P("seq", "ctx", None),
        P("seq", "ctx", None),
        P("seq", None),
        P("seq"),
        P("seq"),
        P("seq"),
        P("seq", None),
        P("seq"),
        P("seq"),
        P("seq", None),
        P("seq"),
        P("seq"),
        P("seq"),
        P("seq", None),
        P("seq"),
        P("seq", None),
        P("seq"),
    )
    sizes = dict(mesh.shape)
    if sizes["seq"] == 4 and sizes["ctx"] == 8:
        fine = Mesh(mesh.devices.reshape((2,) * 5), ("y", "c", "h", "zl", "x"))
        split = {"seq": ("y", "c"), "ctx": ("h", "zl", "x"), None: None}

        def finer(spec):
            return P(*(split[axis] for axis in spec))

        return jax.shard_map(
            group_body,
            mesh=fine,
            in_specs=tuple(finer(spec) for spec in placed),
            out_specs=tuple(finer(spec) for spec in out_placed),
            check_vma=False,
        )
    return jax.shard_map(
        body,
        mesh=mesh,
        in_specs=placed,
        out_specs=out_placed,
        check_vma=False,
    )
```

```python
import math

import jax
import jax.numpy as jnp
from jax import lax
from jax.experimental import pallas as pl
from jax.experimental.pallas import tpu as pltpu
from jax.sharding import Mesh
from jax.sharding import PartitionSpec as P

HEADS = 12
HEAD_DIM = 64


norm_eps = 1e-05
block_keys = 1024


def layer_norm(hidden, norm_gain, offset):
    center = hidden - jnp.mean(hidden, axis=-1, keepdims=True)
    variance = jnp.mean(center * center, axis=-1, keepdims=True)
    return center * lax.rsqrt(variance + norm_eps) * norm_gain + offset


def gelu_exact(values):
    return jax.nn.gelu(values, approximate=False)


def sinusoid(timestep, model_width):
    half_width = model_width // 2
    frequency = jnp.exp(
        -math.log(10000.0) * jnp.arange(half_width).astype(jnp.float32) / half_width
    )
    angles = timestep.astype(jnp.float32)[:, None] * frequency[None, :]
    return jnp.concatenate([jnp.sin(angles), jnp.cos(angles)], axis=-1)


def scores_of(queries, keys_blk, score_scale):
    return score_scale * jnp.einsum(
        "sphe,skhe->shpk", queries, keys_blk, preferred_element_type=jnp.float32
    )


def token_sum(values):
    return jnp.sum(values.astype(jnp.float32), axis=(0, 1))


def softmax_totals(query_low, key_all, score_scale, block_len):
    seq_count, row_count, head_count, head_width = query_low.shape
    blocks = key_all.shape[1] // block_len

    def softmax_block_step(carry, block_index):
        top_now, running = carry
        keys_blk = lax.dynamic_slice_in_dim(key_all, block_index * block_len, block_len, 1)
        scores = scores_of(query_low, keys_blk, score_scale)
        top_new = jnp.maximum(top_now, jnp.max(scores, axis=-1))
        running = running * jnp.exp(top_now - top_new) + jnp.sum(
            jnp.exp(scores - top_new[..., None]), axis=-1
        )
        return ((top_new, running), None)

    initial = (
        jnp.full((seq_count, head_count, row_count), -jnp.inf, jnp.float32),
        jnp.zeros((seq_count, head_count, row_count), jnp.float32),
    )
    (top_now, running), unused = lax.scan(softmax_block_step, initial, jnp.arange(blocks))
    return top_now + jnp.log(running)


def attend(query_low, key_all, value_all, log_totals, score_scale, block_len):
    blocks = key_all.shape[1] // block_len

    def attend_block_step(running, block_index):
        offset = block_index * block_len
        keys_blk = lax.dynamic_slice_in_dim(key_all, offset, block_len, 1)
        values_blk = lax.dynamic_slice_in_dim(value_all, offset, block_len, 1)
        probs_low = jnp.exp(
            scores_of(query_low, keys_blk, score_scale) - log_totals[..., None]
        ).astype(jnp.bfloat16)
        running = running + jnp.einsum(
            "shpk,skhe->sphe", probs_low, values_blk, preferred_element_type=jnp.float32
        )
        return (running, None)

    result, unused = lax.scan(
        attend_block_step, jnp.zeros(query_low.shape, jnp.float32), jnp.arange(blocks)
    )
    return result


def backward_reduce(
    query_low, key_all, value_all, grad_attn, log_totals, delta, score_scale, block_len
):
    blocks = key_all.shape[1] // block_len

    def backward_block_step(carry, block_index):
        grad_query, grad_key, grad_value = carry
        offset = block_index * block_len
        keys_blk = lax.dynamic_slice_in_dim(key_all, offset, block_len, 1)
        values_blk = lax.dynamic_slice_in_dim(value_all, offset, block_len, 1)
        weights = jnp.exp(scores_of(query_low, keys_blk, score_scale) - log_totals[..., None])
        probs_low = weights.astype(jnp.bfloat16)
        value_part = jnp.einsum(
            "shpk,sphe->skhe", probs_low, grad_attn, preferred_element_type=jnp.float32
        )
        grad_probs = jnp.einsum(
            "sphe,skhe->shpk", grad_attn, values_blk, preferred_element_type=jnp.float32
        )
        grad_scores = (weights * (grad_probs - delta[..., None])).astype(jnp.bfloat16)
        grad_query = grad_query + score_scale * jnp.einsum(
            "shpk,skhe->sphe", grad_scores, keys_blk, preferred_element_type=jnp.float32
        )
        key_part = score_scale * jnp.einsum(
            "shpk,sphe->skhe", grad_scores, query_low, preferred_element_type=jnp.float32
        )
        grad_key = lax.dynamic_update_slice_in_dim(grad_key, key_part, offset, 1)
        grad_value = lax.dynamic_update_slice_in_dim(grad_value, value_part, offset, 1)
        return ((grad_query, grad_key, grad_value), None)

    initial = (
        jnp.zeros(query_low.shape, jnp.float32),
        jnp.zeros(key_all.shape, jnp.float32),
        jnp.zeros(value_all.shape, jnp.float32),
    )
    result, unused = lax.scan(backward_block_step, initial, jnp.arange(blocks))
    return result


def body(
    tokens,
    grad_out,
    timestep,
    w_time,
    b_time,
    ln1_gain,
    ln1_bias,
    w_qkv,
    b_query,
    b_value,
    w_out,
    b_out,
    ln2_gain,
    ln2_bias,
    w_up,
    b_up,
    w_down,
    b_down,
):
    (
        time_full,
        time_bias,
        gain_one,
        bias_one,
        qkv_full,
        query_bias,
        value_bias,
        out_full,
        out_bias,
        gain_two,
        bias_two,
        up_full,
        up_bias,
        down_full,
        down_bias,
    ) = (
        lax.all_gather(w_time, "seq", axis=0, tiled=True),
        lax.all_gather(b_time, "seq", axis=0, tiled=True),
        lax.all_gather(ln1_gain, "seq", axis=0, tiled=True),
        lax.all_gather(ln1_bias, "seq", axis=0, tiled=True),
        lax.all_gather(w_qkv, "seq", axis=0, tiled=True),
        lax.all_gather(b_query, "seq", axis=0, tiled=True),
        lax.all_gather(b_value, "seq", axis=0, tiled=True),
        lax.all_gather(w_out, "seq", axis=0, tiled=True),
        lax.all_gather(b_out, "seq", axis=0, tiled=True),
        lax.all_gather(ln2_gain, "seq", axis=0, tiled=True),
        lax.all_gather(ln2_bias, "seq", axis=0, tiled=True),
        lax.all_gather(w_up, "seq", axis=0, tiled=True),
        lax.all_gather(b_up, "seq", axis=0, tiled=True),
        lax.all_gather(w_down, "seq", axis=0, tiled=True),
        lax.all_gather(b_down, "seq", axis=0, tiled=True),
    )
    seq_count, piece_len, model_width = tokens.shape
    score_scale = 1.0 / math.sqrt(HEAD_DIM)
    split_shape = (seq_count, piece_len, HEADS, HEAD_DIM)
    flat_shape = (seq_count, piece_len, model_width)
    sinus_low = sinusoid(timestep, model_width).astype(jnp.bfloat16)
    time_embed = jnp.dot(
        sinus_low, time_full, preferred_element_type=jnp.float32
    ) + time_bias.astype(jnp.float32)
    hidden = tokens.astype(jnp.float32) + time_embed[:, None, :]
    attn_in = layer_norm(hidden, gain_one.astype(jnp.float32), bias_one.astype(jnp.float32)).astype(
        jnp.bfloat16
    )
    qkv_bias = jnp.concatenate([query_bias, jnp.zeros_like(query_bias), value_bias]).astype(
        jnp.float32
    )
    projected = (
        jnp.einsum("spd,de->spe", attn_in, qkv_full, preferred_element_type=jnp.float32) + qkv_bias
    )
    query_low = projected[..., :model_width].astype(jnp.bfloat16).reshape(split_shape)
    key_low = (
        projected[..., model_width : 2 * model_width].astype(jnp.bfloat16).reshape(split_shape)
    )
    value_low = projected[..., 2 * model_width :].astype(jnp.bfloat16).reshape(split_shape)
    key_all, value_all = (
        lax.all_gather(key_low, "ctx", axis=1, tiled=True),
        lax.all_gather(value_low, "ctx", axis=1, tiled=True),
    )
    block_len = min(key_all.shape[1], block_keys)
    log_totals = softmax_totals(query_low, key_all, score_scale, block_len)
    attn = attend(query_low, key_all, value_all, log_totals, score_scale, block_len)
    attn_low = attn.reshape(flat_shape).astype(jnp.bfloat16)
    hidden_two = (
        hidden
        + jnp.einsum("spd,de->spe", attn_low, out_full, preferred_element_type=jnp.float32)
        + out_bias.astype(jnp.float32)
    )
    mlp_in = layer_norm(
        hidden_two, gain_two.astype(jnp.float32), bias_two.astype(jnp.float32)
    ).astype(jnp.bfloat16)
    pre_act = jnp.einsum(
        "spd,df->spf", mlp_in, up_full, preferred_element_type=jnp.float32
    ) + up_bias.astype(jnp.float32)
    act_low = gelu_exact(pre_act).astype(jnp.bfloat16)
    output = (
        hidden_two
        + jnp.einsum("spf,fd->spd", act_low, down_full, preferred_element_type=jnp.float32)
        + down_bias.astype(jnp.float32)
    ).astype(jnp.bfloat16)
    qkv_back, out_back, up_back, down_back, gain_one_back, gain_two_back = (
        lax.all_gather(w_qkv, "seq", axis=0, tiled=True),
        lax.all_gather(w_out, "seq", axis=0, tiled=True),
        lax.all_gather(w_up, "seq", axis=0, tiled=True),
        lax.all_gather(w_down, "seq", axis=0, tiled=True),
        lax.all_gather(ln1_gain, "seq", axis=0, tiled=True),
        lax.all_gather(ln2_gain, "seq", axis=0, tiled=True),
    )
    grad_w_down = jnp.einsum("spf,spd->fd", act_low, grad_out, preferred_element_type=jnp.float32)
    grad_b_down = token_sum(grad_out)
    grad_act = jnp.einsum("spd,fd->spf", grad_out, down_back, preferred_element_type=jnp.float32)
    unused, gelu_pull = jax.vjp(gelu_exact, pre_act)
    grad_pre = gelu_pull(grad_act)[0].astype(jnp.bfloat16)
    grad_w_up = jnp.einsum("spd,spf->df", mlp_in, grad_pre, preferred_element_type=jnp.float32)
    grad_b_up = token_sum(grad_pre)
    grad_mlp = jnp.einsum("spf,df->spd", grad_pre, up_back, preferred_element_type=jnp.float32)
    unused, norm_two_pull = jax.vjp(
        layer_norm, hidden_two, gain_two_back.astype(jnp.float32), bias_two.astype(jnp.float32)
    )
    grad_hidden_two, grad_ln2_gain, grad_ln2_bias = norm_two_pull(grad_mlp)
    grad_hidden_two = grad_hidden_two + grad_out.astype(jnp.float32)
    grad_branch = grad_hidden_two.astype(jnp.bfloat16)
    grad_w_out = jnp.einsum(
        "spd,spe->de", attn_low, grad_branch, preferred_element_type=jnp.float32
    )
    grad_b_out = token_sum(grad_branch)
    grad_attn = (
        jnp.einsum("spe,de->spd", grad_branch, out_back, preferred_element_type=jnp.float32)
        .astype(jnp.bfloat16)
        .reshape(split_shape)
    )
    delta = jnp.transpose(jnp.sum(grad_attn.astype(jnp.float32) * attn, axis=-1), (0, 2, 1))
    grad_query, key_terms, value_terms = backward_reduce(
        query_low, key_all, value_all, grad_attn, log_totals, delta, score_scale, block_len
    )
    grad_key, grad_value = (
        lax.psum_scatter(key_terms, "ctx", scatter_dimension=1, tiled=True),
        lax.psum_scatter(value_terms, "ctx", scatter_dimension=1, tiled=True),
    )
    grad_qkv = jnp.concatenate(
        [
            grad_query.reshape(flat_shape),
            grad_key.reshape(flat_shape),
            grad_value.reshape(flat_shape),
        ],
        axis=-1,
    ).astype(jnp.bfloat16)
    grad_w_qkv = jnp.einsum("spd,spe->de", attn_in, grad_qkv, preferred_element_type=jnp.float32)
    grad_b_query = token_sum(grad_qkv[..., :model_width])
    grad_b_value = token_sum(grad_qkv[..., 2 * model_width :])
    grad_norm = jnp.einsum("spe,de->spd", grad_qkv, qkv_back, preferred_element_type=jnp.float32)
    unused, norm_one_pull = jax.vjp(
        layer_norm, hidden, gain_one_back.astype(jnp.float32), bias_one.astype(jnp.float32)
    )
    grad_hidden_part, grad_ln1_gain, grad_ln1_bias = norm_one_pull(grad_norm)
    grad_hidden = grad_hidden_two + grad_hidden_part
    grad_tokens = grad_hidden.astype(jnp.bfloat16)
    grad_embed = jnp.sum(grad_hidden, axis=1)
    grad_w_time = jnp.einsum(
        "sd,se->de", sinus_low.astype(jnp.float32), grad_embed, precision=lax.Precision.HIGHEST
    )
    grad_b_time = jnp.sum(grad_embed, axis=0)
    shares = (
        lax.psum_scatter(
            grad_w_time.astype(jnp.bfloat16), "seq", scatter_dimension=0, tiled=True
        ).astype(jnp.float32),
        lax.psum_scatter(
            grad_b_time.astype(jnp.bfloat16), "seq", scatter_dimension=0, tiled=True
        ).astype(jnp.float32),
        lax.psum_scatter(
            grad_ln1_gain.astype(jnp.bfloat16), "seq", scatter_dimension=0, tiled=True
        ).astype(jnp.float32),
        lax.psum_scatter(
            grad_ln1_bias.astype(jnp.bfloat16), "seq", scatter_dimension=0, tiled=True
        ).astype(jnp.float32),
        lax.psum_scatter(
            grad_w_qkv.astype(jnp.bfloat16), "seq", scatter_dimension=0, tiled=True
        ).astype(jnp.float32),
        lax.psum_scatter(
            grad_b_query.astype(jnp.bfloat16), "seq", scatter_dimension=0, tiled=True
        ).astype(jnp.float32),
        lax.psum_scatter(
            grad_b_value.astype(jnp.bfloat16), "seq", scatter_dimension=0, tiled=True
        ).astype(jnp.float32),
        lax.psum_scatter(
            grad_w_out.astype(jnp.bfloat16), "seq", scatter_dimension=0, tiled=True
        ).astype(jnp.float32),
        lax.psum_scatter(
            grad_b_out.astype(jnp.bfloat16), "seq", scatter_dimension=0, tiled=True
        ).astype(jnp.float32),
        lax.psum_scatter(
            grad_ln2_gain.astype(jnp.bfloat16), "seq", scatter_dimension=0, tiled=True
        ).astype(jnp.float32),
        lax.psum_scatter(
            grad_ln2_bias.astype(jnp.bfloat16), "seq", scatter_dimension=0, tiled=True
        ).astype(jnp.float32),
        lax.psum_scatter(
            grad_w_up.astype(jnp.bfloat16), "seq", scatter_dimension=0, tiled=True
        ).astype(jnp.float32),
        lax.psum_scatter(
            grad_b_up.astype(jnp.bfloat16), "seq", scatter_dimension=0, tiled=True
        ).astype(jnp.float32),
        lax.psum_scatter(
            grad_w_down.astype(jnp.bfloat16), "seq", scatter_dimension=0, tiled=True
        ).astype(jnp.float32),
        lax.psum_scatter(
            grad_b_down.astype(jnp.bfloat16), "seq", scatter_dimension=0, tiled=True
        ).astype(jnp.float32),
    )
    (
        total_w_time,
        total_b_time,
        total_ln1_gain,
        total_ln1_bias,
        total_w_qkv,
        total_b_query,
        total_b_value,
        total_w_out,
        total_b_out,
        total_ln2_gain,
        total_ln2_bias,
        total_w_up,
        total_b_up,
        total_w_down,
        total_b_down,
    ) = lax.psum(
        (
            shares[0],
            shares[1],
            shares[2],
            shares[3],
            shares[4],
            shares[5],
            shares[6],
            shares[7],
            shares[8],
            shares[9],
            shares[10],
            shares[11],
            shares[12],
            shares[13],
            shares[14],
        ),
        "ctx",
    )
    return (
        output,
        grad_tokens,
        total_w_time,
        total_b_time,
        total_ln1_gain,
        total_ln1_bias,
        total_w_qkv,
        total_b_query,
        total_b_value,
        total_w_out,
        total_b_out,
        total_ln2_gain,
        total_ln2_bias,
        total_w_up,
        total_b_up,
        total_w_down,
        total_b_down,
    )


F32 = jnp.float32
BF16 = jnp.bfloat16
VMEM_BYTES = 56 * 1024 * 1024
RATE = 1.15e9


def swap(value, axis):
    return lax.ppermute(value, axis, [(0, 1), (1, 0)])


def across(value):
    return lax.ppermute(value, ("zl", "x"), [(i, i ^ 3) for i in range(4)])


def pick(value, index):
    return lax.dynamic_index_in_dim(value, index, 0, keepdims=False)


def dot(left, right, left_dim=1, right_dim=0):
    return lax.dot_general(
        left, right, (((left_dim,), (right_dim,)), ((), ())), preferred_element_type=F32
    )


class Values:
    pass


class Steps:
    def __init__(self, ids):
        self.ids = ids
        self.last = None

    def __call__(self, kernel, micros, inputs, outputs, scratch=(), behind=()):
        behind = [*behind] + ([self.last] if self.last is not None else [])
        shapes = [jax.ShapeDtypeStruct(shape, dtype) for shape, dtype in outputs]
        count = 1 + len(inputs)

        def run(*refs):
            kernel(*refs[:count], *refs[count + len(behind) :])

        results = pl.pallas_call(
            run,
            out_shape=shapes,
            in_specs=[pl.BlockSpec(memory_space=pltpu.SMEM)]
            + [pl.BlockSpec(memory_space=pltpu.VMEM)] * len(inputs)
            + [pl.BlockSpec(memory_space=pl.ANY)] * len(behind),
            out_specs=[pl.BlockSpec(memory_space=pltpu.VMEM)] * len(shapes),
            scratch_shapes=list(scratch),
            compiler_params=pltpu.CompilerParams(vmem_limit_bytes=VMEM_BYTES),
            cost_estimate=pl.CostEstimate(
                flops=int(micros * RATE), bytes_accessed=1, transcendentals=0
            ),
            name=kernel.__name__,
        )(self.ids, *inputs, *behind)
        self.last = results[0]
        return results


SEQ, MEMBER, HALF = 0, 1, 2


def normalize(hidden):
    center = hidden - jnp.mean(hidden, axis=-1, keepdims=True)
    rstd = lax.rsqrt(jnp.mean(center * center, axis=-1, keepdims=True) + norm_eps)
    return center * rstd, rstd


def norm_back(e, x, r):
    return r * (e - jnp.mean(e, -1, keepdims=True) - x * jnp.mean(e * x, -1, keepdims=True))


def token_kernel(ids, tokens, mine, far, blank):
    blank[...] = jnp.zeros(blank.shape, blank.dtype)
    mine[...] = tokens[ids[HALF]]
    far[...] = tokens[1 - ids[HALF]]


def pick_kernel(ids, grad_out, far):
    far[...] = grad_out[1 - ids[HALF]]


def column_kernel(ids, w_qkv, out):
    part = w_qkv.shape[1] // 12
    width = w_qkv.shape[1] // 3
    for member in range(4):

        @pl.when(ids[MEMBER] == member)
        def _():
            for t in range(3):
                at = t * width + member * part
                value = w_qkv[:, at : at + part]
                for block in range(4):
                    out[block, :, t * part : (t + 1) * part] = value


def up_kernel(ids, w_up, own, y, c, yc):
    ff = own.shape[1]
    for ref, flip in ((own, 0), (y, 2), (c, 1), (yc, 3)):
        ref[...] = w_up[:, pl.ds(pl.multiple_of((ids[SEQ] ^ flip) * ff, ff), ff)]


def own_kernel(ids, grad_out, far, w_out, own, copy):
    copy[...] = w_out[...]
    half = far.shape[0]
    own[:half] = grad_out[ids[HALF]]
    own[half:] = far[...]


def second_kernel(ids, keep, recv, out):
    out[...] = (keep[...].astype(F32) + recv[1].astype(F32)).astype(BF16)


def both_kernel(ids, left, right, out):
    out[...] = (left[...].astype(F32) + right[...].astype(F32)).astype(BF16)


def chain_kernel(ids, keep, c, first, second):
    first[...] = (keep[0].astype(F32) + c[0].astype(F32)).astype(BF16)
    second[...] = (keep[1].astype(F32) + c[1].astype(F32)).astype(BF16)


def join_kernel(ids, first, y, a, b, c, d, out):
    rows = first.shape[0]
    out[:rows] = (first[...].astype(F32) + y[...].astype(F32)).astype(BF16)
    total = a[...].astype(F32) + b[...].astype(F32) + c[...].astype(F32) + d[...].astype(F32)
    out[rows:] = total.astype(BF16)


def pieces_kernel(ids, a, b, c, d, down, up):
    total = a[...].astype(F32) + b[...].astype(F32) + c[...].astype(F32) + d[...].astype(F32)
    low = total.astype(BF16)
    rows = down.shape[0]
    fine = up.shape[1]
    down[...] = low[:rows]
    for s in range(4):
        up[s] = low[rows + s * fine : rows + (s + 1) * fine]


def attend_kernel(
    ids, tok_own, tok_x, tok_z, tok_d, far_own, far_x, far_z, far_d, sinus, w_time, vec, small, wq,
    attn_in, qkv_t, o_full, o_send, lse, w_t, te,
):
    piece, width = tok_own.shape
    part = width // 4
    rows = wq.shape[1]
    own = 2 * piece
    gi = ids[MEMBER]
    for block in range(4):
        w_t[:, block * rows : (block + 1) * rows] = wq[block].T
    te[...] = dot(sinus[...], w_time[...]) + vec[0:1, :]
    te_row = te[0:1, :]
    gain, offset = vec[1:2, :], vec[2:3, :]
    bias = small[gi].astype(F32).T
    pairs = ((tok_own, far_own), (tok_x, far_x), (tok_z, far_z), (tok_d, far_d))
    for block, (tok, far) in enumerate(pairs):
        normed, _ = normalize(jnp.concatenate([tok[...], far[...]]).astype(F32) + te_row)
        low = (normed * gain + offset).astype(BF16)
        attn_in[block] = low
        qkv = dot(w_t[...], low, 1, 1)
        qkv_t[block, 0:part, :] = (qkv[:part] + bias[:, 3:4]).astype(BF16)
        qkv_t[block, part : 2 * part, :] = qkv[part : 2 * part].astype(BF16)
        qkv_t[block, 2 * part :, :] = (qkv[2 * part :] + bias[:, 4:5]).astype(BF16)

    @pl.loop(0, part // HEAD_DIM)
    def _(head):
        at = pl.multiple_of(head * HEAD_DIM, HEAD_DIM)
        k_t = jnp.concatenate([qkv_t[j, pl.ds(part + at, HEAD_DIM), :] for j in range(4)], 1)
        v_t = jnp.concatenate([qkv_t[j, pl.ds(2 * part + at, HEAD_DIM), :] for j in range(4)], 1)
        for block in range(4):
            q_t = qkv_t[block, pl.ds(at, HEAD_DIM), :] * jnp.asarray(0.125, BF16)
            scores = dot(k_t, q_t, 0, 0)
            top = jnp.max(scores, 0, keepdims=True)
            weights = jnp.exp(scores - top)
            total = jnp.sum(weights, 0, keepdims=True)
            attn = dot(v_t, weights.astype(BF16)) / total
            o_full[block, pl.ds(at, HEAD_DIM), :] = attn
            o_send[gi ^ block, pl.ds(at, HEAD_DIM), :] = attn.astype(BF16)
            lse[head * 4 + block] = jnp.broadcast_to(top + jnp.log(total), (8, own))


def fold(value):
    third = value.shape[0] // 3
    return jnp.concatenate([value[i * third : (i + 1) * third] for i in range(3)], 1)


def unfold(value):
    wide = value.shape[1] // 3
    return jnp.concatenate([value[:, i * wide : (i + 1) * wide] for i in range(3)], 0)


def branch_kernel(
    ids, attn, w_out, tok_own, far_own, te, vec, mlp_in, hidden_two, folds
):
    rows = attn.shape[1]
    te_row = te[0:1, :]
    hidden = jnp.concatenate([tok_own[...], far_own[...]]).astype(F32) + te_row + vec[5:6, :]
    for block in range(4):
        hidden = hidden + dot(attn[block], w_out[block * rows : (block + 1) * rows, :], 0, 0)
    hidden_two[...] = hidden
    normed, _ = normalize(hidden)
    mlp_in[...] = (normed * vec[6:7, :] + vec[7:8, :]).astype(BF16)
    for block in range(4):
        folds[block] = fold(attn[ids[SEQ] ^ block])


def feed_kernel(
    ids, m_own, m_y, m_c, m_yc, go_all, u_own, u_y, u_c, u_yc, w_down, b_up, folds,
    gm_own, gm_pair, gm_send, out_own, out_pair, out_send, act_all, gp_all, w_up,
):
    si = ids[SEQ]
    rows = u_own.shape[0]
    own = m_own.shape[0]
    for ref, flip in ((u_own, 0), (u_y, 2), (u_c, 1), (u_yc, 3)):
        w_up[pl.ds(pl.multiple_of((si ^ flip) * rows, rows), rows), :] = ref[...]
    fine = folds.shape[1]
    out_send[2 * own : 2 * own + fine, :] = folds[1]
    out_send[2 * own + fine :, :] = folds[3]
    for block, (ref, flip) in enumerate(((m_own, 0), (m_y, 2), (m_c, 1), (m_yc, 3))):
        grad_out = go_all[si ^ flip]
        pre = dot(ref[...], w_up[...]) + b_up[...]
        cdf = 0.5 * (1.0 + lax.erf(pre * (0.5**0.5)))
        act = (pre * cdf).astype(BF16)
        grad_act = dot(grad_out, w_down[...], 1, 1)
        slope = cdf + pre * (jnp.exp(-0.5 * pre * pre) * (0.5 / math.pi) ** 0.5)
        grad_pre = (grad_act * slope).astype(BF16)
        act_all[block] = act
        gp_all[block] = grad_pre
        gm = dot(grad_pre, w_up[...], 1, 1)
        out = dot(act, w_down[...])
        if block < 2:
            (gm_own, gm_pair)[block][...] = gm.astype(gm_pair.dtype if block else F32)
            (out_own, out_pair)[block][...] = out.astype(out_pair.dtype if block else F32)
        else:
            gm_send[block - 2] = gm.astype(BF16)
            out_send[(block - 2) * own : (block - 1) * own, :] = out.astype(BF16)


def feed_grad_kernel(
    ids, m_own, m_y, m_c, m_yc, go_all, act_all, gp_all, p_own, p_x, p_z, p_d, grad
):
    si, gi = ids[SEQ], ids[MEMBER]
    width = m_own.shape[1]
    ff = act_all.shape[2]
    part = ff // 4
    rows = width // 4
    fine = rows // 4
    pieces = ((p_own, 0), (p_x, 1), (p_z, 2), (p_d, 3))
    orders = ((m_own, 0), (m_y, 2), (m_c, 1), (m_yc, 3))
    for s in range(4):
        cols = slice(s * part, (s + 1) * part)
        total = jnp.zeros((part, width), F32)
        for block, (_, flip) in enumerate(orders):
            total = total + dot(act_all[block, :, cols], go_all[si ^ flip], 0, 0)
        grad[cols, :] = total.astype(BF16)
    for ref, flip in pieces:
        ref[:part, :] = grad[pl.ds(pl.multiple_of((gi ^ flip) * part, 16), part), :]
    for s in range(4):
        cols = slice(s * rows, (s + 1) * rows)
        total = jnp.zeros((rows, ff), F32)
        for block, (ref, _) in enumerate(orders):
            total = total + dot(ref[:, cols], gp_all[block], 0, 0)
        grad[cols, :] = total.astype(BF16)
    for ref, flip in pieces:
        for s in range(4):
            at = part + 16 + s * fine
            ref[at : at + fine, :] = grad[pl.ds(pl.multiple_of(s * rows + (gi ^ flip) * fine, 16), fine), :]
    b_up = jnp.zeros((1, ff), F32)
    b_down = jnp.zeros((1, width), F32)
    for block in range(4):
        b_up = b_up + jnp.sum(gp_all[block].astype(F32), 0, keepdims=True)
        b_down = b_down + jnp.sum(go_all[block].astype(F32), 0, keepdims=True)
    line = lax.broadcasted_iota(jnp.int32, (16, width), 0)
    extra = jnp.where(line == 0, b_up, jnp.where(line == 1, b_down, 0.0))
    for ref, flip in pieces:
        ref[part : part + 16, :] = jnp.where(gi == flip, extra, 0.0).astype(BF16)


def back_kernel(
    ids, gm_keep, gm_c, gm_y, hidden_two, go_own, w_out, vec, out_far, out_c, folds,
    grad_two, branch, ga_send, sums, out_pair,
):
    rows = w_out.shape[0] // 4
    grad_mlp = gm_keep[...] + gm_c[0].astype(F32) + gm_y[...].astype(F32)
    normed, rstd = normalize(hidden_two[...])
    grad = go_own[...].astype(F32) + norm_back(grad_mlp * vec[6:7, :], normed, rstd)
    grad_two[...] = grad
    low = grad.astype(BF16)
    branch[...] = low
    for block in range(4):
        ga_send[block] = dot(w_out[block * rows : (block + 1) * rows, :], low, 1, 1).astype(BF16)
    sums[0:1, :] = jnp.sum(grad_mlp * normed, 0, keepdims=True)
    sums[1:2, :] = jnp.sum(grad_mlp, 0, keepdims=True)
    sums[2:3, :] = jnp.sum(low.astype(F32), 0, keepdims=True)
    sums[3:4, :] = jnp.sum(grad, 0, keepdims=True)
    sums[4:8, :] = jnp.zeros((4, sums.shape[1]), F32)
    own = out_far.shape[0]
    fine = folds.shape[1]
    out_pair[:own, :] = (out_far[...].astype(F32) + out_c[own : 2 * own, :].astype(F32)).astype(BF16)
    out_pair[own : own + fine, :] = folds[2]
    out_pair[own + fine :, :] = out_c[2 * own + fine :, :]


def attend_back_kernel(
    ids, qkv_t, lse, o_full, ga, w_t, tok_own, tok_x, tok_z, tok_d, far_own, far_x, far_z, far_d, te, vec,
    dqkv_t, gh_send, sums, dk, dv,
):
    part = o_full.shape[1]
    own = 2 * tok_own.shape[0]
    si, gi = ids[SEQ], ids[MEMBER]

    @pl.loop(0, part // HEAD_DIM)
    def _(head):
        at = pl.multiple_of(head * HEAD_DIM, HEAD_DIM)
        k_t = jnp.concatenate([qkv_t[j, pl.ds(part + at, HEAD_DIM), :] for j in range(4)], 1)
        v_t = jnp.concatenate([qkv_t[j, pl.ds(2 * part + at, HEAD_DIM), :] for j in range(4)], 1)
        for block in range(4):
            q_t = qkv_t[block, pl.ds(at, HEAD_DIM), :] * jnp.asarray(0.125, BF16)
            do_t = ga[gi ^ block, pl.ds(at, HEAD_DIM), :]
            delta = jnp.sum(do_t.astype(F32) * o_full[block, pl.ds(at, HEAD_DIM), :], 0, keepdims=True)
            weights = jnp.exp(dot(k_t, q_t, 0, 0) - lse[head * 4 + block, 0:1, :])
            grad_probs = dot(v_t, do_t, 0, 0)
            grad_scores = (weights * (grad_probs - delta)).astype(BF16)
            value_part = dot(do_t, weights.astype(BF16), 1, 1)
            key_part = dot(q_t, grad_scores, 1, 1)
            dqkv_t[block, pl.ds(at, HEAD_DIM), :] = (dot(k_t, grad_scores) * 0.125).astype(BF16)
            if block == 0:
                dv[...] = value_part
                dk[...] = key_part
            else:
                dv[...] += value_part
                dk[...] += key_part
        for block in range(4):
            lanes = slice(block * own, (block + 1) * own)
            dqkv_t[block, pl.ds(part + at, HEAD_DIM), :] = dk[:, lanes].astype(BF16)
            dqkv_t[block, pl.ds(2 * part + at, HEAD_DIM), :] = dv[:, lanes].astype(BF16)

    te_row = te[0:1, :]
    gain = vec[1:2, :]
    sum_gain = jnp.zeros_like(gain)
    sum_bias = jnp.zeros_like(gain)
    sum_hidden = jnp.zeros_like(gain)
    pairs = ((tok_own, far_own), (tok_x, far_x), (tok_z, far_z), (tok_d, far_d))
    for block, (tok, far) in enumerate(pairs):
        normed, rstd = normalize(jnp.concatenate([tok[...], far[...]]).astype(F32) + te_row)
        grad_norm = dot(dqkv_t[block], w_t[...], 0, 0)
        grad = norm_back(grad_norm * gain, normed, rstd)
        gh_send[gi ^ block] = grad.astype(BF16)
        sum_gain = sum_gain + jnp.sum(grad_norm * normed, 0, keepdims=True)
        sum_bias = sum_bias + jnp.sum(grad_norm, 0, keepdims=True)
        sum_hidden = sum_hidden + jnp.sum(grad, 0, keepdims=True)
    sums[0:1, :] = sum_gain
    sums[1:2, :] = sum_bias
    sums[2:3, :] = sum_hidden
    sums[3:8, :] = jnp.zeros((5, sums.shape[1]), F32)


def qkv_grad_kernel(ids, attn_in, dqkv_t, sums_two, sums_one, keep, give):
    si, gi = ids[SEQ], ids[MEMBER]
    cols = dqkv_t.shape[1]
    part = cols // 3
    rows = part
    width = attn_in.shape[2]
    half = width // 2
    grad = jnp.zeros((cols, width), F32)
    tok_sum = jnp.zeros((16, cols), F32)
    for block in range(4):
        grad = grad + dot(dqkv_t[block], attn_in[block])
        tok_sum = tok_sum + dot(jnp.ones((16, dqkv_t.shape[2]), BF16), dqkv_t[block], 1, 1)
    grad = grad.astype(BF16)
    line = lax.broadcasted_iota(jnp.int32, (32, cols), 0)
    embed = sums_one[2:3, :] + sums_two[3:4, :]
    slot = 8 + 2 * (2 * si + ids[HALF])
    lanes = lax.broadcasted_iota(jnp.int32, (1, cols), 1)
    wide = [jnp.concatenate([e, jnp.zeros((1, cols - half), F32)], 1) for e in (embed[:, :half], embed[:, half:])]
    common = jnp.where(line == slot, wide[0], jnp.where(line == slot + 1, wide[1], 0.0))
    for s in range(4):
        here = slice(s * rows, (s + 1) * rows)
        extra = common
        vectors = (
            sums_two[0:1, here], sums_two[1:2, here], sums_two[2:3, here], sums_one[0:1, here], sums_one[1:2, here],
        )
        for i, vector in enumerate(vectors):
            full = jnp.concatenate([vector, jnp.zeros((1, cols - rows), F32)], 1)
            extra = jnp.where(line == i, full, extra)
        extra = jnp.where((line == 5) & (gi == s), tok_sum[0:1, :], extra)
        block = grad[:, here].T
        flip = si ^ s

        @pl.when(flip % 2 == 0)
        def _():
            keep[flip // 2, :rows, :] = block
            keep[flip // 2, rows:, :] = extra.astype(BF16)

        @pl.when(flip % 2 == 1)
        def _():
            give[flip // 2, :rows, :] = block
            give[flip // 2, rows:, :] = extra.astype(BF16)


def out_grad_kernel(ids, folds, out_c, out_y, branch_s, w_own, w_x, w_z, w_d, low):
    si, gi = ids[SEQ], ids[MEMBER]
    rows = low.shape[0]
    cols = w_own.shape[1]
    fine = rows // 4
    third = fine // 3
    own = branch_s.shape[1]
    third_rows = folds.shape[1]
    grad = dot(unfold(folds[0]), branch_s[si])
    grad = grad + dot(unfold(out_c[2 * own : 2 * own + third_rows, :]), branch_s[si ^ 1])
    grad = grad + dot(unfold(out_y[own : own + third_rows, :]), branch_s[si ^ 2])
    grad = grad + dot(unfold(out_y[own + third_rows :, :]), branch_s[si ^ 3])
    low[...] = grad.astype(BF16)
    for ref, flip in ((w_own, 0), (w_x, 1), (w_z, 2), (w_d, 3)):
        lines = low[pl.ds(pl.multiple_of((gi ^ flip) * fine, 16), fine), :]
        ref[:fine, :] = lines[:, :cols]
        ref[fine:, :] = jnp.concatenate([lines[i * third : (i + 1) * third, cols:] for i in range(3)], 1)


def out_kernel(ids, hidden_two, out_keep, out_c, out_y, vec, mine, other):
    half = mine.shape[0]
    out = hidden_two[...] + vec[8:9, :] + out_keep[...] + out_c[: 2 * half].astype(F32) + out_y[: 2 * half].astype(F32)
    mine[...] = out[:half].astype(BF16)
    other[...] = out[half:].astype(BF16)


def hidden_grad_kernel(ids, grad_two, recv, mine, other):
    half = mine.shape[0]
    grad = grad_two[...]
    for member in range(4):
        grad = grad + recv[member].astype(F32)
    mine[...] = grad[:half].astype(BF16)
    other[...] = grad[half:].astype(BF16)


def down_total_kernel(ids, own, x, z, d, w_down, b_up, b_down):
    gi = ids[MEMBER]
    quarter = w_down.shape[1]
    for ref, flip in ((own, 0), (x, 1), (z, 2), (d, 3)):
        w_down[gi ^ flip] = ref[:quarter, :].astype(F32)

        @pl.when(gi == flip)
        def _():
            b_up[...] = ref[quarter : quarter + 1, :].astype(F32)
            full = ref[quarter : quarter + 2, :].astype(F32)
            rows = b_down.shape[1]
            for s in range(4):

                @pl.when(ids[SEQ] == s)
                def _():
                    b_down[...] = full[1:2, s * rows : (s + 1) * rows]


def up_total_kernel(ids, own, x, z, d, w_up):
    gi = ids[MEMBER]
    ff = own.shape[2]
    for ref, flip in ((own, 0), (x, 1), (z, 2), (d, 3)):
        for s in range(4):
            w_up[gi ^ flip, :, s * ff : (s + 1) * ff] = ref[s].astype(F32)


def total_kernel(ids, g_own, g_x, g_z, g_d, sinus, w_qkv, w_out, w_time, vectors, b_time, totals, embeds):
    si, gi = ids[SEQ], ids[MEMBER]
    rows = w_qkv.shape[0]
    cols = g_own.shape[1]
    width = w_qkv.shape[1] // 3
    part = cols // 3
    fine = rows // 4
    third = fine // 3
    for member in range(4):
        for ref, flip in ((g_own, 0), (g_x, 1), (g_z, 2), (g_d, 3)):

            @pl.when(gi ^ flip == member)
            def _():
                for t in range(3):
                    at = t * width + member * part
                    w_qkv[:, at : at + part] = ref[:rows, t * part : (t + 1) * part].astype(F32)
                lines = ref[rows + 32 :, :].astype(F32)
                w_out[member, :, :cols] = lines[:fine]
                for i in range(3):
                    w_out[member, i * third : (i + 1) * third, cols:] = lines[fine:, i * part : (i + 1) * part]

    small = jnp.zeros((32, cols), F32)
    for ref in (g_own, g_x, g_z, g_d):
        small = small + ref[rows : rows + 32, :].astype(F32)
    vectors[...] = small[:8]
    half = width // 2
    totals[...] = small
    for b in range(8):
        embeds[b : b + 1, :half] = totals[8 + 2 * b : 9 + 2 * b, :half]
        embeds[b : b + 1, half:] = totals[9 + 2 * b : 10 + 2 * b, :half]
    full = jnp.sum(embeds[...], 0, keepdims=True)
    for s in range(4):

        @pl.when(si == s)
        def _():
            b_time[...] = full[:, s * rows : (s + 1) * rows]

    w_time[...] = lax.dot_general(
        sinus[...], embeds[...], (((0,), (0,)), ((), ())), precision=lax.Precision.HIGHEST,
        preferred_element_type=F32,
    )


def pair_kernel(ids, grad_mine, out_mine, grad_other, out_other, grad_tokens, output):
    grad_tokens[ids[HALF]] = grad_mine[...]
    grad_tokens[1 - ids[HALF]] = grad_other[...]
    output[ids[HALF]] = out_mine[...]
    output[1 - ids[HALF]] = out_other[...]


def group_body(
    tokens, grad_out, timestep, w_time, b_time, ln1_gain, ln1_bias, w_qkv, b_query, b_value,
    w_out, b_out, ln2_gain, ln2_bias, w_up, b_up, w_down, b_down,
):
    seqs, piece, width = tokens.shape
    rows = w_qkv.shape[0]
    ff = w_down.shape[0]
    own = 2 * piece
    part = width // 4
    heads = part // HEAD_DIM
    yi, ci = lax.axis_index("y"), lax.axis_index("c")
    hi, zi, xi = lax.axis_index("h"), lax.axis_index("zl"), lax.axis_index("x")
    si = 2 * yi + ci
    gi = 2 * zi + xi
    step = Steps(jnp.stack([si, gi, hi]).astype(jnp.int32))

    def members(value):
        return lax.all_to_all(value, ("zl", "x"), split_axis=0, concat_axis=0, tiled=True)

    def shards(value):
        return lax.all_to_all(value, ("y", "c"), split_axis=0, concat_axis=0, tiled=True)

    def gather4(value):
        return [value, swap(value, "x"), swap(value, "zl"), across(value)]

    def trade4(keep, x, z, d):
        return [keep, swap(x, "x"), swap(z, "zl"), across(d)]

    def across_seq(value):
        return lax.ppermute(value, ("y", "c"), [(i, i ^ 3) for i in range(4)])

    half = width // 2
    hidden_low = ((own, width), BF16)
    hidden_full = ((own, width), F32)
    down = ((ff // 4 + 16, width), BF16)
    up = ((4, rows // 4, ff), BF16)
    packed = ((ff // 4 + 16 + rows, width), BF16)
    chain = (2, rows + 32, 3 * part)
    joined = ((rows + 32 + rows // 3, 3 * part), BF16)
    v = Values()

    def sinusoid_at(steps, place):
        freq = jnp.exp(-math.log(10000.0) * (place % half).astype(F32) / half)
        angles = steps[:, None] * freq[None, :]
        return jnp.where(place < half, jnp.sin(angles), jnp.cos(angles)).astype(BF16)

    w_time_f = lax.all_gather(w_time, ("y", "c"), axis=0, tiled=True)
    here = jnp.broadcast_to(pick(timestep, hi).astype(F32), (8,))
    sinus_here = sinusoid_at(here, jnp.arange(width))

    def token():
        tok_own, tok_far, blank = step(token_kernel, 2, [tokens], [((piece, width), BF16)] * 2 + [((1, rows), BF16)])
        v.blank = blank.reshape(rows)
        v.far_own = swap(tok_far, "h")
        v.toks = gather4(tok_own)
        v.fars = gather4(v.far_own)

    def small_parameters():
        low_bits = (timestep % 64).astype(BF16)
        high_bits = (timestep // 64).astype(BF16)
        steps_row = jnp.concatenate([high_bits, low_bits, jnp.zeros((rows - 2 * seqs,), BF16)])
        small = jnp.stack(
            [b_time, ln1_gain, ln1_bias, b_query, b_value, b_out, ln2_gain, ln2_bias, b_down, steps_row] + [v.blank] * 6
        )
        v.small = lax.all_gather(small, ("y", "c"))
        v.vec = jnp.transpose(v.small, (1, 0, 2)).reshape(16, width).astype(F32)

    def column():
        (blocks,) = step(column_kernel, 2, [w_qkv], [((4, rows, 3 * part), BF16)], behind=[v.small])
        v.wq = shards(blocks)

    def up_weights():
        pieces = step(up_kernel, 2, [w_up], [((rows, ff), BF16)] * 4)
        v.ups = [pieces[0], swap(pieces[1], "y"), swap(pieces[2], "c"), across_seq(pieces[3])]

    def pick_grad():
        (send,) = step(pick_kernel, 2, [grad_out], [((piece, width), BF16)])
        v.go_far = swap(send, "h")

    def attend():
        v.attn_in, v.qkv_t, v.o_full, send, v.lse, v.w_t, v.te = step(attend_kernel, 15, [*v.toks, *v.fars, sinus_here, w_time_f, v.vec, v.small, v.wq],
            [((4, own, width), BF16), ((4, 3 * part, own), BF16), ((4, part, own), F32), ((4, part, own), BF16),
             ((4 * heads, 8, own), F32), ((3 * part, width), BF16), ((8, width), F32)], behind=[v.ups[1], v.ups[2]])
        v.attn = members(send)

    def own_grad():
        v.go_own, copy = step(own_kernel, 2, [grad_out, v.go_far, w_out], [hidden_low, ((rows, width), BF16)])
        v.w_out = lax.all_gather(copy, ("y", "c"), axis=0, tiled=True)
        v.go_all = lax.all_gather(v.go_own, ("y", "c"))

    def branch():
        mlp, v.hidden_two, v.folds = step(branch_kernel, 30, [v.attn, v.w_out, v.toks[0], v.far_own, v.te, v.vec],
            [hidden_low, hidden_full, ((4, part // 3, width), BF16)], behind=[v.ups[3]])
        y = swap(mlp, "y")
        v.mlps = [mlp, y, swap(mlp, "c"), swap(y, "c")]

    def feed():
        v.gm_own, v.gm_far, gm_send, v.out_own, v.out_far, out_send, v.act, v.gp = step(feed_kernel, 10,
            [*v.mlps, v.go_all, *v.ups, w_down, b_up.astype(F32).reshape(1, ff), v.folds],
            [hidden_full, hidden_low, ((2, own, width), BF16), hidden_full, hidden_low,
             ((2 * own + 2 * part // 3, width), BF16), *[((4, own, ff), BF16)] * 2],
            [pltpu.VMEM((width, ff), BF16)],
        )
        v.gm_c = swap(gm_send, "c")
        v.out_c = swap(out_send, "c")

    def gm_add():
        (pair,) = step(second_kernel, 2, [v.gm_far, v.gm_c], [hidden_low])
        v.gm_y = swap(pair, "y")

    def feed_grad():
        v.ps = trade4(*step(feed_grad_kernel, 7, [*v.mlps, v.go_all, v.act, v.gp], [packed] * 4,
            [pltpu.VMEM((width, width), BF16)],
        ))

    def back():
        v.grad_two, branch_low, send, v.sums_two, pair = step(back_kernel, 5,
            [v.gm_own, v.gm_c, v.gm_y, v.hidden_two, v.go_own, v.w_out, v.vec, v.out_far, v.out_c,
             v.folds],
            [hidden_full, hidden_low, ((4, part, own), BF16), ((8, width), F32), ((own + 2 * part // 3, width), BF16)],
        )
        v.ga = members(send)
        v.branch_s = lax.all_gather(branch_low, ("y", "c"))
        v.out_y = swap(pair, "y")

    def attend_back():
        v.dqkv, gh, v.sums_one = step(attend_back_kernel, 15,
            [v.qkv_t, v.lse, v.o_full, v.ga, v.w_t, *v.toks, *v.fars, v.te, v.vec],
            [((4, 3 * part, own), BF16), ((4, own, width), BF16), ((8, width), F32)],
            [pltpu.VMEM((HEAD_DIM, 4 * own), F32)] * 2,
        )
        v.gh = members(gh)

    def p_sum():
        v.d_low, v.u_low = step(pieces_kernel, 2, v.ps, [down, up])
        v.d_h = swap(v.d_low, "h")
        v.u_h = swap(v.u_low, "h")

    def qkv_grad():
        v.ch_keep, give = step(qkv_grad_kernel, 5, [v.attn_in, v.dqkv, v.sums_two, v.sums_one], [(chain, BF16)] * 2
        )
        v.ch_c = swap(give, "c")

    def out_grad():
        pieces = step(out_grad_kernel, 3, [v.folds, v.out_c, v.out_y, v.branch_s],
            [((rows // 3, 3 * part), BF16)] * 4, [pltpu.VMEM((rows, width), BF16)],
        )
        v.wos = trade4(*pieces)

    def chain_add():
        v.first, second = step(chain_kernel, 2, [v.ch_keep, v.ch_c], [(chain[1:], BF16)] * 2)
        v.ch_y = swap(second, "y")

    def join():
        (v.now,) = step(join_kernel, 2, [v.first, v.ch_y, *v.wos], [joined])
        v.ch_h = swap(v.now, "h")

    def out():
        v.out_mine, other = step(out_kernel, 2, [v.hidden_two, v.out_own, v.out_c, v.out_y, v.vec],
            [((piece, width), BF16)] * 2,
        )
        v.out_h = swap(other, "h")

    def hidden():
        v.gt_mine, other = step(hidden_grad_kernel, 3, [v.grad_two, v.gh], [((piece, width), BF16)] * 2)
        v.gt_h = swap(other, "h")

    def d_add():
        (value,) = step(both_kernel, 2, [v.d_low, v.d_h], [down])
        v.dg = gather4(value)

    def u_add():
        (value,) = step(both_kernel, 2, [v.u_low, v.u_h], [up])
        v.gu_s = shards(value)
        v.ug = gather4(v.gu_s)

    def now_add():
        (value,) = step(both_kernel, 2, [v.now, v.ch_h], [joined])
        v.qg = gather4(value)

    def pair():
        v.grad_tokens, v.output = step(pair_kernel, 2, [v.gt_mine, v.out_mine, v.gt_h, v.out_h], [((seqs, piece, width), BF16)] * 2
        )

    def total():
        steps = (v.small[:, 9, :seqs].astype(F32) * 64 + v.small[:, 9, seqs : 2 * seqs].astype(F32)).reshape(-1)
        sinus_rows = sinusoid_at(steps, si * rows + jnp.arange(rows)).astype(F32)
        v.w_qkv, v.t_out, v.w_time, v.tv, v.b_time = step(total_kernel, 3, [*v.qg, sinus_rows],
            [((rows, 3 * width), F32), ((4, rows // 4, width), F32), ((rows, width), F32), ((8, 3 * part), F32),
             ((1, rows), F32)],
            [pltpu.VMEM((32, 3 * part), F32), pltpu.VMEM((8, width), F32)],
        )

    def down_total():
        v.w_down, v.b_up, v.b_down = step(down_total_kernel, 3, v.dg, [((4, ff // 4, width), F32), ((1, ff), F32), ((1, rows), F32)]
        )

    def up_total():
        (v.w_up,) = step(up_total_kernel, 3, v.ug, [((4, rows // 4, 4 * ff), F32)])

    for run in (
        token, small_parameters, pick_grad, column, up_weights, own_grad, attend, branch, feed, gm_add, feed_grad,
        back, attend_back, out, p_sum, qkv_grad, chain_add, out_grad, join, d_add, hidden, u_add, now_add, down_total,
        total, pair, up_total,
    ):
        run()
    tv = v.tv
    return (
        v.output, v.grad_tokens, v.w_time, v.b_time.reshape(rows), tv[3, :rows], tv[4, :rows], v.w_qkv,
        tv[5, :part], tv[5, 2 * part :], v.t_out.reshape(rows, width), tv[2, :rows], tv[0, :rows], tv[1, :rows],
        v.w_up.reshape(rows, 4 * ff), v.b_up.reshape(ff), v.w_down.reshape(ff, width), v.b_down.reshape(rows),
    )


def solution(mesh):
    placed = (
        P("seq", "ctx", None),
        P("seq", "ctx", None),
        P("seq"),
        P("seq", None),
        P("seq"),
        P("seq"),
        P("seq"),
        P("seq", None),
        P("seq"),
        P("seq"),
        P("seq", None),
        P("seq"),
        P("seq"),
        P("seq"),
        P("seq", None),
        P("seq"),
        P("seq", None),
        P("seq"),
    )
    out_placed = (
        P("seq", "ctx", None),
        P("seq", "ctx", None),
        P("seq", None),
        P("seq"),
        P("seq"),
        P("seq"),
        P("seq", None),
        P("seq"),
        P("seq"),
        P("seq", None),
        P("seq"),
        P("seq"),
        P("seq"),
        P("seq", None),
        P("seq"),
        P("seq", None),
        P("seq"),
    )
    sizes = dict(mesh.shape)
    if sizes["seq"] == 4 and sizes["ctx"] == 8:
        fine = Mesh(mesh.devices.reshape((2,) * 5), ("y", "c", "h", "zl", "x"))
        split = {"seq": ("y", "c"), "ctx": ("h", "zl", "x"), None: None}

        def finer(spec):
            return P(*(split[axis] for axis in spec))

        return jax.shard_map(
            group_body,
            mesh=fine,
            in_specs=tuple(finer(spec) for spec in placed),
            out_specs=tuple(finer(spec) for spec in out_placed),
            check_vma=False,
        )
    return jax.shard_map(
        body,
        mesh=mesh,
        in_specs=placed,
        out_specs=out_placed,
        check_vma=False,
    )
```

```python
import math

import jax
import jax.numpy as jnp
from jax import lax
from jax.experimental import pallas as pl
from jax.experimental.pallas import tpu as pltpu
from jax.sharding import Mesh
from jax.sharding import PartitionSpec as P

HEADS = 12
HEAD_DIM = 64


norm_eps = 1e-05
block_keys = 1024


def layer_norm(hidden, norm_gain, offset):
    center = hidden - jnp.mean(hidden, axis=-1, keepdims=True)
    variance = jnp.mean(center * center, axis=-1, keepdims=True)
    return center * lax.rsqrt(variance + norm_eps) * norm_gain + offset


def gelu_exact(values):
    return jax.nn.gelu(values, approximate=False)


def sinusoid(timestep, model_width):
    half_width = model_width // 2
    frequency = jnp.exp(
        -math.log(10000.0) * jnp.arange(half_width).astype(jnp.float32) / half_width
    )
    angles = timestep.astype(jnp.float32)[:, None] * frequency[None, :]
    return jnp.concatenate([jnp.sin(angles), jnp.cos(angles)], axis=-1)


def scores_of(queries, keys_blk, score_scale):
    return score_scale * jnp.einsum(
        "sphe,skhe->shpk", queries, keys_blk, preferred_element_type=jnp.float32
    )


def token_sum(values):
    return jnp.sum(values.astype(jnp.float32), axis=(0, 1))


def softmax_totals(query_low, key_all, score_scale, block_len):
    seq_count, row_count, head_count, head_width = query_low.shape
    blocks = key_all.shape[1] // block_len

    def softmax_block_step(carry, block_index):
        top_now, running = carry
        keys_blk = lax.dynamic_slice_in_dim(key_all, block_index * block_len, block_len, 1)
        scores = scores_of(query_low, keys_blk, score_scale)
        top_new = jnp.maximum(top_now, jnp.max(scores, axis=-1))
        running = running * jnp.exp(top_now - top_new) + jnp.sum(
            jnp.exp(scores - top_new[..., None]), axis=-1
        )
        return ((top_new, running), None)

    initial = (
        jnp.full((seq_count, head_count, row_count), -jnp.inf, jnp.float32),
        jnp.zeros((seq_count, head_count, row_count), jnp.float32),
    )
    (top_now, running), unused = lax.scan(softmax_block_step, initial, jnp.arange(blocks))
    return top_now + jnp.log(running)


def attend(query_low, key_all, value_all, log_totals, score_scale, block_len):
    blocks = key_all.shape[1] // block_len

    def attend_block_step(running, block_index):
        offset = block_index * block_len
        keys_blk = lax.dynamic_slice_in_dim(key_all, offset, block_len, 1)
        values_blk = lax.dynamic_slice_in_dim(value_all, offset, block_len, 1)
        probs_low = jnp.exp(
            scores_of(query_low, keys_blk, score_scale) - log_totals[..., None]
        ).astype(jnp.bfloat16)
        running = running + jnp.einsum(
            "shpk,skhe->sphe", probs_low, values_blk, preferred_element_type=jnp.float32
        )
        return (running, None)

    result, unused = lax.scan(
        attend_block_step, jnp.zeros(query_low.shape, jnp.float32), jnp.arange(blocks)
    )
    return result


def backward_reduce(
    query_low, key_all, value_all, grad_attn, log_totals, delta, score_scale, block_len
):
    blocks = key_all.shape[1] // block_len

    def backward_block_step(carry, block_index):
        grad_query, grad_key, grad_value = carry
        offset = block_index * block_len
        keys_blk = lax.dynamic_slice_in_dim(key_all, offset, block_len, 1)
        values_blk = lax.dynamic_slice_in_dim(value_all, offset, block_len, 1)
        weights = jnp.exp(scores_of(query_low, keys_blk, score_scale) - log_totals[..., None])
        probs_low = weights.astype(jnp.bfloat16)
        value_part = jnp.einsum(
            "shpk,sphe->skhe", probs_low, grad_attn, preferred_element_type=jnp.float32
        )
        grad_probs = jnp.einsum(
            "sphe,skhe->shpk", grad_attn, values_blk, preferred_element_type=jnp.float32
        )
        grad_scores = (weights * (grad_probs - delta[..., None])).astype(jnp.bfloat16)
        grad_query = grad_query + score_scale * jnp.einsum(
            "shpk,skhe->sphe", grad_scores, keys_blk, preferred_element_type=jnp.float32
        )
        key_part = score_scale * jnp.einsum(
            "shpk,sphe->skhe", grad_scores, query_low, preferred_element_type=jnp.float32
        )
        grad_key = lax.dynamic_update_slice_in_dim(grad_key, key_part, offset, 1)
        grad_value = lax.dynamic_update_slice_in_dim(grad_value, value_part, offset, 1)
        return ((grad_query, grad_key, grad_value), None)

    initial = (
        jnp.zeros(query_low.shape, jnp.float32),
        jnp.zeros(key_all.shape, jnp.float32),
        jnp.zeros(value_all.shape, jnp.float32),
    )
    result, unused = lax.scan(backward_block_step, initial, jnp.arange(blocks))
    return result


def body(
    tokens,
    grad_out,
    timestep,
    w_time,
    b_time,
    ln1_gain,
    ln1_bias,
    w_qkv,
    b_query,
    b_value,
    w_out,
    b_out,
    ln2_gain,
    ln2_bias,
    w_up,
    b_up,
    w_down,
    b_down,
):
    (
        time_full,
        time_bias,
        gain_one,
        bias_one,
        qkv_full,
        query_bias,
        value_bias,
        out_full,
        out_bias,
        gain_two,
        bias_two,
        up_full,
        up_bias,
        down_full,
        down_bias,
    ) = (
        lax.all_gather(w_time, "seq", axis=0, tiled=True),
        lax.all_gather(b_time, "seq", axis=0, tiled=True),
        lax.all_gather(ln1_gain, "seq", axis=0, tiled=True),
        lax.all_gather(ln1_bias, "seq", axis=0, tiled=True),
        lax.all_gather(w_qkv, "seq", axis=0, tiled=True),
        lax.all_gather(b_query, "seq", axis=0, tiled=True),
        lax.all_gather(b_value, "seq", axis=0, tiled=True),
        lax.all_gather(w_out, "seq", axis=0, tiled=True),
        lax.all_gather(b_out, "seq", axis=0, tiled=True),
        lax.all_gather(ln2_gain, "seq", axis=0, tiled=True),
        lax.all_gather(ln2_bias, "seq", axis=0, tiled=True),
        lax.all_gather(w_up, "seq", axis=0, tiled=True),
        lax.all_gather(b_up, "seq", axis=0, tiled=True),
        lax.all_gather(w_down, "seq", axis=0, tiled=True),
        lax.all_gather(b_down, "seq", axis=0, tiled=True),
    )
    seq_count, piece_len, model_width = tokens.shape
    score_scale = 1.0 / math.sqrt(HEAD_DIM)
    split_shape = (seq_count, piece_len, HEADS, HEAD_DIM)
    flat_shape = (seq_count, piece_len, model_width)
    sinus_low = sinusoid(timestep, model_width).astype(jnp.bfloat16)
    time_embed = jnp.dot(
        sinus_low, time_full, preferred_element_type=jnp.float32
    ) + time_bias.astype(jnp.float32)
    hidden = tokens.astype(jnp.float32) + time_embed[:, None, :]
    attn_in = layer_norm(hidden, gain_one.astype(jnp.float32), bias_one.astype(jnp.float32)).astype(
        jnp.bfloat16
    )
    qkv_bias = jnp.concatenate([query_bias, jnp.zeros_like(query_bias), value_bias]).astype(
        jnp.float32
    )
    projected = (
        jnp.einsum("spd,de->spe", attn_in, qkv_full, preferred_element_type=jnp.float32) + qkv_bias
    )
    query_low = projected[..., :model_width].astype(jnp.bfloat16).reshape(split_shape)
    key_low = (
        projected[..., model_width : 2 * model_width].astype(jnp.bfloat16).reshape(split_shape)
    )
    value_low = projected[..., 2 * model_width :].astype(jnp.bfloat16).reshape(split_shape)
    key_all, value_all = (
        lax.all_gather(key_low, "ctx", axis=1, tiled=True),
        lax.all_gather(value_low, "ctx", axis=1, tiled=True),
    )
    block_len = min(key_all.shape[1], block_keys)
    log_totals = softmax_totals(query_low, key_all, score_scale, block_len)
    attn = attend(query_low, key_all, value_all, log_totals, score_scale, block_len)
    attn_low = attn.reshape(flat_shape).astype(jnp.bfloat16)
    hidden_two = (
        hidden
        + jnp.einsum("spd,de->spe", attn_low, out_full, preferred_element_type=jnp.float32)
        + out_bias.astype(jnp.float32)
    )
    mlp_in = layer_norm(
        hidden_two, gain_two.astype(jnp.float32), bias_two.astype(jnp.float32)
    ).astype(jnp.bfloat16)
    pre_act = jnp.einsum(
        "spd,df->spf", mlp_in, up_full, preferred_element_type=jnp.float32
    ) + up_bias.astype(jnp.float32)
    act_low = gelu_exact(pre_act).astype(jnp.bfloat16)
    output = (
        hidden_two
        + jnp.einsum("spf,fd->spd", act_low, down_full, preferred_element_type=jnp.float32)
        + down_bias.astype(jnp.float32)
    ).astype(jnp.bfloat16)
    qkv_back, out_back, up_back, down_back, gain_one_back, gain_two_back = (
        lax.all_gather(w_qkv, "seq", axis=0, tiled=True),
        lax.all_gather(w_out, "seq", axis=0, tiled=True),
        lax.all_gather(w_up, "seq", axis=0, tiled=True),
        lax.all_gather(w_down, "seq", axis=0, tiled=True),
        lax.all_gather(ln1_gain, "seq", axis=0, tiled=True),
        lax.all_gather(ln2_gain, "seq", axis=0, tiled=True),
    )
    grad_w_down = jnp.einsum("spf,spd->fd", act_low, grad_out, preferred_element_type=jnp.float32)
    grad_b_down = token_sum(grad_out)
    grad_act = jnp.einsum("spd,fd->spf", grad_out, down_back, preferred_element_type=jnp.float32)
    unused, gelu_pull = jax.vjp(gelu_exact, pre_act)
    grad_pre = gelu_pull(grad_act)[0].astype(jnp.bfloat16)
    grad_w_up = jnp.einsum("spd,spf->df", mlp_in, grad_pre, preferred_element_type=jnp.float32)
    grad_b_up = token_sum(grad_pre)
    grad_mlp = jnp.einsum("spf,df->spd", grad_pre, up_back, preferred_element_type=jnp.float32)
    unused, norm_two_pull = jax.vjp(
        layer_norm, hidden_two, gain_two_back.astype(jnp.float32), bias_two.astype(jnp.float32)
    )
    grad_hidden_two, grad_ln2_gain, grad_ln2_bias = norm_two_pull(grad_mlp)
    grad_hidden_two = grad_hidden_two + grad_out.astype(jnp.float32)
    grad_branch = grad_hidden_two.astype(jnp.bfloat16)
    grad_w_out = jnp.einsum(
        "spd,spe->de", attn_low, grad_branch, preferred_element_type=jnp.float32
    )
    grad_b_out = token_sum(grad_branch)
    grad_attn = (
        jnp.einsum("spe,de->spd", grad_branch, out_back, preferred_element_type=jnp.float32)
        .astype(jnp.bfloat16)
        .reshape(split_shape)
    )
    delta = jnp.transpose(jnp.sum(grad_attn.astype(jnp.float32) * attn, axis=-1), (0, 2, 1))
    grad_query, key_terms, value_terms = backward_reduce(
        query_low, key_all, value_all, grad_attn, log_totals, delta, score_scale, block_len
    )
    grad_key, grad_value = (
        lax.psum_scatter(key_terms, "ctx", scatter_dimension=1, tiled=True),
        lax.psum_scatter(value_terms, "ctx", scatter_dimension=1, tiled=True),
    )
    grad_qkv = jnp.concatenate(
        [
            grad_query.reshape(flat_shape),
            grad_key.reshape(flat_shape),
            grad_value.reshape(flat_shape),
        ],
        axis=-1,
    ).astype(jnp.bfloat16)
    grad_w_qkv = jnp.einsum("spd,spe->de", attn_in, grad_qkv, preferred_element_type=jnp.float32)
    grad_b_query = token_sum(grad_qkv[..., :model_width])
    grad_b_value = token_sum(grad_qkv[..., 2 * model_width :])
    grad_norm = jnp.einsum("spe,de->spd", grad_qkv, qkv_back, preferred_element_type=jnp.float32)
    unused, norm_one_pull = jax.vjp(
        layer_norm, hidden, gain_one_back.astype(jnp.float32), bias_one.astype(jnp.float32)
    )
    grad_hidden_part, grad_ln1_gain, grad_ln1_bias = norm_one_pull(grad_norm)
    grad_hidden = grad_hidden_two + grad_hidden_part
    grad_tokens = grad_hidden.astype(jnp.bfloat16)
    grad_embed = jnp.sum(grad_hidden, axis=1)
    grad_w_time = jnp.einsum(
        "sd,se->de", sinus_low.astype(jnp.float32), grad_embed, precision=lax.Precision.HIGHEST
    )
    grad_b_time = jnp.sum(grad_embed, axis=0)
    shares = (
        lax.psum_scatter(
            grad_w_time.astype(jnp.bfloat16), "seq", scatter_dimension=0, tiled=True
        ).astype(jnp.float32),
        lax.psum_scatter(
            grad_b_time.astype(jnp.bfloat16), "seq", scatter_dimension=0, tiled=True
        ).astype(jnp.float32),
        lax.psum_scatter(
            grad_ln1_gain.astype(jnp.bfloat16), "seq", scatter_dimension=0, tiled=True
        ).astype(jnp.float32),
        lax.psum_scatter(
            grad_ln1_bias.astype(jnp.bfloat16), "seq", scatter_dimension=0, tiled=True
        ).astype(jnp.float32),
        lax.psum_scatter(
            grad_w_qkv.astype(jnp.bfloat16), "seq", scatter_dimension=0, tiled=True
        ).astype(jnp.float32),
        lax.psum_scatter(
            grad_b_query.astype(jnp.bfloat16), "seq", scatter_dimension=0, tiled=True
        ).astype(jnp.float32),
        lax.psum_scatter(
            grad_b_value.astype(jnp.bfloat16), "seq", scatter_dimension=0, tiled=True
        ).astype(jnp.float32),
        lax.psum_scatter(
            grad_w_out.astype(jnp.bfloat16), "seq", scatter_dimension=0, tiled=True
        ).astype(jnp.float32),
        lax.psum_scatter(
            grad_b_out.astype(jnp.bfloat16), "seq", scatter_dimension=0, tiled=True
        ).astype(jnp.float32),
        lax.psum_scatter(
            grad_ln2_gain.astype(jnp.bfloat16), "seq", scatter_dimension=0, tiled=True
        ).astype(jnp.float32),
        lax.psum_scatter(
            grad_ln2_bias.astype(jnp.bfloat16), "seq", scatter_dimension=0, tiled=True
        ).astype(jnp.float32),
        lax.psum_scatter(
            grad_w_up.astype(jnp.bfloat16), "seq", scatter_dimension=0, tiled=True
        ).astype(jnp.float32),
        lax.psum_scatter(
            grad_b_up.astype(jnp.bfloat16), "seq", scatter_dimension=0, tiled=True
        ).astype(jnp.float32),
        lax.psum_scatter(
            grad_w_down.astype(jnp.bfloat16), "seq", scatter_dimension=0, tiled=True
        ).astype(jnp.float32),
        lax.psum_scatter(
            grad_b_down.astype(jnp.bfloat16), "seq", scatter_dimension=0, tiled=True
        ).astype(jnp.float32),
    )
    (
        total_w_time,
        total_b_time,
        total_ln1_gain,
        total_ln1_bias,
        total_w_qkv,
        total_b_query,
        total_b_value,
        total_w_out,
        total_b_out,
        total_ln2_gain,
        total_ln2_bias,
        total_w_up,
        total_b_up,
        total_w_down,
        total_b_down,
    ) = lax.psum(
        (
            shares[0],
            shares[1],
            shares[2],
            shares[3],
            shares[4],
            shares[5],
            shares[6],
            shares[7],
            shares[8],
            shares[9],
            shares[10],
            shares[11],
            shares[12],
            shares[13],
            shares[14],
        ),
        "ctx",
    )
    return (
        output,
        grad_tokens,
        total_w_time,
        total_b_time,
        total_ln1_gain,
        total_ln1_bias,
        total_w_qkv,
        total_b_query,
        total_b_value,
        total_w_out,
        total_b_out,
        total_ln2_gain,
        total_ln2_bias,
        total_w_up,
        total_b_up,
        total_w_down,
        total_b_down,
    )


F32 = jnp.float32
BF16 = jnp.bfloat16
VMEM_BYTES = 56 * 1024 * 1024
RATE = 1.15e9


def swap(value, axis):
    return lax.ppermute(value, axis, [(0, 1), (1, 0)])


def across(value):
    return lax.ppermute(value, ("zl", "x"), [(i, i ^ 3) for i in range(4)])


def pick(value, index):
    return lax.dynamic_index_in_dim(value, index, 0, keepdims=False)


def dot(left, right, left_dim=1, right_dim=0):
    return lax.dot_general(
        left, right, (((left_dim,), (right_dim,)), ((), ())), preferred_element_type=F32
    )


class Values:
    pass


class Steps:
    def __init__(self, ids):
        self.ids = ids
        self.last = None

    def __call__(self, kernel, micros, inputs, outputs, scratch=(), behind=()):
        behind = [*behind] + ([self.last] if self.last is not None else [])
        shapes = [jax.ShapeDtypeStruct(shape, dtype) for shape, dtype in outputs]
        count = 1 + len(inputs)

        def run(*refs):
            kernel(*refs[:count], *refs[count + len(behind) :])

        results = pl.pallas_call(
            run,
            out_shape=shapes,
            in_specs=[pl.BlockSpec(memory_space=pltpu.SMEM)]
            + [pl.BlockSpec(memory_space=pltpu.VMEM)] * len(inputs)
            + [pl.BlockSpec(memory_space=pl.ANY)] * len(behind),
            out_specs=[pl.BlockSpec(memory_space=pltpu.VMEM)] * len(shapes),
            scratch_shapes=list(scratch),
            compiler_params=pltpu.CompilerParams(vmem_limit_bytes=VMEM_BYTES),
            cost_estimate=pl.CostEstimate(
                flops=int(micros * RATE), bytes_accessed=1, transcendentals=0
            ),
            name=kernel.__name__,
        )(self.ids, *inputs, *behind)
        self.last = results[0]
        return results


SEQ, MEMBER, HALF = 0, 1, 2


def normalize(hidden):
    center = hidden - jnp.mean(hidden, axis=-1, keepdims=True)
    rstd = lax.rsqrt(jnp.mean(center * center, axis=-1, keepdims=True) + norm_eps)
    return center * rstd, rstd


def norm_back(e, x, r):
    return r * (e - jnp.mean(e, -1, keepdims=True) - x * jnp.mean(e * x, -1, keepdims=True))


def token_kernel(ids, tokens, mine, far, blank):
    blank[...] = jnp.zeros(blank.shape, blank.dtype)
    mine[...] = tokens[ids[HALF]]
    far[...] = tokens[1 - ids[HALF]]


def pick_kernel(ids, grad_out, far):
    far[...] = grad_out[1 - ids[HALF]]


def column_kernel(ids, w_qkv, out):
    part = w_qkv.shape[1] // 12
    width = w_qkv.shape[1] // 3
    for member in range(4):

        @pl.when(ids[MEMBER] == member)
        def _():
            for t in range(3):
                at = t * width + member * part
                value = w_qkv[:, at : at + part]
                for block in range(4):
                    out[block, :, t * part : (t + 1) * part] = value


def up_kernel(ids, w_up, own, y, c, yc):
    ff = own.shape[1]
    for ref, flip in ((own, 0), (y, 2), (c, 1), (yc, 3)):
        ref[...] = w_up[:, pl.ds(pl.multiple_of((ids[SEQ] ^ flip) * ff, ff), ff)]


def own_kernel(ids, grad_out, far, w_out, own, copy):
    copy[...] = w_out[...]
    half = far.shape[0]
    own[:half] = grad_out[ids[HALF]]
    own[half:] = far[...]


def second_kernel(ids, keep, recv, out):
    out[...] = (keep[...].astype(F32) + recv[1].astype(F32)).astype(BF16)


def both_kernel(ids, left, right, out):
    out[...] = (left[...].astype(F32) + right[...].astype(F32)).astype(BF16)


def chain_kernel(ids, keep, c, first, second):
    first[...] = (keep[0].astype(F32) + c[0].astype(F32)).astype(BF16)
    second[...] = (keep[1].astype(F32) + c[1].astype(F32)).astype(BF16)


def join_kernel(ids, first, y, a, b, c, d, out):
    rows = first.shape[0]
    out[:rows] = (first[...].astype(F32) + y[...].astype(F32)).astype(BF16)
    total = a[...].astype(F32) + b[...].astype(F32) + c[...].astype(F32) + d[...].astype(F32)
    out[rows:] = total.astype(BF16)


def pieces_kernel(ids, a, b, c, d, down, up):
    total = a[...].astype(F32) + b[...].astype(F32) + c[...].astype(F32) + d[...].astype(F32)
    low = total.astype(BF16)
    rows = down.shape[0]
    fine = up.shape[1]
    down[...] = low[:rows]
    for s in range(4):
        up[s] = low[rows + s * fine : rows + (s + 1) * fine]


def attend_kernel(
    ids, tok_own, tok_x, tok_z, tok_d, far_own, far_x, far_z, far_d, sinus, w_time, vec, small, wq,
    attn_in, qkv_t, o_full, o_send, lse, w_t, te,
):
    piece, width = tok_own.shape
    part = width // 4
    rows = wq.shape[1]
    own = 2 * piece
    gi = ids[MEMBER]
    for block in range(4):
        w_t[:, block * rows : (block + 1) * rows] = wq[block].T
    te[...] = dot(sinus[...], w_time[...]) + vec[0:1, :]
    te_row = te[0:1, :]
    gain, offset = vec[1:2, :], vec[2:3, :]
    bias = small[gi].astype(F32).T
    pairs = ((tok_own, far_own), (tok_x, far_x), (tok_z, far_z), (tok_d, far_d))
    for block, (tok, far) in enumerate(pairs):
        normed, _ = normalize(jnp.concatenate([tok[...], far[...]]).astype(F32) + te_row)
        low = (normed * gain + offset).astype(BF16)
        attn_in[block] = low
        qkv = dot(w_t[...], low, 1, 1)
        qkv_t[block, 0:part, :] = (qkv[:part] + bias[:, 3:4]).astype(BF16)
        qkv_t[block, part : 2 * part, :] = qkv[part : 2 * part].astype(BF16)
        qkv_t[block, 2 * part :, :] = (qkv[2 * part :] + bias[:, 4:5]).astype(BF16)

    @pl.loop(0, part // HEAD_DIM)
    def _(head):
        at = pl.multiple_of(head * HEAD_DIM, HEAD_DIM)
        k_t = jnp.concatenate([qkv_t[j, pl.ds(part + at, HEAD_DIM), :] for j in range(4)], 1)
        v_t = jnp.concatenate([qkv_t[j, pl.ds(2 * part + at, HEAD_DIM), :] for j in range(4)], 1)
        for block in range(4):
            q_t = qkv_t[block, pl.ds(at, HEAD_DIM), :] * jnp.asarray(0.125, BF16)
            scores = dot(k_t, q_t, 0, 0)
            top = jnp.max(scores, 0, keepdims=True)
            weights = jnp.exp(scores - top)
            total = jnp.sum(weights, 0, keepdims=True)
            attn = dot(v_t, weights.astype(BF16)) / total
            o_full[block, pl.ds(at, HEAD_DIM), :] = attn
            o_send[gi ^ block, pl.ds(at, HEAD_DIM), :] = attn.astype(BF16)
            lse[head * 4 + block] = jnp.broadcast_to(top + jnp.log(total), (8, own))


def fold(value):
    third = value.shape[0] // 3
    return jnp.concatenate([value[i * third : (i + 1) * third] for i in range(3)], 1)


def unfold(value):
    wide = value.shape[1] // 3
    return jnp.concatenate([value[:, i * wide : (i + 1) * wide] for i in range(3)], 0)


def branch_kernel(
    ids, attn, w_out, tok_own, far_own, te, vec, mlp_in, hidden_two, folds
):
    rows = attn.shape[1]
    te_row = te[0:1, :]
    hidden = jnp.concatenate([tok_own[...], far_own[...]]).astype(F32) + te_row + vec[5:6, :]
    for block in range(4):
        hidden = hidden + dot(attn[block], w_out[block * rows : (block + 1) * rows, :], 0, 0)
    hidden_two[...] = hidden
    normed, _ = normalize(hidden)
    mlp_in[...] = (normed * vec[6:7, :] + vec[7:8, :]).astype(BF16)
    for block in range(4):
        folds[block] = fold(attn[ids[SEQ] ^ block])


def feed_kernel(
    ids, m_own, m_y, m_c, m_yc, go_all, u_own, u_y, u_c, u_yc, w_down, b_up, folds,
    gm_own, gm_pair, gm_send, out_own, out_pair, out_send, act_all, gp_all, w_up,
):
    si = ids[SEQ]
    rows = u_own.shape[0]
    own = m_own.shape[0]
    for ref, flip in ((u_own, 0), (u_y, 2), (u_c, 1), (u_yc, 3)):
        w_up[pl.ds(pl.multiple_of((si ^ flip) * rows, rows), rows), :] = ref[...]
    fine = folds.shape[1]
    out_send[2 * own : 2 * own + fine, :] = folds[1]
    out_send[2 * own + fine :, :] = folds[3]
    for block, (ref, flip) in enumerate(((m_own, 0), (m_y, 2), (m_c, 1), (m_yc, 3))):
        grad_out = go_all[si ^ flip]
        pre = dot(ref[...], w_up[...]) + b_up[...]
        cdf = 0.5 * (1.0 + lax.erf(pre * (0.5**0.5)))
        act = (pre * cdf).astype(BF16)
        grad_act = dot(grad_out, w_down[...], 1, 1)
        slope = cdf + pre * (jnp.exp(-0.5 * pre * pre) * (0.5 / math.pi) ** 0.5)
        grad_pre = (grad_act * slope).astype(BF16)
        act_all[block] = act
        gp_all[block] = grad_pre
        gm = dot(grad_pre, w_up[...], 1, 1)
        out = dot(act, w_down[...])
        if block < 2:
            (gm_own, gm_pair)[block][...] = gm.astype(gm_pair.dtype if block else F32)
            (out_own, out_pair)[block][...] = out.astype(out_pair.dtype if block else F32)
        else:
            gm_send[block - 2] = gm.astype(BF16)
            out_send[(block - 2) * own : (block - 1) * own, :] = out.astype(BF16)


def feed_grad_kernel(
    ids, m_own, m_y, m_c, m_yc, go_all, act_all, gp_all, p_own, p_x, p_z, p_d, grad
):
    si, gi = ids[SEQ], ids[MEMBER]
    width = m_own.shape[1]
    ff = act_all.shape[2]
    part = ff // 4
    rows = width // 4
    fine = rows // 4
    pieces = ((p_own, 0), (p_x, 1), (p_z, 2), (p_d, 3))
    orders = ((m_own, 0), (m_y, 2), (m_c, 1), (m_yc, 3))
    for s in range(4):
        cols = slice(s * part, (s + 1) * part)
        total = jnp.zeros((part, width), F32)
        for block, (_, flip) in enumerate(orders):
            total = total + dot(act_all[block, :, cols], go_all[si ^ flip], 0, 0)
        grad[cols, :] = total.astype(BF16)
    for ref, flip in pieces:
        ref[:part, :] = grad[pl.ds(pl.multiple_of((gi ^ flip) * part, 16), part), :]
    for s in range(4):
        cols = slice(s * rows, (s + 1) * rows)
        total = jnp.zeros((rows, ff), F32)
        for block, (ref, _) in enumerate(orders):
            total = total + dot(ref[:, cols], gp_all[block], 0, 0)
        grad[cols, :] = total.astype(BF16)
    for ref, flip in pieces:
        for s in range(4):
            at = part + 16 + s * fine
            ref[at : at + fine, :] = grad[pl.ds(pl.multiple_of(s * rows + (gi ^ flip) * fine, 16), fine), :]
    b_up = jnp.zeros((1, ff), F32)
    b_down = jnp.zeros((1, width), F32)
    for block in range(4):
        b_up = b_up + jnp.sum(gp_all[block].astype(F32), 0, keepdims=True)
        b_down = b_down + jnp.sum(go_all[block].astype(F32), 0, keepdims=True)
    line = lax.broadcasted_iota(jnp.int32, (16, width), 0)
    extra = jnp.where(line == 0, b_up, jnp.where(line == 1, b_down, 0.0))
    for ref, flip in pieces:
        ref[part : part + 16, :] = jnp.where(gi == flip, extra, 0.0).astype(BF16)


def back_kernel(
    ids, gm_keep, gm_c, gm_y, hidden_two, go_own, w_out, vec, out_far, out_c, folds,
    grad_two, branch, ga_send, sums, out_pair,
):
    rows = w_out.shape[0] // 4
    grad_mlp = gm_keep[...] + gm_c[0].astype(F32) + gm_y[...].astype(F32)
    normed, rstd = normalize(hidden_two[...])
    grad = go_own[...].astype(F32) + norm_back(grad_mlp * vec[6:7, :], normed, rstd)
    grad_two[...] = grad
    low = grad.astype(BF16)
    branch[...] = low
    for block in range(4):
        ga_send[block] = dot(w_out[block * rows : (block + 1) * rows, :], low, 1, 1).astype(BF16)
    sums[0:1, :] = jnp.sum(grad_mlp * normed, 0, keepdims=True)
    sums[1:2, :] = jnp.sum(grad_mlp, 0, keepdims=True)
    sums[2:3, :] = jnp.sum(low.astype(F32), 0, keepdims=True)
    sums[3:4, :] = jnp.sum(grad, 0, keepdims=True)
    sums[4:8, :] = jnp.zeros((4, sums.shape[1]), F32)
    own = out_far.shape[0]
    fine = folds.shape[1]
    out_pair[:own, :] = (out_far[...].astype(F32) + out_c[own : 2 * own, :].astype(F32)).astype(BF16)
    out_pair[own : own + fine, :] = folds[2]
    out_pair[own + fine :, :] = out_c[2 * own + fine :, :]


def attend_back_kernel(
    ids, qkv_t, lse, o_full, ga, w_t, tok_own, tok_x, tok_z, tok_d, far_own, far_x, far_z, far_d, te, vec,
    dqkv_t, gh_send, sums, dk, dv,
):
    part = o_full.shape[1]
    own = 2 * tok_own.shape[0]
    si, gi = ids[SEQ], ids[MEMBER]

    @pl.loop(0, part // HEAD_DIM)
    def _(head):
        at = pl.multiple_of(head * HEAD_DIM, HEAD_DIM)
        k_t = jnp.concatenate([qkv_t[j, pl.ds(part + at, HEAD_DIM), :] for j in range(4)], 1)
        v_t = jnp.concatenate([qkv_t[j, pl.ds(2 * part + at, HEAD_DIM), :] for j in range(4)], 1)
        for block in range(4):
            q_t = qkv_t[block, pl.ds(at, HEAD_DIM), :] * jnp.asarray(0.125, BF16)
            do_t = ga[gi ^ block, pl.ds(at, HEAD_DIM), :]
            delta = jnp.sum(do_t.astype(F32) * o_full[block, pl.ds(at, HEAD_DIM), :], 0, keepdims=True)
            weights = jnp.exp(dot(k_t, q_t, 0, 0) - lse[head * 4 + block, 0:1, :])
            grad_probs = dot(v_t, do_t, 0, 0)
            grad_scores = (weights * (grad_probs - delta)).astype(BF16)
            value_part = dot(do_t, weights.astype(BF16), 1, 1)
            key_part = dot(q_t, grad_scores, 1, 1)
            dqkv_t[block, pl.ds(at, HEAD_DIM), :] = (dot(k_t, grad_scores) * 0.125).astype(BF16)
            if block == 0:
                dv[...] = value_part
                dk[...] = key_part
            else:
                dv[...] += value_part
                dk[...] += key_part
        for block in range(4):
            lanes = slice(block * own, (block + 1) * own)
            dqkv_t[block, pl.ds(part + at, HEAD_DIM), :] = dk[:, lanes].astype(BF16)
            dqkv_t[block, pl.ds(2 * part + at, HEAD_DIM), :] = dv[:, lanes].astype(BF16)

    te_row = te[0:1, :]
    gain = vec[1:2, :]
    sum_gain = jnp.zeros_like(gain)
    sum_bias = jnp.zeros_like(gain)
    sum_hidden = jnp.zeros_like(gain)
    pairs = ((tok_own, far_own), (tok_x, far_x), (tok_z, far_z), (tok_d, far_d))
    for block, (tok, far) in enumerate(pairs):
        normed, rstd = normalize(jnp.concatenate([tok[...], far[...]]).astype(F32) + te_row)
        grad_norm = dot(dqkv_t[block], w_t[...], 0, 0)
        grad = norm_back(grad_norm * gain, normed, rstd)
        gh_send[gi ^ block] = grad.astype(BF16)
        sum_gain = sum_gain + jnp.sum(grad_norm * normed, 0, keepdims=True)
        sum_bias = sum_bias + jnp.sum(grad_norm, 0, keepdims=True)
        sum_hidden = sum_hidden + jnp.sum(grad, 0, keepdims=True)
    sums[0:1, :] = sum_gain
    sums[1:2, :] = sum_bias
    sums[2:3, :] = sum_hidden
    sums[3:8, :] = jnp.zeros((5, sums.shape[1]), F32)


def qkv_grad_kernel(ids, attn_in, dqkv_t, sums_two, sums_one, keep, give):
    si, gi = ids[SEQ], ids[MEMBER]
    cols = dqkv_t.shape[1]
    part = cols // 3
    rows = part
    width = attn_in.shape[2]
    half = width // 2
    grad = jnp.zeros((cols, width), F32)
    tok_sum = jnp.zeros((16, cols), F32)
    for block in range(4):
        grad = grad + dot(dqkv_t[block], attn_in[block])
        tok_sum = tok_sum + dot(jnp.ones((16, dqkv_t.shape[2]), BF16), dqkv_t[block], 1, 1)
    grad = grad.astype(BF16)
    line = lax.broadcasted_iota(jnp.int32, (32, cols), 0)
    embed = sums_one[2:3, :] + sums_two[3:4, :]
    slot = 8 + 2 * (2 * si + ids[HALF])
    lanes = lax.broadcasted_iota(jnp.int32, (1, cols), 1)
    wide = [jnp.concatenate([e, jnp.zeros((1, cols - half), F32)], 1) for e in (embed[:, :half], embed[:, half:])]
    common = jnp.where(line == slot, wide[0], jnp.where(line == slot + 1, wide[1], 0.0))
    for s in range(4):
        here = slice(s * rows, (s + 1) * rows)
        extra = common
        vectors = (
            sums_two[0:1, here], sums_two[1:2, here], sums_two[2:3, here], sums_one[0:1, here], sums_one[1:2, here],
        )
        for i, vector in enumerate(vectors):
            full = jnp.concatenate([vector, jnp.zeros((1, cols - rows), F32)], 1)
            extra = jnp.where(line == i, full, extra)
        extra = jnp.where((line == 5) & (gi == s), tok_sum[0:1, :], extra)
        block = grad[:, here].T
        flip = si ^ s

        @pl.when(flip % 2 == 0)
        def _():
            keep[flip // 2, :rows, :] = block
            keep[flip // 2, rows:, :] = extra.astype(BF16)

        @pl.when(flip % 2 == 1)
        def _():
            give[flip // 2, :rows, :] = block
            give[flip // 2, rows:, :] = extra.astype(BF16)


def out_grad_kernel(ids, folds, out_c, out_y, branch_s, w_own, w_x, w_z, w_d, low):
    si, gi = ids[SEQ], ids[MEMBER]
    rows = low.shape[0]
    cols = w_own.shape[1]
    fine = rows // 4
    third = fine // 3
    own = branch_s.shape[1]
    third_rows = folds.shape[1]
    grad = dot(unfold(folds[0]), branch_s[si])
    grad = grad + dot(unfold(out_c[2 * own : 2 * own + third_rows, :]), branch_s[si ^ 1])
    grad = grad + dot(unfold(out_y[own : own + third_rows, :]), branch_s[si ^ 2])
    grad = grad + dot(unfold(out_y[own + third_rows :, :]), branch_s[si ^ 3])
    low[...] = grad.astype(BF16)
    for ref, flip in ((w_own, 0), (w_x, 1), (w_z, 2), (w_d, 3)):
        lines = low[pl.ds(pl.multiple_of((gi ^ flip) * fine, 16), fine), :]
        ref[:fine, :] = lines[:, :cols]
        ref[fine:, :] = jnp.concatenate([lines[i * third : (i + 1) * third, cols:] for i in range(3)], 1)


def out_kernel(ids, hidden_two, out_keep, out_c, out_y, vec, mine, other):
    half = mine.shape[0]
    out = hidden_two[...] + vec[8:9, :] + out_keep[...] + out_c[: 2 * half].astype(F32) + out_y[: 2 * half].astype(F32)
    mine[...] = out[:half].astype(BF16)
    other[...] = out[half:].astype(BF16)


def hidden_grad_kernel(ids, grad_two, recv, mine, other):
    half = mine.shape[0]
    grad = grad_two[...]
    for member in range(4):
        grad = grad + recv[member].astype(F32)
    mine[...] = grad[:half].astype(BF16)
    other[...] = grad[half:].astype(BF16)


def down_total_kernel(ids, own, x, z, d, w_down, b_up, b_down):
    gi = ids[MEMBER]
    quarter = w_down.shape[1]
    for ref, flip in ((own, 0), (x, 1), (z, 2), (d, 3)):
        w_down[gi ^ flip] = ref[:quarter, :].astype(F32)

        @pl.when(gi == flip)
        def _():
            b_up[...] = ref[quarter : quarter + 1, :].astype(F32)[0]
            full = ref[quarter : quarter + 2, :].astype(F32)
            rows = b_down.shape[0]
            for s in range(4):

                @pl.when(ids[SEQ] == s)
                def _():
                    b_down[...] = full[1, s * rows : (s + 1) * rows]


def up_total_kernel(ids, own, x, z, d, w_up):
    gi = ids[MEMBER]
    ff = own.shape[2]
    for ref, flip in ((own, 0), (x, 1), (z, 2), (d, 3)):
        for s in range(4):
            w_up[gi ^ flip, :, s * ff : (s + 1) * ff] = ref[s].astype(F32)


def total_kernel(ids, g_own, g_x, g_z, g_d, sinus, w_qkv, w_out, w_time, vectors, b_time, totals, embeds):
    si, gi = ids[SEQ], ids[MEMBER]
    rows = w_qkv.shape[0]
    cols = g_own.shape[1]
    width = w_qkv.shape[1] // 3
    part = cols // 3
    fine = rows // 4
    third = fine // 3
    for member in range(4):
        for ref, flip in ((g_own, 0), (g_x, 1), (g_z, 2), (g_d, 3)):

            @pl.when(gi ^ flip == member)
            def _():
                for t in range(3):
                    at = t * width + member * part
                    w_qkv[:, at : at + part] = ref[:rows, t * part : (t + 1) * part].astype(F32)
                lines = ref[rows + 32 :, :].astype(F32)
                w_out[member, :, :cols] = lines[:fine]
                for i in range(3):
                    w_out[member, i * third : (i + 1) * third, cols:] = lines[fine:, i * part : (i + 1) * part]

    small = jnp.zeros((32, cols), F32)
    for ref in (g_own, g_x, g_z, g_d):
        small = small + ref[rows : rows + 32, :].astype(F32)
    vectors[...] = small[:8]
    half = width // 2
    totals[...] = small
    for b in range(8):
        embeds[b : b + 1, :half] = totals[8 + 2 * b : 9 + 2 * b, :half]
        embeds[b : b + 1, half:] = totals[9 + 2 * b : 10 + 2 * b, :half]
    full = jnp.sum(embeds[...], 0, keepdims=True)
    for s in range(4):

        @pl.when(si == s)
        def _():
            b_time[...] = full[:, s * rows : (s + 1) * rows]

    w_time[...] = lax.dot_general(
        sinus[...], embeds[...], (((0,), (0,)), ((), ())), precision=lax.Precision.HIGHEST,
        preferred_element_type=F32,
    )


def pair_kernel(ids, grad_mine, out_mine, grad_other, out_other, grad_tokens, output):
    grad_tokens[ids[HALF]] = grad_mine[...]
    grad_tokens[1 - ids[HALF]] = grad_other[...]
    output[ids[HALF]] = out_mine[...]
    output[1 - ids[HALF]] = out_other[...]


def group_body(
    tokens, grad_out, timestep, w_time, b_time, ln1_gain, ln1_bias, w_qkv, b_query, b_value,
    w_out, b_out, ln2_gain, ln2_bias, w_up, b_up, w_down, b_down,
):
    seqs, piece, width = tokens.shape
    rows = w_qkv.shape[0]
    ff = w_down.shape[0]
    own = 2 * piece
    part = width // 4
    heads = part // HEAD_DIM
    yi, ci = lax.axis_index("y"), lax.axis_index("c")
    hi, zi, xi = lax.axis_index("h"), lax.axis_index("zl"), lax.axis_index("x")
    si = 2 * yi + ci
    gi = 2 * zi + xi
    step = Steps(jnp.stack([si, gi, hi]).astype(jnp.int32))

    def members(value):
        return lax.all_to_all(value, ("zl", "x"), split_axis=0, concat_axis=0, tiled=True)

    def shards(value):
        return lax.all_to_all(value, ("y", "c"), split_axis=0, concat_axis=0, tiled=True)

    def gather4(value):
        return [value, swap(value, "x"), swap(value, "zl"), across(value)]

    def trade4(keep, x, z, d):
        return [keep, swap(x, "x"), swap(z, "zl"), across(d)]

    def across_seq(value):
        return lax.ppermute(value, ("y", "c"), [(i, i ^ 3) for i in range(4)])

    half = width // 2
    hidden_low = ((own, width), BF16)
    hidden_full = ((own, width), F32)
    down = ((ff // 4 + 16, width), BF16)
    up = ((4, rows // 4, ff), BF16)
    packed = ((ff // 4 + 16 + rows, width), BF16)
    chain = (2, rows + 32, 3 * part)
    joined = ((rows + 32 + rows // 3, 3 * part), BF16)
    v = Values()

    def sinusoid_at(steps, place):
        freq = jnp.exp(-math.log(10000.0) * (place % half).astype(F32) / half)
        angles = steps[:, None] * freq[None, :]
        return jnp.where(place < half, jnp.sin(angles), jnp.cos(angles)).astype(BF16)

    w_time_f = lax.all_gather(w_time, ("y", "c"), axis=0, tiled=True)
    here = jnp.broadcast_to(pick(timestep, hi).astype(F32), (8,))
    sinus_here = sinusoid_at(here, jnp.arange(width))

    def token():
        tok_own, tok_far, blank = step(token_kernel, 2, [tokens], [((piece, width), BF16)] * 2 + [((1, rows), BF16)])
        v.blank = blank.reshape(rows)
        v.far_own = swap(tok_far, "h")
        v.toks = gather4(tok_own)
        v.fars = gather4(v.far_own)

    def small_parameters():
        low_bits = (timestep % 64).astype(BF16)
        high_bits = (timestep // 64).astype(BF16)
        steps_row = jnp.concatenate([high_bits, low_bits, jnp.zeros((rows - 2 * seqs,), BF16)])
        small = jnp.stack(
            [b_time, ln1_gain, ln1_bias, b_query, b_value, b_out, ln2_gain, ln2_bias, b_down, steps_row] + [v.blank] * 6
        )
        v.small = lax.all_gather(small, ("y", "c"))
        v.vec = jnp.transpose(v.small, (1, 0, 2)).reshape(16, width).astype(F32)

    def column():
        (blocks,) = step(column_kernel, 2, [w_qkv], [((4, rows, 3 * part), BF16)], behind=[v.small])
        v.wq = shards(blocks)

    def up_weights():
        pieces = step(up_kernel, 2, [w_up], [((rows, ff), BF16)] * 4)
        v.ups = [pieces[0], swap(pieces[1], "y"), swap(pieces[2], "c"), across_seq(pieces[3])]

    def pick_grad():
        (send,) = step(pick_kernel, 2, [grad_out], [((piece, width), BF16)])
        v.go_far = swap(send, "h")

    def attend():
        v.attn_in, v.qkv_t, v.o_full, send, v.lse, v.w_t, v.te = step(attend_kernel, 15, [*v.toks, *v.fars, sinus_here, w_time_f, v.vec, v.small, v.wq],
            [((4, own, width), BF16), ((4, 3 * part, own), BF16), ((4, part, own), F32), ((4, part, own), BF16),
             ((4 * heads, 8, own), F32), ((3 * part, width), BF16), ((8, width), F32)], behind=[v.ups[1], v.ups[2]])
        v.attn = members(send)

    def own_grad():
        v.go_own, copy = step(own_kernel, 2, [grad_out, v.go_far, w_out], [hidden_low, ((rows, width), BF16)])
        v.w_out = lax.all_gather(copy, ("y", "c"), axis=0, tiled=True)
        v.go_all = lax.all_gather(v.go_own, ("y", "c"))

    def branch():
        mlp, v.hidden_two, v.folds = step(branch_kernel, 30, [v.attn, v.w_out, v.toks[0], v.far_own, v.te, v.vec],
            [hidden_low, hidden_full, ((4, part // 3, width), BF16)], behind=[v.ups[3]])
        y = swap(mlp, "y")
        v.mlps = [mlp, y, swap(mlp, "c"), swap(y, "c")]

    def feed():
        v.gm_own, v.gm_far, gm_send, v.out_own, v.out_far, out_send, v.act, v.gp = step(feed_kernel, 10,
            [*v.mlps, v.go_all, *v.ups, w_down, b_up.astype(F32).reshape(1, ff), v.folds],
            [hidden_full, hidden_low, ((2, own, width), BF16), hidden_full, hidden_low,
             ((2 * own + 2 * part // 3, width), BF16), *[((4, own, ff), BF16)] * 2],
            [pltpu.VMEM((width, ff), BF16)],
        )
        v.gm_c = swap(gm_send, "c")
        v.out_c = swap(out_send, "c")

    def gm_add():
        (pair,) = step(second_kernel, 2, [v.gm_far, v.gm_c], [hidden_low])
        v.gm_y = swap(pair, "y")

    def feed_grad():
        v.ps = trade4(*step(feed_grad_kernel, 7, [*v.mlps, v.go_all, v.act, v.gp], [packed] * 4,
            [pltpu.VMEM((width, width), BF16)],
        ))

    def back():
        v.grad_two, branch_low, send, v.sums_two, pair = step(back_kernel, 5,
            [v.gm_own, v.gm_c, v.gm_y, v.hidden_two, v.go_own, v.w_out, v.vec, v.out_far, v.out_c,
             v.folds],
            [hidden_full, hidden_low, ((4, part, own), BF16), ((8, width), F32), ((own + 2 * part // 3, width), BF16)],
        )
        v.ga = members(send)
        v.branch_s = lax.all_gather(branch_low, ("y", "c"))
        v.out_y = swap(pair, "y")

    def attend_back():
        v.dqkv, gh, v.sums_one = step(attend_back_kernel, 15,
            [v.qkv_t, v.lse, v.o_full, v.ga, v.w_t, *v.toks, *v.fars, v.te, v.vec],
            [((4, 3 * part, own), BF16), ((4, own, width), BF16), ((8, width), F32)],
            [pltpu.VMEM((HEAD_DIM, 4 * own), F32)] * 2,
        )
        v.gh = members(gh)

    def p_sum():
        v.d_low, v.u_low = step(pieces_kernel, 2, v.ps, [down, up])
        v.d_h = swap(v.d_low, "h")
        v.u_h = swap(v.u_low, "h")

    def qkv_grad():
        v.ch_keep, give = step(qkv_grad_kernel, 5, [v.attn_in, v.dqkv, v.sums_two, v.sums_one], [(chain, BF16)] * 2
        )
        v.ch_c = swap(give, "c")

    def out_grad():
        pieces = step(out_grad_kernel, 3, [v.folds, v.out_c, v.out_y, v.branch_s],
            [((rows // 3, 3 * part), BF16)] * 4, [pltpu.VMEM((rows, width), BF16)],
        )
        v.wos = trade4(*pieces)

    def chain_add():
        v.first, second = step(chain_kernel, 2, [v.ch_keep, v.ch_c], [(chain[1:], BF16)] * 2)
        v.ch_y = swap(second, "y")

    def join():
        (v.now,) = step(join_kernel, 2, [v.first, v.ch_y, *v.wos], [joined])
        v.ch_h = swap(v.now, "h")

    def out():
        v.out_mine, other = step(out_kernel, 2, [v.hidden_two, v.out_own, v.out_c, v.out_y, v.vec],
            [((piece, width), BF16)] * 2,
        )
        v.out_h = swap(other, "h")

    def hidden():
        v.gt_mine, other = step(hidden_grad_kernel, 3, [v.grad_two, v.gh], [((piece, width), BF16)] * 2)
        v.gt_h = swap(other, "h")

    def d_add():
        (value,) = step(both_kernel, 2, [v.d_low, v.d_h], [down])
        v.dg = gather4(value)

    def u_add():
        (value,) = step(both_kernel, 2, [v.u_low, v.u_h], [up])
        v.gu_s = shards(value)
        v.ug = gather4(v.gu_s)

    def now_add():
        (value,) = step(both_kernel, 2, [v.now, v.ch_h], [joined])
        v.qg = gather4(value)

    def pair():
        v.grad_tokens, v.output = step(pair_kernel, 2, [v.gt_mine, v.out_mine, v.gt_h, v.out_h], [((seqs, piece, width), BF16)] * 2
        )

    def total():
        steps = (v.small[:, 9, :seqs].astype(F32) * 64 + v.small[:, 9, seqs : 2 * seqs].astype(F32)).reshape(-1)
        sinus_rows = sinusoid_at(steps, si * rows + jnp.arange(rows)).astype(F32)
        v.w_qkv, v.t_out, v.w_time, v.tv, v.b_time = step(total_kernel, 3, [*v.qg, sinus_rows],
            [((rows, 3 * width), F32), ((4, rows // 4, width), F32), ((rows, width), F32), ((8, 3 * part), F32),
             ((1, rows), F32)],
            [pltpu.VMEM((32, 3 * part), F32), pltpu.VMEM((8, width), F32)],
        )

    def down_total():
        v.w_down, v.b_up, v.b_down = step(down_total_kernel, 3, v.dg, [((4, ff // 4, width), F32), ((ff,), F32), ((rows,), F32)]
        )

    def up_total():
        (v.w_up,) = step(up_total_kernel, 3, v.ug, [((4, rows // 4, 4 * ff), F32)])

    for run in (
        token, small_parameters, pick_grad, column, up_weights, own_grad, attend, branch, feed, gm_add, feed_grad,
        back, attend_back, out, p_sum, qkv_grad, chain_add, out_grad, join, d_add, hidden, u_add, now_add, down_total,
        total, pair, up_total,
    ):
        run()
    tv = v.tv
    return (
        v.output, v.grad_tokens, v.w_time, v.b_time.reshape(rows), tv[3, :rows], tv[4, :rows], v.w_qkv,
        tv[5, :part], tv[5, 2 * part :], v.t_out.reshape(rows, width), tv[2, :rows], tv[0, :rows], tv[1, :rows],
        v.w_up.reshape(rows, 4 * ff), v.b_up, v.w_down.reshape(ff, width), v.b_down,
    )


def solution(mesh):
    placed = (
        P("seq", "ctx", None),
        P("seq", "ctx", None),
        P("seq"),
        P("seq", None),
        P("seq"),
        P("seq"),
        P("seq"),
        P("seq", None),
        P("seq"),
        P("seq"),
        P("seq", None),
        P("seq"),
        P("seq"),
        P("seq"),
        P("seq", None),
        P("seq"),
        P("seq", None),
        P("seq"),
    )
    out_placed = (
        P("seq", "ctx", None),
        P("seq", "ctx", None),
        P("seq", None),
        P("seq"),
        P("seq"),
        P("seq"),
        P("seq", None),
        P("seq"),
        P("seq"),
        P("seq", None),
        P("seq"),
        P("seq"),
        P("seq"),
        P("seq", None),
        P("seq"),
        P("seq", None),
        P("seq"),
    )
    sizes = dict(mesh.shape)
    if sizes["seq"] == 4 and sizes["ctx"] == 8:
        fine = Mesh(mesh.devices.reshape((2,) * 5), ("y", "c", "h", "zl", "x"))
        split = {"seq": ("y", "c"), "ctx": ("h", "zl", "x"), None: None}

        def finer(spec):
            return P(*(split[axis] for axis in spec))

        return jax.shard_map(
            group_body,
            mesh=fine,
            in_specs=tuple(finer(spec) for spec in placed),
            out_specs=tuple(finer(spec) for spec in out_placed),
            check_vma=False,
        )
    return jax.shard_map(
        body,
        mesh=mesh,
        in_specs=placed,
        out_specs=out_placed,
        check_vma=False,
    )
```
